32 devices in a mesh: dp: 4 (over y, core), seq: 2 (over x), tensor: 4 (over z).
Axes of the slice: x: 2, y: 2, z: 4, core: 2. Of those that a mesh axis runs over, the one named last changes fastest.
Arguments:
- hidden_in: bfloat16 [4, 1024, 1024], P('dp', ('seq', 'tensor')), may hold values from -6 to 6
- cotangent: bfloat16 [4, 1024, 1024], P('dp', ('seq', 'tensor')), may hold values from -6 to 6
- piece_starts: int32 [4, 2], P('dp'), may hold values from 0 to 768, as said below
- expert_ids: int32 [4, 1024, 8], P('dp', 'seq'), may hold values from 0 to 15, all different within a row
- claim_order: int32 [4, 1024], P('dp', 'seq'), may hold values from 0 to 511, as said below
- first_gain: bfloat16 [1024], P(('dp', 'seq', 'tensor')), may hold values from 0.25 to 1.75
- second_gain: bfloat16 [1024], P(('dp', 'seq', 'tensor')), may hold values from 0.25 to 1.75
- router: bfloat16 [1024, 16], P(('dp', 'seq', 'tensor')), may hold values from -0.09375 to 0.09375
- w_query: bfloat16 [1024, 1024], P(('dp', 'seq'), 'tensor'), may hold values from -0.25 to 0.25
- key_projection: bfloat16 [1024, 512], P(('dp', 'seq'), 'tensor'), may hold values from -0.25 to 0.25
- value_projection: bfloat16 [1024, 512], P(('dp', 'seq'), 'tensor'), may hold values from -0.1875 to 0.1875
- w_out: bfloat16 [1024, 1024], P(('dp', 'seq'), 'tensor'), may hold values from -1.5 to 1.5
- w_gate: bfloat16 [16, 1024, 512], P(None, ('dp', 'seq'), 'tensor'), may hold values from -0.1875 to 0.1875
- w_up: bfloat16 [16, 1024, 512], P(None, ('dp', 'seq'), 'tensor'), may hold values from -0.1875 to 0.1875
- w_down: bfloat16 [16, 1024, 512], P(None, ('dp', 'seq'), 'tensor'), may hold values from -1 to 1
Outputs:
- output: bfloat16 [4, 1024, 1024], P('dp', ('seq', 'tensor'))
- input_grad: bfloat16 [4, 1024, 1024], P('dp', ('seq', 'tensor'))
- query_grad: float32 [1024, 1024], P(('dp', 'seq'), 'tensor')
- key_grad: float32 [1024, 512], P(('dp', 'seq'), 'tensor')
- value_grad: float32 [1024, 512], P(('dp', 'seq'), 'tensor')
- out_grad: float32 [1024, 1024], P(('dp', 'seq'), 'tensor')
- gate_grad: float32 [16, 1024, 512], P(None, ('dp', 'seq'), 'tensor')
- up_grad: float32 [16, 1024, 512], P(None, ('dp', 'seq'), 'tensor')
- down_grad: float32 [16, 1024, 512], P(None, ('dp', 'seq'), 'tensor')
- first_gain_grad: float32 [1024], P(('dp', 'seq', 'tensor'))
- second_gain_grad: float32 [1024], P(('dp', 'seq', 'tensor'))
- router_grad: float32 [1024, 16], P(('dp', 'seq', 'tensor'))
The draws below stay inside these ranges and needn't reach their ends.
Inputs may be any that keep to these rules, and one draw needn't show every extreme that they name: `piece_starts`: pieces of a sequence come in increasing order and don't intersect. `claim_order`: within each dispatch group the 512 values are a permutation. `expert_ids`: a token names 8 different experts.
All inputs are finite; a program needn't handle non-finite values.
Results may differ from the reference program's by a relative error of at most 0.028.
Values may be sent and summed in bfloat16 or wider, within the bound.
No kernel may reach another device: no remote copies, remote signals or barrier semaphores. Data moves between devices by JAX's collectives and lax.ppermute only.
A program may use at most 320 MiB of HBM per device.

```python
import math
import jax
import jax.numpy as jnp
from jax import lax

MODEL_WIDTH = 1024
QUERY_HEADS = 16
KEY_VALUE_HEADS = 8
HEAD_SIZE = 64
F = 512
TOPK = 8
E = 16
SEQS = 1
TOK_SEQ = 512
PIECE = 256
SEQUENCE_LENGTH = 1024
B = 4
PIECES = 2
CAP = 320
N_DP = 4
N_SEQ = 2


def draw_piece_starts(key, part):
    offsets = jax.random.randint(key, (B, PIECES), PIECE // 2, PIECE + PIECE // 2 + 1)
    last_offsets = jnp.minimum(offsets[:, PIECES - 1], PIECE)
    offsets = offsets.at[:, PIECES - 1].set(last_offsets)
    offsets = offsets.at[0, 0].set(0).at[0, PIECES - 1].set(PIECE)
    return (jnp.arange(PIECES, dtype=jnp.int32)[None, :] * (2 * PIECE) + offsets).astype(jnp.int32)


def draw_claim_order(key, part):
    group_count = B // SEQS * (SEQUENCE_LENGTH // TOK_SEQ)
    members = SEQS * TOK_SEQ
    key_rows = jax.random.split(key, group_count)

    def shuffle(one_key):
        return jax.random.permutation(one_key, members)
    ranks = jax.vmap(shuffle)(key_rows)
    ranks = ranks.reshape(B // SEQS, SEQUENCE_LENGTH // TOK_SEQ, SEQS, TOK_SEQ)
    return jnp.swapaxes(ranks, 1, 2).reshape(B, SEQUENCE_LENGTH).astype(jnp.int32)


def shard_levels(own_key, extent, cuts, smallest, high):
    level = 1.0
    for axis_at, blocks in cuts:
        draws = jax.random.uniform(jax.random.fold_in(jax.random.fold_in(own_key, 6), axis_at), (blocks,), jnp.float32, smallest / len(cuts), high / len(cuts))
        level = level * jnp.repeat(jnp.exp(draws), extent[axis_at] // blocks).reshape((-1,) + (1,) * (len(extent) - 1 - axis_at))
    return level


def choose_distinct(stream_key, rows, count, top, lift):
    sequence = jax.random.permutation(jax.random.fold_in(stream_key, 1), count)
    favour = sequence
    for power in range(3):
        favour = favour * favour // count
    favour = favour * lift // count
    chance = jax.random.randint(jax.random.fold_in(stream_key, 2), (rows, count), 0, 4096) + favour
    holders = jax.random.permutation(jax.random.fold_in(stream_key, 3), rows)[jnp.arange(count) % rows]
    chance = jnp.where(jnp.arange(rows)[:, None] == holders[None, :], 1 << 14, chance)
    score = chance * count + jnp.arange(count)
    return lax.top_k(score.astype(jnp.int32), top)[1].astype(jnp.int32)


def centred(own_key, dims, scale, limit, shards=(), kind=jnp.bfloat16):
    loudness = shard_levels(own_key, dims, shards, -0.22, 0.18) if shards else 1.0
    array = jax.random.normal(own_key, dims, jnp.float32) * scale * loudness
    return jnp.minimum(jnp.maximum(array, -limit), limit).astype(kind)


def setup_inputs(seed: int = 0) -> dict:
    keys = jax.random.split(jax.random.key(seed), 16)
    return {
        "hidden_in": centred(keys[0], (B, SEQUENCE_LENGTH, MODEL_WIDTH), 1.0, 6.0, ((0, 4), (1, 8))),
        "cotangent": centred(keys[1], (B, SEQUENCE_LENGTH, MODEL_WIDTH), 1.0, 6.0, ((0, 4), (1, 8))),
        "piece_starts": draw_piece_starts(jax.random.fold_in(keys[15], 71), 0),
        "expert_ids": choose_distinct(keys[3], B * SEQUENCE_LENGTH, E, TOPK, 4096).reshape((B, SEQUENCE_LENGTH, TOPK)),
        "claim_order": draw_claim_order(jax.random.fold_in(keys[15], 71), 0),
        "first_gain": jnp.clip(1.0 + 0.15 * jax.random.normal(keys[5], (MODEL_WIDTH,), jnp.float32), 0.25, 1.75).astype(jnp.bfloat16),
        "second_gain": jnp.clip(1.0 + 0.15 * jax.random.normal(keys[6], (MODEL_WIDTH,), jnp.float32), 0.25, 1.75).astype(jnp.bfloat16),
        "router": centred(keys[7], (MODEL_WIDTH, E), (4 * MODEL_WIDTH) ** -0.5, 0.09375, ((0, 32),)),
        "w_query": centred(keys[8], (MODEL_WIDTH, QUERY_HEADS * HEAD_SIZE), (MODEL_WIDTH // 2) ** -0.5, 0.25, ((0, 8), (1, 4))),
        "key_projection": centred(keys[9], (MODEL_WIDTH, KEY_VALUE_HEADS * HEAD_SIZE), (MODEL_WIDTH // 2) ** -0.5, 0.25, ((0, 8), (1, 4))),
        "value_projection": centred(keys[10], (MODEL_WIDTH, KEY_VALUE_HEADS * HEAD_SIZE), MODEL_WIDTH ** -0.5, 0.1875, ((0, 8), (1, 4))),
        "w_out": centred(keys[11], (MODEL_WIDTH, QUERY_HEADS * HEAD_SIZE), (QUERY_HEADS * HEAD_SIZE // 64) ** -0.5, 1.5, ((0, 8), (1, 4))),
        "w_gate": centred(keys[12], (E, MODEL_WIDTH, F), MODEL_WIDTH ** -0.5, 0.1875, ((1, 8), (2, 4))),
        "w_up": centred(keys[13], (E, MODEL_WIDTH, F), MODEL_WIDTH ** -0.5, 0.1875, ((1, 8), (2, 4))),
        "w_down": centred(keys[14], (E, MODEL_WIDTH, F), (F // 16) ** -0.5, 1.0, ((1, 8), (2, 4))),
    }


@jax.custom_vjp
def low(v):
    return lax.optimization_barrier(v.astype(jnp.bfloat16)).astype(jnp.float32)

@jax.custom_vjp
def low_back(v):
    return v

def low_keep(v):
    return (low(v), None)

def low_pass(kept, grad):
    return (grad,)

def back_keep(v):
    return (v, None)

def back_low(kept, grad):
    return (low(grad),)
low.defvjp(low_keep, low_pass)
low_back.defvjp(back_keep, back_low)
highest = lax.Precision.HIGHEST
norm_eps = 1e-06
masked_fill = -1e+30

def rms_scale(value_rows, gain):
    return value_rows * lax.rsqrt(lax.optimization_barrier(jnp.mean(value_rows * value_rows, axis=-1, keepdims=True)) + norm_eps) * gain

def rotary(value_rows, positions, sign):
    half = HEAD_SIZE // 2
    index = jnp.arange(half).astype(jnp.float32)
    freqs = jnp.exp(index * (-2.0 * math.log(10000.0) / HEAD_SIZE))
    angles = positions.astype(jnp.float32)[:, None] * freqs[None, :]
    cosine = jnp.cos(angles)[:, None, :]
    sine = sign * jnp.sin(angles)[:, None, :]
    shaped = value_rows.reshape(value_rows.shape[:-1] + (value_rows.shape[-1] // HEAD_SIZE, HEAD_SIZE))
    leading = shaped[..., :half]
    second = shaped[..., half:]
    turned = jnp.concatenate([leading * cosine - second * sine, second * cosine + leading * sine], axis=-1)
    return turned.reshape(value_rows.shape)

def piece_ids(positions, starts):
    inside = (positions[..., :, None] >= starts[..., None, :]) & (positions[..., :, None] < starts[..., None, :] + PIECE)
    labels = jnp.arange(1, starts.shape[-1] + 1, dtype=jnp.int32)
    return lax.optimization_barrier(jnp.max(jnp.where(inside, labels, 0), axis=-1)) - 1

def attend_sequence(inputs):
    query_rows, key_rows, value_rows, starts = inputs
    positions = jnp.arange(SEQUENCE_LENGTH, dtype=jnp.int32)
    labels = piece_ids(positions, starts)
    expert_block = math.gcd(SEQUENCE_LENGTH, 512)
    group_width = QUERY_HEADS // KEY_VALUE_HEADS
    heads_of_key = key_rows.reshape(SEQUENCE_LENGTH, KEY_VALUE_HEADS, HEAD_SIZE)
    heads_of_value = value_rows.reshape(SEQUENCE_LENGTH, KEY_VALUE_HEADS, HEAD_SIZE)

    def one_block(leading):
        row_values = lax.dynamic_slice_in_dim(query_rows, leading, expert_block, 0).reshape(expert_block, KEY_VALUE_HEADS, group_width, HEAD_SIZE)
        row_pos = leading + jnp.arange(expert_block, dtype=jnp.int32)
        row_ids = lax.dynamic_slice_in_dim(labels, leading, expert_block, 0)
        allowed = (positions[None, :] <= row_pos[:, None]) | (row_ids[:, None] == labels[None, :]) & (row_ids[:, None] >= 0)
        scores = low_back(jnp.einsum('qgrd,kgd->grqk', row_values, heads_of_key, precision=highest) * HEAD_SIZE ** (-0.5))
        scores = jnp.where(allowed[None, None], scores, masked_fill)
        weights = low(jax.nn.softmax(scores, axis=-1))
        mixed = jnp.einsum('grqk,kgd->qgrd', weights, heads_of_value, precision=highest)
        return mixed.reshape(expert_block, QUERY_HEADS * HEAD_SIZE)
    firsts = jnp.arange(SEQUENCE_LENGTH // expert_block, dtype=jnp.int32) * expert_block
    return lax.map(jax.checkpoint(one_block), firsts).reshape(SEQUENCE_LENGTH, QUERY_HEADS * HEAD_SIZE)

def route_slots(expert_ids, claim, count):
    experts = jnp.arange(E, dtype=jnp.int32)
    chosen = lax.optimization_barrier(jnp.sum((expert_ids[:, :, None] == experts[None, None, :]).astype(jnp.int32), axis=1, dtype=jnp.int32))
    order = jnp.zeros((count,), jnp.int32).at[claim].set(jnp.arange(count, dtype=jnp.int32))
    ranked = chosen[order]
    earlier = jnp.cumsum(ranked, axis=0, dtype=jnp.int32) - ranked
    place = jnp.take_along_axis(earlier[claim], expert_ids, axis=1)
    slot = jnp.where(place < CAP, expert_ids * CAP + place, E * CAP).astype(jnp.int32)
    owner = jnp.broadcast_to(jnp.arange(count, dtype=jnp.int32)[:, None], expert_ids.shape)
    slot_token = jnp.full((E * CAP,), count, jnp.int32).at[slot.reshape(-1)].set(owner.reshape(-1), mode='drop')
    return (slot, slot_token)

def expert_group(inputs, gate_w, up_w, down_w):
    normed, logits, expert_ids, claim = inputs
    count = normed.shape[0]
    gates = jax.nn.softmax(jnp.take_along_axis(logits, expert_ids, axis=1), axis=-1)
    slot, slot_token = route_slots(expert_ids, claim, count)
    slot_gate = jnp.zeros((E * CAP,), gates.dtype).at[slot.reshape(-1)].set(gates.reshape(-1), mode='drop')
    taken = jnp.take(normed, slot_token, axis=0, mode='fill', fill_value=0.0).reshape(E, CAP, MODEL_WIDTH)
    gate_pre = low_back(jnp.einsum('ecd,edf->ecf', taken, gate_w, precision=highest))
    up_pre = low_back(jnp.einsum('ecd,edf->ecf', taken, up_w, precision=highest))
    active = low(jax.nn.silu(gate_pre) * up_pre)
    slot_out = low_back(jnp.einsum('ecf,edf->ecd', active, down_w, precision=highest))
    weighted = slot_out.reshape(E * CAP, MODEL_WIDTH) * slot_gate[:, None]
    return jnp.zeros((count, MODEL_WIDTH), normed.dtype).at[slot_token].add(weighted, mode='drop')

def to_groups(value_rows):
    shaped = value_rows.reshape((N_DP, SEQS, N_SEQ, TOK_SEQ) + value_rows.shape[2:])
    return jnp.swapaxes(shaped, 1, 2).reshape((N_DP * N_SEQ, SEQS * TOK_SEQ) + value_rows.shape[2:])

def from_groups(value_rows):
    shaped = value_rows.reshape((N_DP, N_SEQ, SEQS, TOK_SEQ) + value_rows.shape[2:])
    return jnp.swapaxes(shaped, 1, 2).reshape((N_DP * SEQS, N_SEQ * TOK_SEQ) + value_rows.shape[2:])

def reference(hidden_in, cotangent, piece_starts, expert_ids, claim_order, first_gain, second_gain, router, w_query, key_projection, value_projection, w_out, w_gate, w_up, w_down):
    positions = jnp.arange(SEQUENCE_LENGTH, dtype=jnp.int32)

    def forward(inputs, gain_one, gain_two, router_w, query_matrix, key_matrix, value_matrix, output_matrix, gate_w, up_w, down_w):
        normed = low(rms_scale(inputs, gain_one))
        query_before_rotary = jnp.einsum('bld,dc->blc', normed, query_matrix, precision=highest)
        key_before_rotary = jnp.einsum('bld,dc->blc', normed, key_matrix, precision=highest)
        value_before_rotary = jnp.einsum('bld,dc->blc', normed, value_matrix, precision=highest)
        query_rows = low(rotary(low_back(query_before_rotary), positions, 1.0))
        key_rows = low(rotary(low_back(key_before_rotary), positions, 1.0))
        value_rows = low(low_back(value_before_rotary))
        mixed = lax.map(jax.checkpoint(attend_sequence), (query_rows, key_rows, value_rows, piece_starts))
        mixed = low(low_back(mixed))
        branch = low_back(jnp.einsum('blc,dc->bld', mixed, output_matrix, precision=highest))
        middle = inputs + branch
        second = low(rms_scale(middle, gain_two))
        logits = jnp.einsum('bld,de->ble', second, router_w, precision=highest)

        def group_fn(parts):
            return expert_group(parts, gate_w, up_w, down_w)
        experts_out = lax.map(jax.checkpoint(group_fn), (to_groups(second), to_groups(logits), to_groups(expert_ids), to_groups(claim_order)))
        return middle + low_back(from_groups(experts_out))
    floats = [a.astype(jnp.float32) for a in (hidden_in, first_gain, second_gain, router, w_query, key_projection, value_projection, w_out, w_gate, w_up, w_down)]
    result, pullback = jax.vjp(forward, *floats)
    grads = pullback(cotangent.astype(jnp.float32))
    return (result.astype(jnp.bfloat16), grads[0].astype(jnp.bfloat16), grads[4], grads[5], grads[6], grads[7], grads[8], grads[9], grads[10], grads[1], grads[2], grads[3])
```

```python
import functools
import math

import jax
import jax.numpy as jnp
from jax import lax
from jax.experimental import pallas as pl
from jax.experimental.pallas import tpu as pltpu
from jax.sharding import PartitionSpec as P

HEAD = 64
E = 16
PIECE = 256
CAP = 320
EPS = 1e-06
FILL = -1e30
EXPERTS_PER_STEP = 2
ROW_TILE = 256
f32 = jnp.float32
bf16 = jnp.bfloat16

NT = (((1,), (1,)), ((), ()))
NN = (((1,), (0,)), ((), ()))


def dot(a, b, dims=NN):
    return lax.dot_general(a, b, dims, preferred_element_type=f32)


def full(shape):
    rank = len(shape)
    return pl.BlockSpec(shape, lambda *_: (0,) * rank)


def whole_call(body, outs, args, scratch=(), flops=0, prefetch=0):
    moved = sum(math.prod(a.shape) * a.dtype.itemsize for a in (*args, *outs))
    return pl.pallas_call(
        body,
        out_shape=outs,
        grid_spec=pltpu.PrefetchScalarGridSpec(
            num_scalar_prefetch=prefetch,
            grid=(1,),
            in_specs=[full(a.shape) for a in args[prefetch:]],
            out_specs=[full(o.shape) for o in outs],
            scratch_shapes=list(scratch),
        ),
        cost_estimate=pl.CostEstimate(flops=int(flops), bytes_accessed=int(moved), transcendentals=0),
    )(*args)


def sds(shape, dtype):
    return jax.ShapeDtypeStruct(shape, dtype)


def reorder_kernel(where, a_ref, b_ref, a_out, b_out):
    wide = a_ref.shape[1] // where.shape[0]
    for i in range(where.shape[0]):
        source = pl.ds(pl.multiple_of(where[i] * wide, wide), wide)
        a_out[:, i * wide : (i + 1) * wide] = a_ref[:, source]
        b_out[:, i * wide : (i + 1) * wide] = b_ref[:, source]


def turn(v, cos, sin):
    lane = lax.broadcasted_iota(jnp.int32, v.shape, 1) % HEAD
    other = jnp.where(lane < HEAD // 2, pltpu.roll(v, 128 - HEAD // 2, 1), pltpu.roll(v, HEAD // 2, 1))
    return v * cos + other * sin


def rows_of(refs, rows):
    parts = []
    for r in refs:
        parts += [r[i, 0:rows, :] for i in range(r.shape[0])]
    return jnp.concatenate(parts, axis=0)


def qkv_kernel(n, rows, *refs):
    xs, (gain, cos, sin, wa, wb), (x1, q, kv) = refs[:n], refs[n : n + 5], refs[n + 5 :]
    m = xs[0].shape[0]
    for j in range(n):
        v = xs[j][...].astype(f32)
        r = lax.rsqrt(jnp.mean(v * v, axis=-1, keepdims=True) + EPS)
        x1[j * m : (j + 1) * m, :] = (v * r * gain[...]).astype(bf16)
    out = dot(x1[...], rows_of((wa, wb), rows))
    c, s = cos[...], sin[...]
    q[:, 0:128] = turn(out[:, 0:128], c, s).astype(bf16)
    q[:, 128:256] = turn(out[:, 128:256], c, s).astype(bf16)
    kv[:, 0:128] = turn(out[:, 256:384], c, s).astype(bf16)
    kv[:, 128:256] = out[:, 384:512].astype(bf16)


SCORE = HEAD ** (-0.5) * math.log2(math.e)


def attend_kernel(parts, n, q, lim, *refs):
    kvs, poss = refs[:parts], refs[parts : 2 * parts]
    mixed, (ot, lse) = refs[2 * parts : 2 * parts + n], refs[2 * parts + n : 2 * parts + n + 2]
    qs, ks, vt, kp = refs[2 * parts + n + 2 :]
    count = q.shape[0]
    heads = q.shape[1] // HEAD
    first = 0
    for kvr, pr in zip(kvs, poss):
        span = slice(first, first + kvr.shape[0])
        first += kvr.shape[0]
        v = kvr[:, 128:256].astype(f32).T.astype(bf16)
        for g in range(2):
            ks[g, span, :] = kvr[:, g * HEAD : (g + 1) * HEAD]
            vt[g, :, span] = v[g * HEAD : (g + 1) * HEAD, :]
        kp[span, :] = pr[...]
    for h in range(heads):
        qs[h] = q[:, h * HEAD : (h + 1) * HEAD]
    tiles = count // ROW_TILE

    def body(i, carry):
        h, t = i // tiles, i % tiles
        at = pl.ds(pl.multiple_of(t * ROW_TILE, ROW_TILE), ROW_TILE)
        g = h // 2
        s = dot(ks[g], qs[h, at, :], NT)
        s = jnp.where(kp[...] <= lim[:, at], s, FILL)
        top = jnp.max(s, axis=0, keepdims=True)
        p = jnp.exp2((s - top) * SCORE)
        total = jnp.sum(p, axis=0, keepdims=True)
        o = dot(vt[g], p.astype(bf16))
        ot[h, :, at] = o / total
        lse[h, :, at] = top * SCORE + jnp.log2(total)
        return carry

    lax.fori_loop(0, heads * tiles, body, 0)
    out = ot[...].reshape(heads * HEAD, count).T.astype(bf16)
    m = count // n
    for j in range(n):
        mixed[j][...] = out[j * m : (j + 1) * m, :]


def attend_back_kernel(n, last, q, lim, kv, kpos, lse, ot, *refs):
    dos_in, refs = refs[:n], refs[n:]
    if last:
        (dq_in, cos, sin), refs = refs[:3], refs[3:]
    dkv, dq_out = refs[:2]
    qs, dos, ks, vs, kt, delta, dk, dv, dqt = refs[2:]
    count = q.shape[0]
    heads = q.shape[1] // HEAD
    m = count // n
    for j in range(n):
        block = dos_in[j][...]
        turned = block.astype(f32).T
        for h in range(heads):
            span = slice(h * HEAD, (h + 1) * HEAD)
            dos[h, j * m : (j + 1) * m, :] = block[:, span]
            delta[h, :, j * m : (j + 1) * m] = jnp.sum(
                turned[span, :] * ot[h, :, j * m : (j + 1) * m], axis=0, keepdims=True
            )
    k_turned = kv[:, 0:128].astype(f32).T.astype(bf16)
    for g in range(2):
        ks[g] = kv[:, g * HEAD : (g + 1) * HEAD]
        vs[g] = kv[:, 128 + g * HEAD : 128 + (g + 1) * HEAD]
        kt[g] = k_turned[g * HEAD : (g + 1) * HEAD, :]
    for h in range(heads):
        qs[h] = q[:, h * HEAD : (h + 1) * HEAD]
    dk[...] = jnp.zeros_like(dk)
    dv[...] = jnp.zeros_like(dv)
    tiles = count // ROW_TILE

    def body(i, carry):
        h, t = i // tiles, i % tiles
        at = pl.ds(pl.multiple_of(t * ROW_TILE, ROW_TILE), ROW_TILE)
        g = h // 2
        q_h, do_h = qs[h, at, :], dos[h, at, :]
        s = dot(ks[g], q_h, NT)
        p = jnp.where(kpos[...] <= lim[:, at], jnp.exp2(s * SCORE - lse[h, :, at]), 0.0)
        dp = dot(vs[g], do_h, NT)
        ds = (p * (dp - delta[h, :, at])).astype(bf16)
        dv[g] += dot(p.astype(bf16), do_h)
        dk[g] += dot(ds, q_h)
        dqt[h, :, at] = dot(kt[g], ds)
        return carry

    lax.fori_loop(0, heads * tiles, body, 0)
    scale = HEAD ** (-0.5)
    dkv[...] = jnp.concatenate([dk[0] * scale, dk[1] * scale, dv[0], dv[1]], axis=1).astype(dkv.dtype)
    if last:
        whole = ((dqt[...] + dq_in[...]).reshape(heads * HEAD, count) * scale).T
        for half in range(2):
            lanes = slice(half * 128, (half + 1) * 128)
            dq_out[:, lanes] = turn(whole[:, lanes], cos[...], -sin[...]).astype(bf16)
    else:
        dq_out[...] = dqt[...]


def middle_kernel(n, x, gain, wa, wb, *refs):
    mixed, (middle, second) = refs[:n], refs[n:]
    rows = wa.shape[1]
    both = jnp.concatenate([r[...] for r in mixed], axis=1)
    value = x[...].astype(f32) + dot(both, rows_of((wa, wb), rows), NT)
    middle[...] = value
    r = lax.rsqrt(jnp.mean(value * value, axis=-1, keepdims=True) + EPS)
    second[...] = (value * r * gain[...]).astype(bf16)


def middle_back_kernel(n, middle, gain, cot, wa, wb, *refs):
    parts, refs = refs[:n], refs[n:]
    middle_grad, branch, gain_grad = refs[:3]
    pieces = refs[3:]
    u = parts[0][...].astype(f32)
    for r in parts[1:]:
        u = u + r[...].astype(f32)
    value = middle[...]
    r = lax.rsqrt(jnp.mean(value * value, axis=-1, keepdims=True) + EPS)
    normal = value * r
    gain_grad[...] = jnp.sum(u * normal, axis=0, keepdims=True)
    scaled = u * gain[...]
    grad = cot[...].astype(f32) + r * (scaled - normal * jnp.mean(scaled * normal, axis=-1, keepdims=True))
    middle_grad[...] = grad
    low = grad.astype(bf16)
    branch[...] = low
    rows = wa.shape[1]
    out = dot(low, rows_of((wa, wb), rows)).astype(bf16)
    wide = out.shape[1] // n
    for j in range(n):
        pieces[j][...] = out[:, j * wide : (j + 1) * wide]


def pick(table, index):
    lane = lax.broadcasted_iota(jnp.int32, table.shape, 1)
    return jnp.sum(jnp.where(lane == index, table, 0.0), axis=1, keepdims=True)


def expert_kernel(n, pieces, chosen, kept, router, *refs):
    xs, cs, ws, refs = refs[:n], refs[n : 2 * n], refs[2 * n : 2 * n + pieces], refs[2 * n + pieces :]
    outs, (active_out, gate_out, up_out, router_grad) = refs[:n], refs[n : n + 4]
    x, c, w, total, soft, share = refs[n + 4 :]
    step, steps = pl.program_id(0), pl.num_programs(0)
    m = xs[0].shape[0]
    eb = EXPERTS_PER_STEP
    fe = ws[0].shape[3]
    wide = eb * fe

    @pl.when(step == 0)
    def _():
        for j in range(n):
            x[j * m : (j + 1) * m, :] = xs[j][...]
            c[j * m : (j + 1) * m, :] = cs[j][...]
        logits = jnp.where(chosen[...] > 0.0, dot(x[...], router[...]), FILL)
        top = jnp.max(logits, axis=1, keepdims=True)
        e = jnp.where(chosen[...] > 0.0, jnp.exp(logits - top), 0.0)
        soft[...] = e / jnp.sum(e, axis=1, keepdims=True)
        total[...] = jnp.zeros_like(total)
        share[...] = jnp.zeros_like(share)

    first = 0
    for r in ws:
        span = slice(first, first + r.shape[2])
        first += r.shape[2]
        for kind in range(3):
            for i in range(eb):
                w[span, kind * wide + i * fe : kind * wide + (i + 1) * fe] = r[kind, i]
    gu = dot(x[...], w[:, : 2 * wide])
    down = dot(c[...], w[:, 2 * wide :])
    table = soft[...] * kept[...]
    lane = lax.broadcasted_iota(jnp.int32, share.shape, 1)
    sums = jnp.zeros(share.shape, f32)
    gate_parts, up_parts = [], []
    for i in range(eb):
        span = slice(i * fe, (i + 1) * fe)
        gate, up, d = gu[:, span], gu[:, wide + i * fe : wide + (i + 1) * fe], down[:, span]
        index = step * eb + i
        weight = pick(table, index)
        sig = jax.nn.sigmoid(gate)
        silu = gate * sig
        active = silu * up
        active_out[:, span] = (active * weight).astype(bf16)
        sums = sums + jnp.where(lane == index, jnp.sum(active * d, axis=1, keepdims=True), 0.0)
        ag = d * weight
        gp = (ag * up * (sig * (1.0 + gate * (1.0 - sig)))).astype(bf16)
        ug = (ag * silu).astype(bf16)
        gate_out[:, span] = gp
        up_out[:, span] = ug
        gate_parts.append(gp)
        up_parts.append(ug)
    share[...] += sums
    total[...] += dot(jnp.concatenate(gate_parts + up_parts, axis=1), w[:, : 2 * wide], NT)

    @pl.when(step == steps - 1)
    def _():
        pair = share[...] * kept[...]
        mine = soft[...]
        logit = mine * (pair - jnp.sum(mine * pair, axis=1, keepdims=True))
        high = logit.astype(bf16)
        low = (logit - high.astype(f32)).astype(bf16)
        value = total[...] + (dot(high, router[...], NT) + dot(low, router[...], NT))
        for j in range(n):
            outs[j][...] = value[j * m : (j + 1) * m, :].astype(bf16)
        across = (((0,), (0,)), ((), ()))
        router_grad[...] = dot(high, x[...], across) + dot(low, x[...], across)


def expert_back_kernel(n, pieces, rows, active, gate, up, *refs):
    xs, cs, ws, refs = refs[:n], refs[n : 2 * n], refs[2 * n : 2 * n + pieces], refs[2 * n + pieces :]
    outs, (keep, send) = refs[:n], refs[n : n + 2]
    xt, ct, w, total = refs[n + 2 :]
    step, steps = pl.program_id(0), pl.num_programs(0)
    m = xs[0].shape[0]
    eb = EXPERTS_PER_STEP
    fe = ws[0].shape[3]

    @pl.when(step == 0)
    def _():
        for j in range(n):
            xt[:, j * m : (j + 1) * m] = xs[j][...].T
            ct[:, j * m : (j + 1) * m] = cs[j][...].T
        total[...] = jnp.zeros_like(total)

    first = 0
    for r in ws:
        span = slice(first, first + r.shape[2])
        first += r.shape[2]
        for i in range(eb):
            w[span, i * fe : (i + 1) * fe] = r[0, i]
    total[...] += dot(active[...], w[...], NT)
    half = keep.shape[0]
    for kind, (left, right) in enumerate(((xt, gate), (xt, up), (ct, active))):
        value = dot(left[...], right[...]).astype(bf16)
        for b in range(2 * half):
            target = keep if b < half else send
            for i in range(eb):
                target[b % half, kind, i] = value[b * rows : (b + 1) * rows, i * fe : (i + 1) * fe]

    @pl.when(step == steps - 1)
    def _():
        for j in range(n):
            outs[j][...] = total[j * m : (j + 1) * m, :].astype(bf16)


def qkv_back_kernel(n, rows, dq, dkv, got, cos, sin, wa, wb, *refs):
    xs, refs = refs[:n], refs[n:]
    outs, (grads, gain_grad) = refs[:n], refs[n:]
    m = xs[0].shape[0]
    both = dkv[...].astype(f32)
    if got is not None:
        both = both + got[...].astype(f32)
    grads[:, 0:256] = dq[...]
    grads[:, 256:384] = turn(both[:, 0:128], cos[...], -sin[...]).astype(bf16)
    grads[:, 384:512] = both[:, 128:256].astype(bf16)
    u = dot(grads[...], rows_of((wa, wb), rows), NT)
    sums = jnp.zeros(gain_grad.shape, f32)
    for j in range(n):
        v = xs[j][...].astype(f32)
        r = lax.rsqrt(jnp.mean(v * v, axis=-1, keepdims=True) + EPS)
        part = u[j * m : (j + 1) * m, :]
        sums = sums + jnp.sum(part * (v * r), axis=0, keepdims=True)
        outs[j][...] = part.astype(bf16)
    gain_grad[...] = sums


def weight_back_kernel(n, rows, x1, grads, *refs):
    bs, ms, (keep, send) = refs[:n], refs[n : 2 * n], refs[2 * n :]
    first = dot(x1[...].T, grads[...]).astype(bf16)
    branch = jnp.concatenate([r[...] for r in bs], axis=0)
    mixed = jnp.concatenate([r[...] for r in ms], axis=0)
    second = dot(branch.T, mixed).astype(bf16)
    half = keep.shape[0]
    wide = first.shape[1]
    for b in range(2 * half):
        target = keep if b < half else send
        target[b % half, :, 0:wide] = first[b * rows : (b + 1) * rows, :]
        target[b % half, :, wide:] = second[b * rows : (b + 1) * rows, :]


def put(out, value, where):
    wide = out.shape[1] // where.shape[0]
    if wide % 128:
        out[...] = value
        return
    for i in range(where.shape[0]):
        out[:, pl.ds(pl.multiple_of(where[i] * wide, wide), wide)] = value[:, i * wide : (i + 1) * wide]


def input_kernel(n, where, x, gain, middle_grad, *refs):
    parts, out = refs[:n], refs[n]
    u = parts[0][...].astype(f32)
    for r in parts[1:]:
        u = u + r[...].astype(f32)
    v = x[...].astype(f32)
    r = lax.rsqrt(jnp.mean(v * v, axis=-1, keepdims=True) + EPS)
    normal = v * r
    scaled = u * gain[...]
    grad = r * (scaled - normal * jnp.mean(scaled * normal, axis=-1, keepdims=True))
    put(out, (middle_grad[...] + grad).astype(bf16), where)


def output_kernel(n, where, middle, *refs):
    parts, out = refs[:n], refs[n]
    u = middle[...]
    for r in parts:
        u = u + r[...].astype(f32)
    put(out, u.astype(bf16), where)


def tensor_shift(v, s):
    n = lax.axis_size("tensor")
    return lax.ppermute(v, "tensor", [(i, (i + s) % n) for i in range(n)])


def swap_x(v):
    return lax.ppermute(v, "seq", [(0, 1), (1, 0)])


def swap_core(v):
    return lax.ppermute(v, "dp", [(i, i ^ 1) for i in range(4)])


def swap_y(v):
    return lax.ppermute(v, "dp", [(i, i ^ 2) for i in range(4)])


def swap_xy(v):
    return lax.ppermute(v, ("dp", "seq"), [(i, i ^ 5) for i in range(8)])


def plane_gather(v, fancy):
    if fancy:
        near = jnp.stack([v, swap_x(v), swap_y(v), swap_xy(v)])
        return near, swap_core(near)
    every = lax.all_gather(v, ("dp", "seq"), axis=0, tiled=False)
    half = every.shape[0] // 2
    return every[:half], every[half:]


def plane_scatter(keep, send, fancy):
    if not fancy:
        both = jnp.concatenate([keep, send], axis=0)
        return lax.psum_scatter(both, ("dp", "seq"), scatter_dimension=0, tiled=False).astype(f32)
    near = keep.astype(f32) + swap_core(send).astype(f32)
    low = near[1:].astype(bf16)
    return (
        near[0]
        + swap_x(low[0]).astype(f32)
        + swap_y(low[1]).astype(f32)
        + swap_xy(low[2]).astype(f32)
    )


def plane_scatter_large(keep, send, fancy):
    if not fancy:
        return plane_scatter(keep, send, fancy)
    near = keep.astype(f32) + swap_core(send).astype(f32)
    half = near.shape[-2] // 2
    far = near[3].astype(bf16)
    got_x, got_y = swap_x(far[..., :half, :]), swap_y(far[..., half:, :])
    to_y = jnp.concatenate([near[2][..., :half, :] + got_x.astype(f32), near[2][..., half:, :]], axis=-2)
    to_x = jnp.concatenate([near[1][..., :half, :], near[1][..., half:, :] + got_y.astype(f32)], axis=-2)
    return near[0] + swap_x(to_x.astype(bf16)).astype(f32) + swap_y(to_y.astype(bf16)).astype(f32)


def gather_experts(packed, fancy):
    if not fancy:
        every = lax.all_gather(packed, ("dp", "seq"), axis=2, tiled=True)
        return [every]
    half = packed.shape[2] // 2
    on_x, on_y = swap_x(packed), swap_y(packed)
    far_a = swap_x(on_y[:, :, :half])
    far_b = swap_y(on_x[:, :, half:])
    near = [packed, on_x, on_y, far_a, far_b]
    return near + [swap_core(v) for v in near]


def per_device(
    hidden_in,
    cotangent,
    piece_starts,
    expert_ids,
    claim_order,
    first_gain,
    second_gain,
    router,
    w_query,
    key_projection,
    value_projection,
    w_out,
    w_gate,
    w_up,
    w_down,
):
    n_dp, n_seq, n = lax.axis_size("dp"), lax.axis_size("seq"), lax.axis_size("tensor")
    fancy = n_dp == 4 and n_seq == 2
    n_p = n_dp * n_seq
    me = lax.axis_index("tensor")
    seq_at = lax.axis_index("seq")
    place = lax.axis_index("dp") * n_seq + seq_at
    m, d = hidden_in.shape[1:]
    count = m * n
    rows = d // n_p
    if hidden_in.shape[0] != 1 or expert_ids.shape[1] != count:
        raise ValueError("shapes")
    wide = w_query.shape[1]
    order = (0, 1, 4, 5, 2, 3, 6, 7) if fancy else tuple(range(n_p))
    where = (place ^ jnp.array(order, jnp.int32)) if fancy else jnp.arange(n_p, dtype=jnp.int32)

    own, cot = hidden_in[0], cotangent[0]
    if fancy:
        own, cot = whole_call(
            reorder_kernel, (sds(own.shape, bf16), sds(cot.shape, bf16)), (where, own, cot), prefetch=1
        )
    xs = [own] + [tensor_shift(own, j) for j in range(1, n)]

    qkv_w = jnp.concatenate([w_query, key_projection, value_projection], axis=1)
    cols = qkv_w.shape[1]
    small = jnp.concatenate([router.reshape(-1), first_gain, second_gain])
    size = small.shape[0]
    small = jnp.pad(small, (0, 16 * cols - size)).reshape(16, cols)
    wa, wb = plane_gather(jnp.concatenate([qkv_w, small], axis=0), fancy)
    tail = jnp.concatenate([wa[:, rows:], wb[:, rows:]], axis=0).reshape(n_p, -1)[:, :size]
    tails = [tail] + [tensor_shift(tail, j) for j in range(1, n)]
    stacked = jnp.stack(tails).astype(f32)
    which = (me - jnp.arange(n)) % n
    pick_rows = (which[:, None] == jnp.arange(n)[None, :]).astype(f32)
    natural = jnp.sum(pick_rows[:, :, None, None] * stacked[None], axis=1)
    shard = first_gain.shape[0]
    gain_one = jnp.transpose(natural[:, :, size - 2 * shard : size - shard], (1, 0, 2)).reshape(1, d)
    gain_two = jnp.transpose(natural[:, :, size - shard :], (1, 0, 2)).reshape(1, d)
    router_all = (
        jnp.transpose(natural[:, :, : size - 2 * shard].reshape(n, n_p, shard, E), (1, 0, 2, 3))
        .reshape(d, E)
        .astype(bf16)
    )

    blocks = (me - jnp.arange(n, dtype=jnp.int32)) % n
    positions = (seq_at * count + blocks[:, None] * m + jnp.arange(m, dtype=jnp.int32)[None, :]).reshape(count)
    starts = piece_starts[0]
    inside = (positions[:, None] >= starts[None, :]) & (positions[:, None] < starts[None, :] + PIECE)
    limit = jnp.maximum(
        positions, jnp.max(jnp.where(inside, starts[None, :] + PIECE - 1, -1), axis=1)
    ).reshape(1, count)
    half = HEAD // 2
    freqs = jnp.exp(jnp.arange(half).astype(f32) * (-2.0 * math.log(10000.0) / HEAD))
    angles = positions.astype(f32)[:, None] * freqs[None, :]
    cosine, sine = jnp.cos(angles), jnp.sin(angles)
    cos = jnp.concatenate([cosine] * 4, axis=1)
    sin = jnp.concatenate([-sine, sine] * 2, axis=1)

    ids, claim = expert_ids[0], claim_order[0]
    experts = jnp.arange(E, dtype=jnp.int32)
    chosen = jnp.max((ids[:, :, None] == experts[None, None, :]).astype(f32), axis=1)
    before = (claim[None, :] < claim[:, None]).astype(bf16)
    taken = dot(before, chosen.astype(bf16))
    kept = jnp.where(taken < CAP, chosen, 0.0)
    tables = jnp.concatenate([chosen, kept], axis=1).reshape(n, m, 2 * E)
    tables = jnp.sum(
        (blocks[:, None] == jnp.arange(n)[None, :]).astype(f32)[:, :, None, None] * tables[None], axis=1
    ).reshape(count, 2 * E)
    chosen, kept = tables[:, :E], tables[:, E:]

    x1, q, kv = whole_call(
        functools.partial(qkv_kernel, n, rows),
        (sds((count, d), bf16), sds((count, wide), bf16), sds((count, 256), bf16)),
        (*xs, gain_one, cos, sin, wa, wb),
        flops=2 * count * d * cols,
    )
    key_pos = positions.reshape(count, 1)
    if fancy:
        kvs = [kv, swap_x(kv)]
        poss = [key_pos, key_pos + (1 - 2 * seq_at) * count]
    else:
        kvs = [lax.all_gather(kv, "seq", axis=0, tiled=True)]
        poss = [lax.all_gather(key_pos.astype(f32), "seq", axis=0, tiled=True).astype(jnp.int32)]
    span = sum(v.shape[0] for v in kvs)
    heads = wide // HEAD
    got = whole_call(
        functools.partial(attend_kernel, len(kvs), n),
        tuple([sds((m, wide), bf16)] * n) + (sds((heads, HEAD, count), f32), sds((heads, 1, count), f32)),
        (q, limit, *kvs, *poss),
        scratch=(
            pltpu.VMEM((heads, count, HEAD), bf16),
            pltpu.VMEM((2, span, HEAD), bf16),
            pltpu.VMEM((2, HEAD, span), bf16),
            pltpu.VMEM((span, 1), jnp.int32),
        ),
        flops=4 * count * span * wide * 4,
    )
    mixed, (mixed_t, lse) = got[:n], got[n:]

    out_w = jnp.concatenate([w_out] + [tensor_shift(w_out, -j) for j in range(1, n)], axis=1)
    oa, ob = plane_gather(out_w, fancy)
    mine = [mixed[0]] + [tensor_shift(mixed[j], -j) for j in range(1, n)]
    middle, second = whole_call(
        functools.partial(middle_kernel, n),
        (sds((m, d), f32), sds((m, d), bf16)),
        (own, gain_two, oa, ob, *mine),
        flops=2 * m * d * d,
    )

    seconds = [second] + [tensor_shift(second, j) for j in range(1, n)]
    cots = [cot] + [tensor_shift(cot, j) for j in range(1, n)]
    ws = gather_experts(jnp.stack([w_gate, w_up, w_down]), fancy)
    eb, fe = EXPERTS_PER_STEP, w_gate.shape[2]
    steps = E // eb
    block = pl.BlockSpec((count, eb * fe), lambda s: (0, s))
    wide_out = sds((count, E * fe), bf16)
    got = pl.pallas_call(
        functools.partial(expert_kernel, n, len(ws)),
        out_shape=tuple([sds((m, d), bf16)] * n) + (wide_out, wide_out, wide_out, sds((E, d), f32)),
        grid=(steps,),
        in_specs=[full((count, E)), full((count, E)), full((d, E))]
        + [full((m, d))] * (2 * n)
        + [pl.BlockSpec((3, eb, w.shape[2], fe), lambda s: (0, s, 0, 0)) for w in ws],
        out_specs=[full((m, d))] * n + [block] * 3 + [full((E, d))],
        scratch_shapes=[
            pltpu.VMEM((count, d), bf16),
            pltpu.VMEM((count, d), bf16),
            pltpu.VMEM((d, 3 * eb * fe), bf16),
            pltpu.VMEM((count, d), f32),
            pltpu.VMEM((count, E), f32),
            pltpu.VMEM((count, E), f32),
        ],
        cost_estimate=pl.CostEstimate(
            flops=10 * count * d * E * fe, bytes_accessed=3 * d * E * fe * 2, transcendentals=count * E * fe
        ),
    )(chosen, kept, router_all, *seconds, *cots, *ws)
    second_parts, (active, gate_g, up_g, router_part) = got[:n], got[n:]
    half_p = n_p // 2
    grad_shape = sds((half_p, 3, E, rows, fe), bf16)
    grad_block = pl.BlockSpec((half_p, 3, eb, rows, fe), lambda s: (0, 0, s, 0, 0))
    got = pl.pallas_call(
        functools.partial(expert_back_kernel, n, len(ws), rows),
        out_shape=tuple([sds((m, d), bf16)] * n) + (grad_shape, grad_shape),
        grid=(steps,),
        in_specs=[block] * 3
        + [full((m, d))] * (2 * n)
        + [pl.BlockSpec((1, eb, w.shape[2], fe), lambda s: (2, s, 0, 0)) for w in ws],
        out_specs=[full((m, d))] * n + [grad_block] * 2,
        scratch_shapes=[
            pltpu.VMEM((d, count), bf16),
            pltpu.VMEM((d, count), bf16),
            pltpu.VMEM((d, eb * fe), bf16),
            pltpu.VMEM((count, d), f32),
        ],
        cost_estimate=pl.CostEstimate(
            flops=8 * count * d * E * fe, bytes_accessed=4 * d * E * fe * 2, transcendentals=0
        ),
    )(active, gate_g, up_g, *seconds, *cots, *ws)
    out_parts, (keep, send) = got[:n], got[n:]

    sums = [second_parts[0]] + [tensor_shift(second_parts[j], -j) for j in range(1, n)]
    got = whole_call(
        functools.partial(middle_back_kernel, n),
        (sds((m, d), f32), sds((m, d), bf16), sds((1, d), f32)) + tuple([sds((m, wide), bf16)] * n),
        (middle, gain_two, cot, oa, ob, *sums),
        flops=2 * m * d * d,
    )
    (middle_grad, branch, gain_two_part), pieces = got[:3], got[3:]
    mixed_grads = [pieces[0]] + [tensor_shift(pieces[j], j) for j in range(1, n)]
    branches = [branch] + [tensor_shift(branch, j) for j in range(1, n)]

    def attend_back(kv_one, pos_one, dtype, extra):
        one = kv_one.shape[0]
        last = bool(extra)
        return whole_call(
            functools.partial(attend_back_kernel, n, last),
            (
                sds((one, 256), dtype),
                sds((count, wide), bf16) if last else sds((heads, HEAD, count), f32),
            ),
            (q, limit, kv_one, pos_one, lse, mixed_t, *mixed_grads, *extra),
            scratch=(
                pltpu.VMEM((heads, count, HEAD), bf16),
                pltpu.VMEM((heads, count, HEAD), bf16),
                pltpu.VMEM((2, one, HEAD), bf16),
                pltpu.VMEM((2, one, HEAD), bf16),
                pltpu.VMEM((2, HEAD, one), bf16),
                pltpu.VMEM((heads, 1, count), f32),
                pltpu.VMEM((2, one, HEAD), f32),
                pltpu.VMEM((2, one, HEAD), f32),
                pltpu.VMEM((heads, HEAD, count), f32),
            ),
            flops=10 * count * one * wide * 4,
        )

    if fancy:
        far, dq_far = attend_back(kvs[1], poss[1], bf16, ())
        got_kv = (swap_x(far),)
        dkv, dq = attend_back(kvs[0], poss[0], f32, (dq_far, cos, sin))
    else:
        zero = jnp.zeros((heads, HEAD, count), f32)
        dkv, dq = attend_back(kvs[0], poss[0], bf16, (zero, cos, sin))
        dkv = lax.psum_scatter(dkv, "seq", scatter_dimension=0, tiled=True)
        got_kv = (jnp.zeros((count, 256), bf16),)

    got = whole_call(
        functools.partial(qkv_back_kernel, n, rows),
        tuple([sds((m, d), bf16)] * n) + (sds((count, cols), bf16), sds((1, d), f32)),
        (dq, dkv, *got_kv, cos, sin, wa, wb, *xs),
        flops=2 * count * d * cols,
    )
    first_parts, (grads, gain_one_part) = got[:n], got[n:]
    sums = [first_parts[0]] + [tensor_shift(first_parts[j], -j) for j in range(1, n)]
    weight_shape = sds((half_p, rows, cols + wide), bf16)
    weight_keep, weight_send = whole_call(
        functools.partial(weight_back_kernel, n, rows),
        (weight_shape, weight_shape),
        (x1, grads, *branches, *mixed),
        flops=2 * count * d * (cols + wide),
    )

    (input_grad,) = whole_call(
        functools.partial(input_kernel, n), (sds((m, d), bf16),), (where, own, gain_one, middle_grad, *sums), prefetch=1
    )
    out_sums = [out_parts[0]] + [tensor_shift(out_parts[j], -j) for j in range(1, n)]
    (output,) = whole_call(
        functools.partial(output_kernel, n), (sds((m, d), bf16),), (where, middle, *out_sums), prefetch=1
    )
    weights = plane_scatter(weight_keep, weight_send, fancy)
    expert_grads = plane_scatter_large(keep, send, fancy)

    vectors = jnp.concatenate([router_part, gain_one_part, gain_two_part], axis=0)
    lines = vectors.shape[0]
    vectors = jnp.transpose(vectors.reshape(lines, n_p, rows), (1, 0, 2))
    if fancy:
        vectors = vectors[:4] + swap_core(vectors[4:])
        vectors = vectors[:2] + swap_y(vectors[2:])
        vectors = vectors[0] + swap_x(vectors[1])
    else:
        vectors = lax.psum_scatter(vectors, ("dp", "seq"), scatter_dimension=0, tiled=False)
    total = vectors
    for j in range(1, n):
        total = total + tensor_shift(vectors, j)
    total = lax.dynamic_slice_in_dim(total, me * shard, shard, axis=1)
    kv_wide = key_projection.shape[1]
    return (
        output[None],
        input_grad[None],
        weights[:, :wide],
        weights[:, wide : wide + kv_wide],
        weights[:, wide + kv_wide : cols],
        weights[:, cols:],
        expert_grads[0],
        expert_grads[1],
        expert_grads[2],
        total[E],
        total[E + 1],
        total[:E].T,
    )


def solution(mesh):
    placed = (
        P("dp", ("seq", "tensor"), None),
        P("dp", ("seq", "tensor"), None),
        P("dp", None),
        P("dp", "seq", None),
        P("dp", "seq"),
        P(("dp", "seq", "tensor")),
        P(("dp", "seq", "tensor")),
        P(("dp", "seq", "tensor"), None),
        P(("dp", "seq"), "tensor"),
        P(("dp", "seq"), "tensor"),
        P(("dp", "seq"), "tensor"),
        P(("dp", "seq"), "tensor"),
        P(None, ("dp", "seq"), "tensor"),
        P(None, ("dp", "seq"), "tensor"),
        P(None, ("dp", "seq"), "tensor"),
    )
    return jax.shard_map(
        per_device,
        mesh=mesh,
        in_specs=placed,
        out_specs=(
            P("dp", ("seq", "tensor"), None),
            P("dp", ("seq", "tensor"), None),
            P(("dp", "seq"), "tensor"),
            P(("dp", "seq"), "tensor"),
            P(("dp", "seq"), "tensor"),
            P(("dp", "seq"), "tensor"),
            P(None, ("dp", "seq"), "tensor"),
            P(None, ("dp", "seq"), "tensor"),
            P(None, ("dp", "seq"), "tensor"),
            P(("dp", "seq", "tensor")),
            P(("dp", "seq", "tensor")),
            P(("dp", "seq", "tensor"), None),
        ),
        check_vma=False,
    )
```

```python
import functools
import math

import jax
import jax.numpy as jnp
from jax import lax
from jax.experimental import pallas as pl
from jax.experimental.pallas import tpu as pltpu
from jax.sharding import PartitionSpec as P

HEAD = 64
E = 16
PIECE = 256
CAP = 320
EPS = 1e-06
FILL = -1e30
EXPERTS_PER_STEP = 2
ROW_TILE = 256
LINES = 32
f32 = jnp.float32
bf16 = jnp.bfloat16

NT = (((1,), (1,)), ((), ()))
NN = (((1,), (0,)), ((), ()))


def dot(a, b, dims=NN):
    return lax.dot_general(a, b, dims, preferred_element_type=f32)


def full(shape):
    rank = len(shape)
    return pl.BlockSpec(shape, lambda *_: (0,) * rank)


def whole_call(body, outs, args, scratch=(), flops=0, prefetch=0):
    moved = sum(math.prod(a.shape) * a.dtype.itemsize for a in (*args, *outs))
    return pl.pallas_call(
        body,
        out_shape=outs,
        grid_spec=pltpu.PrefetchScalarGridSpec(
            num_scalar_prefetch=prefetch,
            grid=(1,),
            in_specs=[full(a.shape) for a in args[prefetch:]],
            out_specs=[full(o.shape) for o in outs],
            scratch_shapes=list(scratch),
        ),
        cost_estimate=pl.CostEstimate(flops=0, bytes_accessed=0, transcendentals=0),
    )(*args)


def sds(shape, dtype):
    return jax.ShapeDtypeStruct(shape, dtype)


def turn(v, cos, sin):
    lane = lax.broadcasted_iota(jnp.int32, v.shape, 1) % HEAD
    other = jnp.where(lane < HEAD // 2, pltpu.roll(v, 128 - HEAD // 2, 1), pltpu.roll(v, HEAD // 2, 1))
    return v * cos + other * sin


def lay(out, stacks, where, rows):
    first = 0
    for r in stacks:
        for i in range(r.shape[0]):
            out[pl.ds(pl.multiple_of(where[first + i] * rows, rows), rows), :] = r[i, 0:rows, :]
        first += r.shape[0]


def qkv_kernel(n, rows, where, *refs):
    xs, (gain, cos, sin, wa, wb), (x1, q, kv, w) = refs[:n], refs[n : n + 5], refs[n + 5 :]
    lay(w, (wa, wb), where, rows)
    m = xs[0].shape[0]
    x_width = x1.shape[1]
    for j in range(n):
        v = xs[j][:, : x_width].astype(f32)
        r = lax.rsqrt(jnp.mean(v * v, axis=-1, keepdims=True) + EPS)
        x1[j * m : (j + 1) * m, :] = (v * r * gain[...]).astype(bf16)
    out = dot(x1[...], w[...])
    c, s = cos[...], sin[...]
    q[:, 0:128] = turn(out[:, 0:128], c, s).astype(bf16)
    q[:, 128:256] = turn(out[:, 128:256], c, s).astype(bf16)
    kv[:, 0:128] = turn(out[:, 256:384], c, s).astype(bf16)
    kv[:, 128:256] = out[:, 384:512].astype(bf16)


SCORE = HEAD ** (-0.5) * math.log2(math.e)


def attend_kernel(parts, n, q, lim, *refs):
    kvs, poss = refs[:parts], refs[parts : 2 * parts]
    mixed, (ot, lse) = refs[2 * parts : 2 * parts + n], refs[2 * parts + n : 2 * parts + n + 2]
    qs, ks, vt, kp = refs[2 * parts + n + 2 :]
    count = q.shape[0]
    heads = q.shape[1] // HEAD
    first = 0
    for kvr, pr in zip(kvs, poss):
        span = slice(first, first + kvr.shape[0])
        first += kvr.shape[0]
        v = kvr[:, 128:256].astype(f32).T.astype(bf16)
        for g in range(2):
            ks[g, span, :] = kvr[:, g * HEAD : (g + 1) * HEAD]
            vt[g, :, span] = v[g * HEAD : (g + 1) * HEAD, :]
        kp[span, :] = pr[...]
    for h in range(heads):
        qs[h] = q[:, h * HEAD : (h + 1) * HEAD]
    tiles = count // ROW_TILE

    def body(i, carry):
        h, t = i // tiles, i % tiles
        at = pl.ds(pl.multiple_of(t * ROW_TILE, ROW_TILE), ROW_TILE)
        g = h // 2
        s = dot(ks[g], qs[h, at, :], NT)
        s = jnp.where(kp[...] <= lim[:, at], s, FILL)
        top = jnp.max(s, axis=0, keepdims=True)
        p = jnp.exp2((s - top) * SCORE)
        total = jnp.sum(p, axis=0, keepdims=True)
        o = dot(vt[g], p.astype(bf16))
        ot[h, :, at] = o / total
        lse[h, :, at] = top * SCORE + jnp.log2(total)
        return carry

    lax.fori_loop(0, heads * tiles, body, 0)
    out = ot[...].reshape(heads * HEAD, count).T.astype(bf16)
    m = count // n
    for j in range(n):
        mixed[j][...] = out[j * m : (j + 1) * m, :]


def attend_back_kernel(n, last, q, lim, kv, kpos, lse, ot, *refs):
    dos_in, refs = refs[:n], refs[n:]
    if last:
        (dq_in, cos, sin), refs = refs[:3], refs[3:]
    dkv, dq_out = refs[:2]
    qs, dos, ks, vs, kt, delta, dk, dv, dqt = refs[2:]
    count = q.shape[0]
    heads = q.shape[1] // HEAD
    m = count // n
    for j in range(n):
        block = dos_in[j][...]
        turned = block.astype(f32).T
        for h in range(heads):
            span = slice(h * HEAD, (h + 1) * HEAD)
            dos[h, j * m : (j + 1) * m, :] = block[:, span]
            delta[h, :, j * m : (j + 1) * m] = jnp.sum(
                turned[span, :] * ot[h, :, j * m : (j + 1) * m], axis=0, keepdims=True
            )
    k_turned = kv[:, 0:128].astype(f32).T.astype(bf16)
    for g in range(2):
        ks[g] = kv[:, g * HEAD : (g + 1) * HEAD]
        vs[g] = kv[:, 128 + g * HEAD : 128 + (g + 1) * HEAD]
        kt[g] = k_turned[g * HEAD : (g + 1) * HEAD, :]
    for h in range(heads):
        qs[h] = q[:, h * HEAD : (h + 1) * HEAD]
    dk[...] = jnp.zeros_like(dk)
    dv[...] = jnp.zeros_like(dv)
    tiles = count // ROW_TILE

    def body(i, carry):
        h, t = i // tiles, i % tiles
        at = pl.ds(pl.multiple_of(t * ROW_TILE, ROW_TILE), ROW_TILE)
        g = h // 2
        q_h, do_h = qs[h, at, :], dos[h, at, :]
        s = dot(ks[g], q_h, NT)
        p = jnp.where(kpos[...] <= lim[:, at], jnp.exp2(s * SCORE - lse[h, :, at]), 0.0)
        dp = dot(vs[g], do_h, NT)
        ds = (p * (dp - delta[h, :, at])).astype(bf16)
        dv[g] += dot(p.astype(bf16), do_h)
        dk[g] += dot(ds, q_h)
        dqt[h, :, at] = dot(kt[g], ds)
        return carry

    lax.fori_loop(0, heads * tiles, body, 0)
    scale = HEAD ** (-0.5)
    dkv[...] = jnp.concatenate([dk[0] * scale, dk[1] * scale, dv[0], dv[1]], axis=1).astype(dkv.dtype)
    if last:
        whole = ((dqt[...] + dq_in[...]).reshape(heads * HEAD, count) * scale).T
        for half in range(2):
            lanes = slice(half * 128, (half + 1) * 128)
            dq_out[:, lanes] = turn(whole[:, lanes], cos[...], -sin[...]).astype(bf16)
    else:
        dq_out[...] = dqt[...]


def middle_kernel(n, where, x, gain, wa, wb, *refs):
    mixed, (middle, second, w) = refs[:n], refs[n:]
    lay(w, (wa, wb), where, wa.shape[1])
    both = jnp.concatenate([r[...] for r in mixed], axis=1)
    value = x[...].astype(f32) + dot(both, w[...], NT)
    middle[...] = value
    r = lax.rsqrt(jnp.mean(value * value, axis=-1, keepdims=True) + EPS)
    second[...] = (value * r * gain[...]).astype(bf16)


def middle_back_kernel(n, where, middle, gain, cot, wa, wb, *refs):
    parts, refs = refs[:n], refs[n:]
    middle_grad, branch, gain_grad = refs[:3]
    pieces, w = refs[3:-1], refs[-1]
    lay(w, (wa, wb), where, wa.shape[1])
    u = parts[0][...].astype(f32)
    for r in parts[1:]:
        u = u + r[...].astype(f32)
    value = middle[...]
    r = lax.rsqrt(jnp.mean(value * value, axis=-1, keepdims=True) + EPS)
    normal = value * r
    gain_grad[...] = jnp.sum(u * normal, axis=0, keepdims=True)
    scaled = u * gain[...]
    grad = cot[...].astype(f32) + r * (scaled - normal * jnp.mean(scaled * normal, axis=-1, keepdims=True))
    middle_grad[...] = grad
    low = grad.astype(bf16)
    branch[...] = low
    out = dot(low, w[...]).astype(bf16)
    wide = out.shape[1] // n
    for j in range(n):
        pieces[j][...] = out[:, j * wide : (j + 1) * wide]


def pick(table, index):
    lane = lax.broadcasted_iota(jnp.int32, table.shape, 1)
    return jnp.sum(jnp.where(lane == index, table, 0.0), axis=1, keepdims=True)


def expert_kernel(n, chosen, kept, router, ws, *refs):
    xs, cs, refs = refs[:n], refs[n : 2 * n], refs[2 * n :]
    outs, (active_out, gate_out, up_out, router_grad) = refs[:n], refs[n : n + 4]
    x, c, w, total, soft, share = refs[n + 4 :]
    step, steps = pl.program_id(0), pl.num_programs(0)
    m = xs[0].shape[0]
    eb = EXPERTS_PER_STEP
    blocks, _, _, rows, fe = ws.shape
    wide = eb * fe

    @pl.when(step == 0)
    def _():
        for j in range(n):
            x[j * m : (j + 1) * m, :] = xs[j][...]
            c[j * m : (j + 1) * m, :] = cs[j][...]
        logits = jnp.where(chosen[...] > 0.0, dot(x[...], router[...]), FILL)
        top = jnp.max(logits, axis=1, keepdims=True)
        e = jnp.where(chosen[...] > 0.0, jnp.exp(logits - top), 0.0)
        soft[...] = e / jnp.sum(e, axis=1, keepdims=True)
        total[...] = jnp.zeros_like(total)
        share[...] = jnp.zeros_like(share)

    for b in range(blocks):
        for kind in range(3):
            for i in range(eb):
                at = kind * wide + i * fe
                w[b * rows : (b + 1) * rows, at : at + fe] = ws[b, kind, i]
    gu = dot(x[...], w[:, : 2 * wide])
    down = dot(c[...], w[:, 2 * wide :])
    table = soft[...] * kept[...]
    lane = lax.broadcasted_iota(jnp.int32, share.shape, 1)
    sums = jnp.zeros(share.shape, f32)
    gate_parts, up_parts = [], []
    for i in range(eb):
        span = slice(i * fe, (i + 1) * fe)
        gate, up, d = gu[:, span], gu[:, wide + i * fe : wide + (i + 1) * fe], down[:, span]
        index = step * eb + i
        weight = pick(table, index)
        sig = jax.nn.sigmoid(gate)
        silu = gate * sig
        active = silu * up
        active_out[:, span] = (active * weight).astype(bf16)
        sums = sums + jnp.where(lane == index, jnp.sum(active * d, axis=1, keepdims=True), 0.0)
        ag = d * weight
        gp = (ag * up * (sig * (1.0 + gate * (1.0 - sig)))).astype(bf16)
        ug = (ag * silu).astype(bf16)
        gate_out[:, span] = gp
        up_out[:, span] = ug
        gate_parts.append(gp)
        up_parts.append(ug)
    share[...] += sums
    total[...] += dot(jnp.concatenate(gate_parts + up_parts, axis=1), w[:, : 2 * wide], NT)

    @pl.when(step == steps - 1)
    def _():
        pair = share[...] * kept[...]
        mine = soft[...]
        logit = mine * (pair - jnp.sum(mine * pair, axis=1, keepdims=True))
        high = logit.astype(bf16)
        low = (logit - high.astype(f32)).astype(bf16)
        value = total[...] + (dot(high, router[...], NT) + dot(low, router[...], NT))
        for j in range(n):
            outs[j][...] = value[j * m : (j + 1) * m, :].astype(bf16)
        across_rows = (((0,), (0,)), ((), ()))
        router_grad[...] = dot(high, x[...], across_rows) + dot(low, x[...], across_rows)


def expert_back_kernel(n, active, gate, up, ws, *refs):
    xs, cs, refs = refs[:n], refs[n : 2 * n], refs[2 * n :]
    outs, grads = refs[:n], refs[n]
    xt, ct, w, total = refs[n + 1 :]
    step, steps = pl.program_id(0), pl.num_programs(0)
    m = xs[0].shape[0]
    eb = EXPERTS_PER_STEP
    blocks, _, _, rows, fe = ws.shape

    @pl.when(step == 0)
    def _():
        for j in range(n):
            xt[:, j * m : (j + 1) * m] = xs[j][...].T
            ct[:, j * m : (j + 1) * m] = cs[j][...].T
        total[...] = jnp.zeros_like(total)

    for b in range(blocks):
        for i in range(eb):
            w[b * rows : (b + 1) * rows, i * fe : (i + 1) * fe] = ws[b, 0, i]
    total[...] += dot(active[...], w[...], NT)
    for kind, (left, right) in enumerate(((xt, gate), (xt, up), (ct, active))):
        value = dot(left[...], right[...]).astype(bf16)
        for b in range(blocks):
            for i in range(eb):
                grads[b, kind, i] = value[b * rows : (b + 1) * rows, i * fe : (i + 1) * fe]

    @pl.when(step == steps - 1)
    def _():
        for j in range(n):
            outs[j][...] = total[j * m : (j + 1) * m, :].astype(bf16)


def qkv_back_kernel(n, rows, where, dq, dkv, got, cos, sin, wa, wb, *refs):
    xs, refs = refs[:n], refs[n:]
    outs, (grads, gain_grad, w) = refs[:n], refs[n:]
    lay(w, (wa, wb), where, rows)
    m = xs[0].shape[0]
    both = dkv[...].astype(f32)
    if got is not None:
        both = both + got[...].astype(f32)
    grads[:, 0:256] = dq[...]
    grads[:, 256:384] = turn(both[:, 0:128], cos[...], -sin[...]).astype(bf16)
    grads[:, 384:512] = both[:, 128:256].astype(bf16)
    u = dot(grads[...], w[...], NT)
    sums = jnp.zeros(gain_grad.shape, f32)
    x_width = u.shape[1]
    for j in range(n):
        v = xs[j][:, : x_width].astype(f32)
        r = lax.rsqrt(jnp.mean(v * v, axis=-1, keepdims=True) + EPS)
        part = u[j * m : (j + 1) * m, :]
        sums = sums + jnp.sum(part * (v * r), axis=0, keepdims=True)
        outs[j][...] = part.astype(bf16)
    gain_grad[...] = sums


def weight_back_kernel(n, rows, where, x1, grads, router_part, gain_one, gain_two, *refs):
    bs, ms, (keep, send, value, vectors) = refs[:n], refs[n : 2 * n], refs[2 * n :]
    wide = grads.shape[1]
    value[:, :wide] = dot(x1[...].T, grads[...]).astype(bf16)
    branch = jnp.concatenate([r[...] for r in bs], axis=0)
    mixed = jnp.concatenate([r[...] for r in ms], axis=0)
    value[:, wide:] = dot(branch.T, mixed).astype(bf16)
    lines = vectors.shape[1]
    for q in range(vectors.shape[0]):
        columns = slice(q * rows, (q + 1) * rows)
        block = [router_part[:, columns], gain_one[:, columns], gain_two[:, columns]]
        block.append(jnp.zeros((lines - E - 2, rows), f32))
        vectors[q] = jnp.concatenate(block, axis=0).astype(bf16)
    half = keep.shape[0]
    for b in range(2 * half):
        target = keep if b < half else send
        target[b % half, 0:rows, :] = value[pl.ds(pl.multiple_of(where[b] * rows, rows), rows), :]
        target[b % half, rows : rows + lines, 0:rows] = vectors[where[b]]
        target[b % half, rows : rows + lines, rows:] = jnp.zeros((lines, value.shape[1] - rows), bf16)


def input_kernel(n, x, gain, middle_grad, *refs):
    parts, out = refs[:n], refs[n]
    u = parts[0][...].astype(f32)
    for r in parts[1:]:
        u = u + r[...].astype(f32)
    v = x[...].astype(f32)
    r = lax.rsqrt(jnp.mean(v * v, axis=-1, keepdims=True) + EPS)
    normal = v * r
    scaled = u * gain[...]
    grad = r * (scaled - normal * jnp.mean(scaled * normal, axis=-1, keepdims=True))
    out[...] = (middle_grad[...] + grad).astype(bf16)


def output_kernel(n, middle, *refs):
    parts, out = refs[:n], refs[n]
    u = middle[...]
    for r in parts:
        u = u + r[...].astype(f32)
    out[...] = u.astype(bf16)


def across(v, j):
    return lax.ppermute(v, "tensor", [(i, i ^ j) for i in range(lax.axis_size("tensor"))])


def spread(v):
    return [v] + [across(v, j) for j in range(1, lax.axis_size("tensor"))]


def spread_by_two(v):
    if lax.axis_size("tensor") != 4:
        return spread(v)
    near = across(v, 1)
    return [v, near, across(v, 2), across(near, 2)]


def collect(parts):
    return [parts[0]] + [across(parts[j], j) for j in range(1, len(parts))]


def after(v, *others):
    return lax.optimization_barrier((v, *others))[0]


def swap_x(v):
    return lax.ppermute(v, "seq", [(0, 1), (1, 0)])


def swap_core(v):
    return lax.ppermute(v, "dp", [(i, i ^ 1) for i in range(4)])


def swap_y(v):
    return lax.ppermute(v, "dp", [(i, i ^ 2) for i in range(4)])


def swap_xy(v):
    return lax.ppermute(v, ("dp", "seq"), [(i, i ^ 5) for i in range(8)])


def after_all(values, others):
    return lax.optimization_barrier((*values, *others))[: len(values)]


def plane_gather(v, fancy, near=False):
    if fancy and near:
        near = jnp.stack([v, swap_x(v), swap_y(v), swap_xy(v)])
        return near, swap_core(near)
    if fancy:
        near = jnp.stack([v, swap_x(v)])
        near = jnp.concatenate([near, swap_y(near)])
        return near, swap_core(near)
    every = lax.all_gather(v, ("dp", "seq"), axis=0, tiled=False)
    half = every.shape[0] // 2
    return every[:half], every[half:]


def plane_scatter(keep, send, fancy):
    if not fancy:
        both = jnp.concatenate([keep, send], axis=0)
        return lax.psum_scatter(both, ("dp", "seq"), scatter_dimension=0, tiled=False).astype(f32)
    got = swap_core(send)
    far = swap_y((keep[2:].astype(f32) + got[2:].astype(f32)).astype(bf16))
    mine = keep[:2].astype(f32) + got[:2].astype(f32) + far.astype(f32)
    return mine[0] + swap_x(mine[1].astype(bf16)).astype(f32)


def per_device(
    hidden_in,
    cotangent,
    piece_starts,
    expert_ids,
    claim_order,
    first_gain,
    second_gain,
    router,
    w_query,
    key_projection,
    value_projection,
    w_out,
    w_gate,
    w_up,
    w_down,
):
    n_dp, n_seq, n = lax.axis_size("dp"), lax.axis_size("seq"), lax.axis_size("tensor")
    fancy = n_dp == 4 and n_seq == 2
    n_p = n_dp * n_seq
    me = lax.axis_index("tensor")
    seq_at = lax.axis_index("seq")
    place = lax.axis_index("dp") * n_seq + seq_at
    m, d = hidden_in.shape[1:]
    count = m * n
    rows = d // n_p
    if hidden_in.shape[0] != 1 or expert_ids.shape[1] != count:
        raise ValueError("shapes")
    wide = w_query.shape[1]
    order = (0, 1, 4, 5, 2, 3, 6, 7) if fancy else tuple(range(n_p))
    where = (place ^ jnp.array(order, jnp.int32)) if fancy else jnp.arange(n_p, dtype=jnp.int32)

    own, cot = hidden_in[0], cotangent[0]
    joined = m == w_out.shape[0]
    xs = spread(jnp.concatenate([own, w_out], axis=1) if joined else own)

    shard = first_gain.shape[0]
    small = jnp.concatenate([router.reshape(-1), first_gain, second_gain])
    size = small.shape[0]
    qkv_w = jnp.concatenate([w_query, key_projection, value_projection], axis=1)
    cols = qkv_w.shape[1]
    small = jnp.pad(small, (0, 16 * cols - size)).reshape(16, cols)
    wa, wb = plane_gather(jnp.concatenate([qkv_w, small], axis=0), fancy)
    tail = jnp.concatenate([wa[:, rows:], wb[:, rows:]], axis=0).reshape(n_p, -1)[:, :size]
    stacked = jnp.stack(spread(tail)).astype(f32)
    which = me ^ jnp.arange(n)
    pick_rows = (which[:, None] == jnp.arange(n)[None, :]).astype(f32)
    ordered = (where[None, :] == jnp.arange(n_p, dtype=jnp.int32)[:, None]).astype(f32)
    stacked = jnp.sum(pick_rows[:, :, None, None] * stacked[None], axis=1)
    tail = jnp.sum(ordered[:, None, :, None] * stacked[None], axis=2)
    gain_one = tail[:, :, size - 2 * shard : size - shard].reshape(1, d)
    gain_two = tail[:, :, size - shard :].reshape(1, d)
    router_all = tail[:, :, : size - 2 * shard].reshape(d, E).astype(bf16)

    blocks = me ^ jnp.arange(n, dtype=jnp.int32)
    positions = (seq_at * count + blocks[:, None] * m + jnp.arange(m, dtype=jnp.int32)[None, :]).reshape(count)
    starts = piece_starts[0]
    inside = (positions[:, None] >= starts[None, :]) & (positions[:, None] < starts[None, :] + PIECE)
    limit = jnp.maximum(
        positions, jnp.max(jnp.where(inside, starts[None, :] + PIECE - 1, -1), axis=1)
    ).reshape(1, count)
    half = HEAD // 2
    freqs = jnp.exp(jnp.arange(half).astype(f32) * (-2.0 * math.log(10000.0) / HEAD))
    angles = positions.astype(f32)[:, None] * freqs[None, :]
    cosine, sine = jnp.cos(angles), jnp.sin(angles)
    cos = jnp.concatenate([cosine] * 4, axis=1)
    sin = jnp.concatenate([-sine, sine] * 2, axis=1)

    ids, claim = expert_ids[0], claim_order[0]
    experts = jnp.arange(E, dtype=jnp.int32)
    chosen = jnp.max((ids[:, :, None] == experts[None, None, :]).astype(f32), axis=1)
    before = (claim[None, :] < claim[:, None]).astype(bf16)
    taken = dot(before, chosen.astype(bf16))
    kept = jnp.where(taken < CAP, chosen, 0.0)
    tables = jnp.concatenate([chosen, kept], axis=1).reshape(n, m, 2 * E)
    tables = jnp.sum(
        (blocks[:, None] == jnp.arange(n)[None, :]).astype(f32)[:, :, None, None] * tables[None], axis=1
    ).reshape(count, 2 * E)
    chosen, kept = tables[:, :E], tables[:, E:]

    x1, q, kv = whole_call(
        functools.partial(qkv_kernel, n, rows),
        (sds((count, d), bf16), sds((count, wide), bf16), sds((count, 256), bf16)),
        (where, *xs, gain_one, cos, sin, wa, wb),
        scratch=(pltpu.VMEM((d, cols), bf16),),
        flops=2 * count * d * cols,
        prefetch=1,
    )
    key_pos = positions.reshape(count, 1)
    if fancy:
        kvs = [kv, swap_x(kv)]
        poss = [key_pos, key_pos + (1 - 2 * seq_at) * count]
    else:
        kvs = [lax.all_gather(kv, "seq", axis=0, tiled=True)]
        poss = [lax.all_gather(key_pos.astype(f32), "seq", axis=0, tiled=True).astype(jnp.int32)]
    span = sum(v.shape[0] for v in kvs)
    heads = wide // HEAD
    got = whole_call(
        functools.partial(attend_kernel, len(kvs), n),
        tuple([sds((m, wide), bf16)] * n) + (sds((heads, HEAD, count), f32), sds((heads, 1, count), f32)),
        (q, limit, *kvs, *poss),
        scratch=(
            pltpu.VMEM((heads, count, HEAD), bf16),
            pltpu.VMEM((2, span, HEAD), bf16),
            pltpu.VMEM((2, HEAD, span), bf16),
            pltpu.VMEM((span, 1), jnp.int32),
        ),
        flops=4 * count * span * wide * 4,
    )
    mixed, (mixed_t, lse) = got[:n], got[n:]

    out_w = jnp.concatenate([v[:, d:] for v in xs] if joined else spread(w_out), axis=1)
    oa, ob = plane_gather(after(out_w, kv), fancy, near=True)
    mine = collect(mixed)
    middle, second = whole_call(
        functools.partial(middle_kernel, n),
        (sds((m, d), f32), sds((m, d), bf16)),
        (where, own, gain_two, oa, ob, *mine),
        scratch=(pltpu.VMEM((d, n * wide), bf16),),
        flops=2 * m * d * d,
        prefetch=1,
    )

    seconds = spread(second)
    cots = [cot] + spread(after(cot, kv))[1:]
    packed = jnp.stack([w_gate, w_up, w_down])
    ws = lax.all_gather(packed, ("dp", "seq"), axis=0, tiled=False)
    eb, fe = EXPERTS_PER_STEP, w_gate.shape[2]
    steps = E // eb
    block = pl.BlockSpec((count, eb * fe), lambda s: (0, s))
    wide_out = sds((count, E * fe), bf16)
    got = pl.pallas_call(
        functools.partial(expert_kernel, n),
        out_shape=tuple([sds((m, d), bf16)] * n) + (wide_out, wide_out, wide_out, sds((E, d), f32)),
        grid=(steps,),
        in_specs=[full((count, E)), full((count, E)), full((d, E))]
        + [pl.BlockSpec((n_p, 3, eb, rows, fe), lambda s: (0, 0, s, 0, 0))]
        + [full((m, d))] * (2 * n),
        out_specs=[full((m, d))] * n + [block] * 3 + [full((E, d))],
        scratch_shapes=[
            pltpu.VMEM((count, d), bf16),
            pltpu.VMEM((count, d), bf16),
            pltpu.VMEM((d, 3 * eb * fe), bf16),
            pltpu.VMEM((count, d), f32),
            pltpu.VMEM((count, E), f32),
            pltpu.VMEM((count, E), f32),
        ],
        cost_estimate=pl.CostEstimate(flops=0, bytes_accessed=0, transcendentals=0),
    )(chosen, kept, router_all, ws, *seconds, *cots)
    second_parts, (active, gate_g, up_g, router_part) = got[:n], got[n:]
    half_p = n_p // 2
    got = pl.pallas_call(
        functools.partial(expert_back_kernel, n),
        out_shape=tuple([sds((m, d), bf16)] * n) + (sds((n_p, 3, E, rows, fe), bf16),),
        grid=(steps,),
        in_specs=[block] * 3
        + [pl.BlockSpec((n_p, 1, eb, rows, fe), lambda s: (0, 2, s, 0, 0))]
        + [full((m, d))] * (2 * n),
        out_specs=[full((m, d))] * n + [pl.BlockSpec((n_p, 3, eb, rows, fe), lambda s: (0, 0, s, 0, 0))],
        scratch_shapes=[
            pltpu.VMEM((d, count), bf16),
            pltpu.VMEM((d, count), bf16),
            pltpu.VMEM((d, eb * fe), bf16),
            pltpu.VMEM((count, d), f32),
        ],
        cost_estimate=pl.CostEstimate(flops=0, bytes_accessed=0, transcendentals=0),
    )(active, gate_g, up_g, ws, *seconds, *cots)
    out_parts, expert_parts = got[:n], got[n]

    sums = collect(second_parts)
    expert_parts = after(expert_parts, *sums)
    expert_grads = lax.psum_scatter(expert_parts, ("dp", "seq"), scatter_dimension=0, tiled=False).astype(f32)
    got = whole_call(
        functools.partial(middle_back_kernel, n),
        (sds((m, d), f32), sds((m, d), bf16), sds((1, d), f32)) + tuple([sds((m, wide), bf16)] * n),
        (where, middle, gain_two, cot, oa, ob, *sums),
        scratch=(pltpu.VMEM((d, n * wide), bf16),),
        flops=2 * m * d * d,
        prefetch=1,
    )
    (middle_grad, branch, gain_two_part), pieces = got[:3], got[3:]
    mixed_grads = collect(pieces)
    branches = [branch] + spread_by_two(after(branch, *mixed_grads))[1:]

    def attend_back(kv_one, pos_one, dtype, extra):
        one = kv_one.shape[0]
        last = bool(extra)
        return whole_call(
            functools.partial(attend_back_kernel, n, last),
            (
                sds((one, 256), dtype),
                sds((count, wide), bf16) if last else sds((heads, HEAD, count), f32),
            ),
            (q, limit, kv_one, pos_one, lse, mixed_t, *mixed_grads, *extra),
            scratch=(
                pltpu.VMEM((heads, count, HEAD), bf16),
                pltpu.VMEM((heads, count, HEAD), bf16),
                pltpu.VMEM((2, one, HEAD), bf16),
                pltpu.VMEM((2, one, HEAD), bf16),
                pltpu.VMEM((2, HEAD, one), bf16),
                pltpu.VMEM((heads, 1, count), f32),
                pltpu.VMEM((2, one, HEAD), f32),
                pltpu.VMEM((2, one, HEAD), f32),
                pltpu.VMEM((heads, HEAD, count), f32),
            ),
            flops=10 * count * one * wide * 4,
        )

    if fancy:
        far, dq_far = attend_back(kvs[1], poss[1], bf16, ())
        got_kv = (swap_x(far),)
        dkv, dq = attend_back(kvs[0], poss[0], f32, (dq_far, cos, sin))
    else:
        zero = jnp.zeros((heads, HEAD, count), f32)
        dkv, dq = attend_back(kvs[0], poss[0], bf16, (zero, cos, sin))
        dkv = lax.psum_scatter(dkv, "seq", scatter_dimension=0, tiled=True)
        got_kv = (jnp.zeros((count, 256), bf16),)

    dq_ready = after(dq, *branches[1:3])
    got = whole_call(
        functools.partial(qkv_back_kernel, n, rows),
        tuple([sds((m, d), bf16)] * n) + (sds((count, cols), bf16), sds((1, d), f32)),
        (where, dq_ready, dkv, *got_kv, cos, sin, wa, wb, *xs),
        scratch=(pltpu.VMEM((d, cols), bf16),),
        flops=2 * count * d * cols,
        prefetch=1,
    )
    first_parts, (grads, gain_one_part) = got[:n], got[n:]
    sums = collect(first_parts)
    weight_shape = sds((half_p, rows + LINES, cols + wide), bf16)
    weight_keep, weight_send = whole_call(
        functools.partial(weight_back_kernel, n, rows),
        (weight_shape, weight_shape),
        (where, x1, grads, router_part, gain_one_part, gain_two_part, *branches, *mixed),
        scratch=(pltpu.VMEM((d, cols + wide), bf16), pltpu.VMEM((n_p, LINES, rows), bf16)),
        flops=2 * count * d * (cols + wide),
        prefetch=1,
    )

    (input_grad,) = whole_call(
        functools.partial(input_kernel, n), (sds((m, d), bf16),), (own, gain_one, middle_grad, *sums)
    )
    out_sums = [out_parts[0]] + collect([sums[0], *after_all(out_parts[1:], sums)])[1:]
    (output,) = whole_call(
        functools.partial(output_kernel, n), (sds((m, d), bf16),), (middle, *out_sums)
    )
    weights = plane_scatter(weight_keep, weight_send, fancy)
    total = weights[rows : rows + E + 2, :rows]
    for bit in range(n.bit_length() - 1):
        total = total + across(total, 1 << bit)
    total = lax.dynamic_slice_in_dim(total, me * shard, shard, axis=1)
    weights = weights[:rows]
    kv_wide = key_projection.shape[1]
    return (
        output[None],
        input_grad[None],
        weights[:, :wide],
        weights[:, wide : wide + kv_wide],
        weights[:, wide + kv_wide : cols],
        weights[:, cols:],
        expert_grads[0],
        expert_grads[1],
        expert_grads[2],
        total[E],
        total[E + 1],
        total[:E].T,
    )


def solution(mesh):
    placed = (
        P("dp", ("seq", "tensor"), None),
        P("dp", ("seq", "tensor"), None),
        P("dp", None),
        P("dp", "seq", None),
        P("dp", "seq"),
        P(("dp", "seq", "tensor")),
        P(("dp", "seq", "tensor")),
        P(("dp", "seq", "tensor"), None),
        P(("dp", "seq"), "tensor"),
        P(("dp", "seq"), "tensor"),
        P(("dp", "seq"), "tensor"),
        P(("dp", "seq"), "tensor"),
        P(None, ("dp", "seq"), "tensor"),
        P(None, ("dp", "seq"), "tensor"),
        P(None, ("dp", "seq"), "tensor"),
    )
    return jax.shard_map(
        per_device,
        mesh=mesh,
        in_specs=placed,
        out_specs=(
            P("dp", ("seq", "tensor"), None),
            P("dp", ("seq", "tensor"), None),
            P(("dp", "seq"), "tensor"),
            P(("dp", "seq"), "tensor"),
            P(("dp", "seq"), "tensor"),
            P(("dp", "seq"), "tensor"),
            P(None, ("dp", "seq"), "tensor"),
            P(None, ("dp", "seq"), "tensor"),
            P(None, ("dp", "seq"), "tensor"),
            P(("dp", "seq", "tensor")),
            P(("dp", "seq", "tensor")),
            P(("dp", "seq", "tensor"), None),
        ),
        check_vma=False,
    )
```

```python
import functools
import math

import jax
import jax.numpy as jnp
from jax import lax
from jax.experimental import pallas as pl
from jax.experimental.pallas import tpu as pltpu
from jax.sharding import PartitionSpec as P

HEAD = 64
E = 16
PIECE = 256
CAP = 320
EPS = 1e-06
FILL = -1e30
EXPERTS_PER_STEP = 2
ROW_TILE = 256
LINES = 32
f32 = jnp.float32
bf16 = jnp.bfloat16

NT = (((1,), (1,)), ((), ()))
NN = (((1,), (0,)), ((), ()))


def dot(a, b, dims=NN):
    return lax.dot_general(a, b, dims, preferred_element_type=f32)


def full(shape):
    rank = len(shape)
    return pl.BlockSpec(shape, lambda *_: (0,) * rank)


def whole_call(body, outs, args, scratch=(), flops=0, prefetch=0, cost=0):
    moved = sum(math.prod(a.shape) * a.dtype.itemsize for a in (*args, *outs))
    return pl.pallas_call(
        body,
        out_shape=outs,
        grid_spec=pltpu.PrefetchScalarGridSpec(
            num_scalar_prefetch=prefetch,
            grid=(1,),
            in_specs=[full(a.shape) for a in args[prefetch:]],
            out_specs=[full(o.shape) for o in outs],
            scratch_shapes=list(scratch),
        ),
        cost_estimate=pl.CostEstimate(flops=int(cost), bytes_accessed=0, transcendentals=0),
    )(*args)


def sds(shape, dtype):
    return jax.ShapeDtypeStruct(shape, dtype)


def turn(v, cos, sin):
    lane = lax.broadcasted_iota(jnp.int32, v.shape, 1) % HEAD
    other = jnp.where(lane < HEAD // 2, pltpu.roll(v, 128 - HEAD // 2, 1), pltpu.roll(v, HEAD // 2, 1))
    return v * cos + other * sin


def lay(out, stacks, where, rows):
    first = 0
    for r in stacks:
        for i in range(r.shape[0]):
            out[pl.ds(pl.multiple_of(where[first + i] * rows, rows), rows), :] = r[i, 0:rows, :]
        first += r.shape[0]


def qkv_kernel(n, rows, where, *refs):
    xs, (gain, cos, sin, wa, wb), (x1, q, kv, w) = refs[:n], refs[n : n + 5], refs[n + 5 :]
    lay(w, (wa, wb), where, rows)
    m = xs[0].shape[0]
    x_width = x1.shape[1]
    for j in range(n):
        v = xs[j][:, : x_width].astype(f32)
        r = lax.rsqrt(jnp.mean(v * v, axis=-1, keepdims=True) + EPS)
        x1[j * m : (j + 1) * m, :] = (v * r * gain[...]).astype(bf16)
    out = dot(x1[...], w[...])
    c, s = cos[...], sin[...]
    q[:, 0:128] = turn(out[:, 0:128], c, s).astype(bf16)
    q[:, 128:256] = turn(out[:, 128:256], c, s).astype(bf16)
    kv[:, 0:128] = turn(out[:, 256:384], c, s).astype(bf16)
    kv[:, 128:256] = out[:, 384:512].astype(bf16)


SCORE = HEAD ** (-0.5) * math.log2(math.e)


def attend_kernel(parts, n, q, lim, *refs):
    kvs, poss = refs[:parts], refs[parts : 2 * parts]
    mixed, (ot, lse) = refs[2 * parts : 2 * parts + n], refs[2 * parts + n : 2 * parts + n + 2]
    qs, ks, vt, kp = refs[2 * parts + n + 2 :]
    count = q.shape[0]
    heads = q.shape[1] // HEAD
    first = 0
    for kvr, pr in zip(kvs, poss):
        span = slice(first, first + kvr.shape[0])
        first += kvr.shape[0]
        v = kvr[:, 128:256].astype(f32).T.astype(bf16)
        for g in range(2):
            ks[g, span, :] = kvr[:, g * HEAD : (g + 1) * HEAD]
            vt[g, :, span] = v[g * HEAD : (g + 1) * HEAD, :]
        kp[span, :] = pr[...]
    for h in range(heads):
        qs[h] = q[:, h * HEAD : (h + 1) * HEAD]
    tiles = count // ROW_TILE

    def body(i, carry):
        h, t = i // tiles, i % tiles
        at = pl.ds(pl.multiple_of(t * ROW_TILE, ROW_TILE), ROW_TILE)
        g = h // 2
        s = dot(ks[g], qs[h, at, :], NT)
        s = jnp.where(kp[...] <= lim[:, at], s, FILL)
        top = jnp.max(s, axis=0, keepdims=True)
        p = jnp.exp2((s - top) * SCORE)
        total = jnp.sum(p, axis=0, keepdims=True)
        o = dot(vt[g], p.astype(bf16))
        ot[h, :, at] = o / total
        lse[h, :, at] = top * SCORE + jnp.log2(total)
        return carry

    lax.fori_loop(0, heads * tiles, body, 0)
    out = ot[...].reshape(heads * HEAD, count).T.astype(bf16)
    m = count // n
    for j in range(n):
        mixed[j][...] = out[j * m : (j + 1) * m, :]


def attend_back_kernel(n, last, q, lim, kv, kpos, lse, ot, *refs):
    dos_in, refs = refs[:n], refs[n:]
    if last:
        (dq_in, cos, sin), refs = refs[:3], refs[3:]
    dkv, dq_out = refs[:2]
    qs, dos, ks, vs, kt, delta, dk, dv, dqt = refs[2:]
    count = q.shape[0]
    heads = q.shape[1] // HEAD
    m = count // n
    for j in range(n):
        block = dos_in[j][...]
        turned = block.astype(f32).T
        for h in range(heads):
            span = slice(h * HEAD, (h + 1) * HEAD)
            dos[h, j * m : (j + 1) * m, :] = block[:, span]
            delta[h, :, j * m : (j + 1) * m] = jnp.sum(
                turned[span, :] * ot[h, :, j * m : (j + 1) * m], axis=0, keepdims=True
            )
    k_turned = kv[:, 0:128].astype(f32).T.astype(bf16)
    for g in range(2):
        ks[g] = kv[:, g * HEAD : (g + 1) * HEAD]
        vs[g] = kv[:, 128 + g * HEAD : 128 + (g + 1) * HEAD]
        kt[g] = k_turned[g * HEAD : (g + 1) * HEAD, :]
    for h in range(heads):
        qs[h] = q[:, h * HEAD : (h + 1) * HEAD]
    dk[...] = jnp.zeros_like(dk)
    dv[...] = jnp.zeros_like(dv)
    tiles = count // ROW_TILE

    def body(i, carry):
        h, t = i // tiles, i % tiles
        at = pl.ds(pl.multiple_of(t * ROW_TILE, ROW_TILE), ROW_TILE)
        g = h // 2
        q_h, do_h = qs[h, at, :], dos[h, at, :]
        s = dot(ks[g], q_h, NT)
        p = jnp.where(kpos[...] <= lim[:, at], jnp.exp2(s * SCORE - lse[h, :, at]), 0.0)
        dp = dot(vs[g], do_h, NT)
        ds = (p * (dp - delta[h, :, at])).astype(bf16)
        dv[g] += dot(p.astype(bf16), do_h)
        dk[g] += dot(ds, q_h)
        dqt[h, :, at] = dot(kt[g], ds)
        return carry

    lax.fori_loop(0, heads * tiles, body, 0)
    scale = HEAD ** (-0.5)
    dkv[...] = jnp.concatenate([dk[0] * scale, dk[1] * scale, dv[0], dv[1]], axis=1).astype(dkv.dtype)
    if last:
        whole = ((dqt[...] + dq_in[...]).reshape(heads * HEAD, count) * scale).T
        for half in range(2):
            lanes = slice(half * 128, (half + 1) * 128)
            dq_out[:, lanes] = turn(whole[:, lanes], cos[...], -sin[...]).astype(bf16)
    else:
        dq_out[...] = dqt[...]


def middle_kernel(n, where, x, gain, wa, wb, *refs):
    mixed, (middle, second, w) = refs[:n], refs[n:]
    lay(w, (wa, wb), where, wa.shape[1])
    both = jnp.concatenate([r[...] for r in mixed], axis=1)
    value = x[...].astype(f32) + dot(both, w[...], NT)
    middle[...] = value
    r = lax.rsqrt(jnp.mean(value * value, axis=-1, keepdims=True) + EPS)
    second[...] = (value * r * gain[...]).astype(bf16)


def middle_back_kernel(n, where, middle, gain, cot, wa, wb, *refs):
    parts, refs = refs[:n], refs[n:]
    middle_grad, branch, gain_grad = refs[:3]
    pieces, w = refs[3:-1], refs[-1]
    lay(w, (wa, wb), where, wa.shape[1])
    u = parts[0][...].astype(f32)
    for r in parts[1:]:
        u = u + r[...].astype(f32)
    value = middle[...]
    r = lax.rsqrt(jnp.mean(value * value, axis=-1, keepdims=True) + EPS)
    normal = value * r
    gain_grad[...] = jnp.sum(u * normal, axis=0, keepdims=True)
    scaled = u * gain[...]
    grad = cot[...].astype(f32) + r * (scaled - normal * jnp.mean(scaled * normal, axis=-1, keepdims=True))
    middle_grad[...] = grad
    low = grad.astype(bf16)
    branch[...] = low
    out = dot(low, w[...]).astype(bf16)
    wide = out.shape[1] // n
    for j in range(n):
        pieces[j][...] = out[:, j * wide : (j + 1) * wide]


def pick(table, index):
    lane = lax.broadcasted_iota(jnp.int32, table.shape, 1)
    return jnp.sum(jnp.where(lane == index, table, 0.0), axis=1, keepdims=True)


def expert_kernel(n, chosen, kept, router, ws, *refs):
    xs, cs, refs = refs[:n], refs[n : 2 * n], refs[2 * n :]
    outs, (active_out, gate_out, up_out, router_grad) = refs[:n], refs[n : n + 4]
    x, c, w, total, soft, share = refs[n + 4 :]
    step, steps = pl.program_id(0), pl.num_programs(0)
    m = xs[0].shape[0]
    eb = EXPERTS_PER_STEP
    blocks, _, _, rows, fe = ws.shape
    wide = eb * fe

    @pl.when(step == 0)
    def _():
        for j in range(n):
            x[j * m : (j + 1) * m, :] = xs[j][...]
            c[j * m : (j + 1) * m, :] = cs[j][...]
        logits = jnp.where(chosen[...] > 0.0, dot(x[...], router[...]), FILL)
        top = jnp.max(logits, axis=1, keepdims=True)
        e = jnp.where(chosen[...] > 0.0, jnp.exp(logits - top), 0.0)
        soft[...] = e / jnp.sum(e, axis=1, keepdims=True)
        total[...] = jnp.zeros_like(total)
        share[...] = jnp.zeros_like(share)

    for b in range(blocks):
        for kind in range(3):
            for i in range(eb):
                at = kind * wide + i * fe
                w[b * rows : (b + 1) * rows, at : at + fe] = ws[b, kind, i]
    gu = dot(x[...], w[:, : 2 * wide])
    down = dot(c[...], w[:, 2 * wide :])
    table = soft[...] * kept[...]
    lane = lax.broadcasted_iota(jnp.int32, share.shape, 1)
    sums = jnp.zeros(share.shape, f32)
    gate_parts, up_parts = [], []
    for i in range(eb):
        span = slice(i * fe, (i + 1) * fe)
        gate, up, d = gu[:, span], gu[:, wide + i * fe : wide + (i + 1) * fe], down[:, span]
        index = step * eb + i
        weight = pick(table, index)
        sig = jax.nn.sigmoid(gate)
        silu = gate * sig
        active = silu * up
        active_out[:, span] = (active * weight).astype(bf16)
        sums = sums + jnp.where(lane == index, jnp.sum(active * d, axis=1, keepdims=True), 0.0)
        ag = d * weight
        gp = (ag * up * (sig * (1.0 + gate * (1.0 - sig)))).astype(bf16)
        ug = (ag * silu).astype(bf16)
        gate_out[:, span] = gp
        up_out[:, span] = ug
        gate_parts.append(gp)
        up_parts.append(ug)
    share[...] += sums
    total[...] += dot(jnp.concatenate(gate_parts + up_parts, axis=1), w[:, : 2 * wide], NT)

    @pl.when(step == steps - 1)
    def _():
        pair = share[...] * kept[...]
        mine = soft[...]
        logit = mine * (pair - jnp.sum(mine * pair, axis=1, keepdims=True))
        high = logit.astype(bf16)
        low = (logit - high.astype(f32)).astype(bf16)
        value = total[...] + (dot(high, router[...], NT) + dot(low, router[...], NT))
        for j in range(n):
            outs[j][...] = value[j * m : (j + 1) * m, :].astype(bf16)
        across_rows = (((0,), (0,)), ((), ()))
        router_grad[...] = dot(high, x[...], across_rows) + dot(low, x[...], across_rows)


def expert_back_kernel(n, active, gate, up, ws, *refs):
    xs, cs, refs = refs[:n], refs[n : 2 * n], refs[2 * n :]
    outs, grads = refs[:n], refs[n]
    xt, ct, w, total = refs[n + 1 :]
    step, steps = pl.program_id(0), pl.num_programs(0)
    m = xs[0].shape[0]
    eb = EXPERTS_PER_STEP
    blocks, _, _, rows, fe = ws.shape

    @pl.when(step == 0)
    def _():
        for j in range(n):
            xt[:, j * m : (j + 1) * m] = xs[j][...].T
            ct[:, j * m : (j + 1) * m] = cs[j][...].T
        total[...] = jnp.zeros_like(total)

    for b in range(blocks):
        for i in range(eb):
            w[b * rows : (b + 1) * rows, i * fe : (i + 1) * fe] = ws[b, 0, i]
    total[...] += dot(active[...], w[...], NT)
    for kind, (left, right) in enumerate(((xt, gate), (xt, up), (ct, active))):
        value = dot(left[...], right[...]).astype(bf16)
        for b in range(blocks):
            for i in range(eb):
                grads[b, kind, i] = value[b * rows : (b + 1) * rows, i * fe : (i + 1) * fe]

    @pl.when(step == steps - 1)
    def _():
        for j in range(n):
            outs[j][...] = total[j * m : (j + 1) * m, :].astype(bf16)


def qkv_back_kernel(n, rows, where, dq, dkv, got, cos, sin, wa, wb, *refs):
    xs, refs = refs[:n], refs[n:]
    outs, (grads, gain_grad, w) = refs[:n], refs[n:]
    lay(w, (wa, wb), where, rows)
    m = xs[0].shape[0]
    both = dkv[...].astype(f32)
    if got is not None:
        both = both + got[...].astype(f32)
    grads[:, 0:256] = dq[...]
    grads[:, 256:384] = turn(both[:, 0:128], cos[...], -sin[...]).astype(bf16)
    grads[:, 384:512] = both[:, 128:256].astype(bf16)
    u = dot(grads[...], w[...], NT)
    sums = jnp.zeros(gain_grad.shape, f32)
    x_width = u.shape[1]
    for j in range(n):
        v = xs[j][:, : x_width].astype(f32)
        r = lax.rsqrt(jnp.mean(v * v, axis=-1, keepdims=True) + EPS)
        part = u[j * m : (j + 1) * m, :]
        sums = sums + jnp.sum(part * (v * r), axis=0, keepdims=True)
        outs[j][...] = part.astype(bf16)
    gain_grad[...] = sums


def weight_back_kernel(n, rows, where, x1, grads, router_part, gain_one, gain_two, *refs):
    bs, ms, (keep, send, value, vectors) = refs[:n], refs[n : 2 * n], refs[2 * n :]
    wide = grads.shape[1]
    value[:, :wide] = dot(x1[...].T, grads[...]).astype(bf16)
    branch = jnp.concatenate([r[...] for r in bs], axis=0)
    mixed = jnp.concatenate([r[...] for r in ms], axis=0)
    value[:, wide:] = dot(branch.T, mixed).astype(bf16)
    lines = vectors.shape[1]
    for q in range(vectors.shape[0]):
        columns = slice(q * rows, (q + 1) * rows)
        block = [router_part[:, columns], gain_one[:, columns], gain_two[:, columns]]
        block.append(jnp.zeros((lines - E - 2, rows), f32))
        vectors[q] = jnp.concatenate(block, axis=0).astype(bf16)
    half = keep.shape[0]
    for b in range(2 * half):
        target = keep if b < half else send
        target[b % half, 0:rows, :] = value[pl.ds(pl.multiple_of(where[b] * rows, rows), rows), :]
        target[b % half, rows : rows + lines, 0:rows] = vectors[where[b]]
        target[b % half, rows : rows + lines, rows:] = jnp.zeros((lines, value.shape[1] - rows), bf16)


def input_kernel(n, x, gain, middle_grad, *refs):
    parts, out = refs[:n], refs[n]
    u = parts[0][...].astype(f32)
    for r in parts[1:]:
        u = u + r[...].astype(f32)
    v = x[...].astype(f32)
    r = lax.rsqrt(jnp.mean(v * v, axis=-1, keepdims=True) + EPS)
    normal = v * r
    scaled = u * gain[...]
    grad = r * (scaled - normal * jnp.mean(scaled * normal, axis=-1, keepdims=True))
    out[...] = (middle_grad[...] + grad).astype(bf16)


def output_kernel(n, middle, *refs):
    parts, out = refs[:n], refs[n]
    u = middle[...]
    for r in parts:
        u = u + r[...].astype(f32)
    out[...] = u.astype(bf16)


def across(v, j):
    return lax.ppermute(v, "tensor", [(i, i ^ j) for i in range(lax.axis_size("tensor"))])


def spread(v):
    return [v] + [across(v, j) for j in range(1, lax.axis_size("tensor"))]


def spread_by_two(v):
    if lax.axis_size("tensor") != 4:
        return spread(v)
    near = across(v, 1)
    return [v, near, across(v, 2), across(near, 2)]


def collect(parts):
    return [parts[0]] + [across(parts[j], j) for j in range(1, len(parts))]


def after(v, *others):
    return lax.optimization_barrier((v, *others))[0]


def swap_x(v):
    return lax.ppermute(v, "seq", [(0, 1), (1, 0)])


def swap_core(v):
    return lax.ppermute(v, "dp", [(i, i ^ 1) for i in range(4)])


def swap_y(v):
    return lax.ppermute(v, "dp", [(i, i ^ 2) for i in range(4)])


def swap_xy(v):
    return lax.ppermute(v, ("dp", "seq"), [(i, i ^ 5) for i in range(8)])


def after_all(values, others):
    return lax.optimization_barrier((*values, *others))[: len(values)]


def plane_gather(v, fancy, near=False, first=()):
    if fancy and near:
        near = after(jnp.stack([v, swap_x(v), swap_y(v), swap_xy(v)]), *first)
        return near, swap_core(near)
    if fancy:
        near = jnp.stack([v, swap_x(v)])
        near = jnp.concatenate([near, swap_y(near)])
        return near, swap_core(near)
    every = lax.all_gather(v, ("dp", "seq"), axis=0, tiled=False)
    half = every.shape[0] // 2
    return every[:half], every[half:]


def plane_scatter(keep, send, fancy):
    if not fancy:
        both = jnp.concatenate([keep, send], axis=0)
        return lax.psum_scatter(both, ("dp", "seq"), scatter_dimension=0, tiled=False).astype(f32)
    got = swap_core(send)
    far = swap_y((keep[2:].astype(f32) + got[2:].astype(f32)).astype(bf16))
    mine = keep[:2].astype(f32) + got[:2].astype(f32) + far.astype(f32)
    return mine[0] + swap_x(mine[1].astype(bf16)).astype(f32)


def per_device(
    hidden_in,
    cotangent,
    piece_starts,
    expert_ids,
    claim_order,
    first_gain,
    second_gain,
    router,
    w_query,
    key_projection,
    value_projection,
    w_out,
    w_gate,
    w_up,
    w_down,
):
    n_dp, n_seq, n = lax.axis_size("dp"), lax.axis_size("seq"), lax.axis_size("tensor")
    fancy = n_dp == 4 and n_seq == 2
    n_p = n_dp * n_seq
    me = lax.axis_index("tensor")
    seq_at = lax.axis_index("seq")
    place = lax.axis_index("dp") * n_seq + seq_at
    m, d = hidden_in.shape[1:]
    count = m * n
    rows = d // n_p
    if hidden_in.shape[0] != 1 or expert_ids.shape[1] != count:
        raise ValueError("shapes")
    wide = w_query.shape[1]
    order = (0, 1, 4, 5, 2, 3, 6, 7) if fancy else tuple(range(n_p))
    where = (place ^ jnp.array(order, jnp.int32)) if fancy else jnp.arange(n_p, dtype=jnp.int32)

    own, cot = hidden_in[0], cotangent[0]

    shard = first_gain.shape[0]
    small = jnp.concatenate([router.reshape(-1), first_gain, second_gain])
    size = small.shape[0]
    smalls = spread(small.reshape(1, size))
    which = me ^ jnp.arange(n)
    pick_rows = (which[:, None] == jnp.arange(n)[None, :]).astype(f32)
    stacked = jnp.concatenate(smalls, axis=0).astype(f32)
    natural = jnp.sum(pick_rows[:, :, None] * stacked[None], axis=1).astype(bf16)
    qkv_w = jnp.concatenate([w_query, key_projection, value_projection], axis=1)
    cols = qkv_w.shape[1]
    natural = jnp.pad(natural.reshape(-1), (0, 16 * cols - n * size)).reshape(16, cols)
    xs = spread(own)
    wa, wb = plane_gather(jnp.concatenate([qkv_w, natural], axis=0), fancy, near=True)
    tail = jnp.concatenate([wa[:, rows:], wb[:, rows:]], axis=0).reshape(n_p, -1)[:, : n * size]
    ordered = (where[None, :] == jnp.arange(n_p, dtype=jnp.int32)[:, None]).astype(f32)
    tail = jnp.sum(ordered[:, :, None] * tail.astype(f32)[None], axis=1).reshape(n_p, n, size)
    gain_one = tail[:, :, size - 2 * shard : size - shard].reshape(1, d)
    gain_two = tail[:, :, size - shard :].reshape(1, d)
    router_all = tail[:, :, : size - 2 * shard].reshape(d, E).astype(bf16)

    blocks = me ^ jnp.arange(n, dtype=jnp.int32)
    positions = (seq_at * count + blocks[:, None] * m + jnp.arange(m, dtype=jnp.int32)[None, :]).reshape(count)
    starts = piece_starts[0]
    inside = (positions[:, None] >= starts[None, :]) & (positions[:, None] < starts[None, :] + PIECE)
    limit = jnp.maximum(
        positions, jnp.max(jnp.where(inside, starts[None, :] + PIECE - 1, -1), axis=1)
    ).reshape(1, count)
    half = HEAD // 2
    freqs = jnp.exp(jnp.arange(half).astype(f32) * (-2.0 * math.log(10000.0) / HEAD))
    angles = positions.astype(f32)[:, None] * freqs[None, :]
    cosine, sine = jnp.cos(angles), jnp.sin(angles)
    cos = jnp.concatenate([cosine] * 4, axis=1)
    sin = jnp.concatenate([-sine, sine] * 2, axis=1)

    ids, claim = expert_ids[0], claim_order[0]
    experts = jnp.arange(E, dtype=jnp.int32)
    chosen = jnp.max((ids[:, :, None] == experts[None, None, :]).astype(f32), axis=1)
    before = (claim[None, :] < claim[:, None]).astype(bf16)
    taken = dot(before, chosen.astype(bf16))
    kept = jnp.where(taken < CAP, chosen, 0.0)
    tables = jnp.concatenate([chosen, kept], axis=1).reshape(n, m, 2 * E)
    tables = jnp.sum(
        (blocks[:, None] == jnp.arange(n)[None, :]).astype(f32)[:, :, None, None] * tables[None], axis=1
    ).reshape(count, 2 * E)
    chosen, kept = tables[:, :E], tables[:, E:]

    x1, q, kv = whole_call(
        functools.partial(qkv_kernel, n, rows),
        (sds((count, d), bf16), sds((count, wide), bf16), sds((count, 256), bf16)),
        (where, *xs, gain_one, cos, sin, wa, wb),
        scratch=(pltpu.VMEM((d, cols), bf16),),
        flops=2 * count * d * cols,
        prefetch=1,
    )
    key_pos = positions.reshape(count, 1)
    if fancy:
        kvs = [kv, swap_x(kv)]
        poss = [key_pos, key_pos + (1 - 2 * seq_at) * count]
    else:
        kvs = [lax.all_gather(kv, "seq", axis=0, tiled=True)]
        poss = [lax.all_gather(key_pos.astype(f32), "seq", axis=0, tiled=True).astype(jnp.int32)]
    span = sum(v.shape[0] for v in kvs)
    heads = wide // HEAD
    got = whole_call(
        functools.partial(attend_kernel, len(kvs), n),
        tuple([sds((m, wide), bf16)] * n) + (sds((heads, HEAD, count), f32), sds((heads, 1, count), f32)),
        (q, limit, *kvs, *poss),
        scratch=(
            pltpu.VMEM((heads, count, HEAD), bf16),
            pltpu.VMEM((2, span, HEAD), bf16),
            pltpu.VMEM((2, HEAD, span), bf16),
            pltpu.VMEM((span, 1), jnp.int32),
        ),
        cost=10 ** 10,
    )
    mixed, (mixed_t, lse) = got[:n], got[n:]

    out_w = jnp.concatenate(spread(after(w_out, wa)), axis=1)
    cots = [cot] + spread(after(cot, kv))[1:]
    oa, ob = plane_gather(after(out_w, kvs[-1]), fancy, near=True, first=())
    mine = collect([mixed[0], *after_all(mixed[1:], cots[1:])])
    oa, ob = (oa, swap_core(after(oa, *mine))) if fancy else (oa, ob)
    middle, second = whole_call(
        functools.partial(middle_kernel, n),
        (sds((m, d), f32), sds((m, d), bf16)),
        (where, own, gain_two, oa, ob, *mine),
        scratch=(pltpu.VMEM((d, n * wide), bf16),),
        flops=2 * m * d * d,
        prefetch=1,
    )

    seconds = spread(second)

    packed = jnp.stack([w_gate, w_up, w_down])
    ws = lax.all_gather(packed, ("dp", "seq"), axis=0, tiled=False)
    eb, fe = EXPERTS_PER_STEP, w_gate.shape[2]
    steps = E // eb
    block = pl.BlockSpec((count, eb * fe), lambda s: (0, s))
    wide_out = sds((count, E * fe), bf16)
    got = pl.pallas_call(
        functools.partial(expert_kernel, n),
        out_shape=tuple([sds((m, d), bf16)] * n) + (wide_out, wide_out, wide_out, sds((E, d), f32)),
        grid=(steps,),
        in_specs=[full((count, E)), full((count, E)), full((d, E))]
        + [pl.BlockSpec((n_p, 3, eb, rows, fe), lambda s: (0, 0, s, 0, 0))]
        + [full((m, d))] * (2 * n),
        out_specs=[full((m, d))] * n + [block] * 3 + [full((E, d))],
        scratch_shapes=[
            pltpu.VMEM((count, d), bf16),
            pltpu.VMEM((count, d), bf16),
            pltpu.VMEM((d, 3 * eb * fe), bf16),
            pltpu.VMEM((count, d), f32),
            pltpu.VMEM((count, E), f32),
            pltpu.VMEM((count, E), f32),
        ],
        cost_estimate=pl.CostEstimate(flops=0, bytes_accessed=0, transcendentals=0),
    )(chosen, kept, router_all, ws, *seconds, *cots)
    second_parts, (active, gate_g, up_g, router_part) = got[:n], got[n:]
    half_p = n_p // 2
    got = pl.pallas_call(
        functools.partial(expert_back_kernel, n),
        out_shape=tuple([sds((m, d), bf16)] * n) + (sds((n_p, 3, E, rows, fe), bf16),),
        grid=(steps,),
        in_specs=[block] * 3
        + [pl.BlockSpec((n_p, 1, eb, rows, fe), lambda s: (0, 2, s, 0, 0))]
        + [full((m, d))] * (2 * n),
        out_specs=[full((m, d))] * n + [pl.BlockSpec((n_p, 3, eb, rows, fe), lambda s: (0, 0, s, 0, 0))],
        scratch_shapes=[
            pltpu.VMEM((d, count), bf16),
            pltpu.VMEM((d, count), bf16),
            pltpu.VMEM((d, eb * fe), bf16),
            pltpu.VMEM((count, d), f32),
        ],
        cost_estimate=pl.CostEstimate(flops=0, bytes_accessed=0, transcendentals=0),
    )(active, gate_g, up_g, ws, *seconds, *cots)
    out_parts, expert_parts = got[:n], got[n]

    sums = collect(second_parts)
    expert_parts = after(expert_parts, *sums)
    expert_grads = lax.psum_scatter(expert_parts, ("dp", "seq"), scatter_dimension=0, tiled=False)
    got = whole_call(
        functools.partial(middle_back_kernel, n),
        (sds((m, d), f32), sds((m, d), bf16), sds((1, d), f32)) + tuple([sds((m, wide), bf16)] * n),
        (where, middle, gain_two, cot, oa, ob, *sums),
        scratch=(pltpu.VMEM((d, n * wide), bf16),),
        flops=2 * m * d * d,
        prefetch=1,
    )
    (middle_grad, branch, gain_two_part), pieces = got[:3], got[3:]
    mixed_grads = collect(pieces)
    branches = [branch] + spread_by_two(after(branch, *mixed_grads))[1:]

    def attend_back(kv_one, pos_one, dtype, extra):
        one = kv_one.shape[0]
        last = bool(extra)
        return whole_call(
            functools.partial(attend_back_kernel, n, last),
            (
                sds((one, 256), dtype),
                sds((count, wide), bf16) if last else sds((heads, HEAD, count), f32),
            ),
            (q, limit, kv_one, pos_one, lse, mixed_t, *mixed_grads, *extra),
            scratch=(
                pltpu.VMEM((heads, count, HEAD), bf16),
                pltpu.VMEM((heads, count, HEAD), bf16),
                pltpu.VMEM((2, one, HEAD), bf16),
                pltpu.VMEM((2, one, HEAD), bf16),
                pltpu.VMEM((2, HEAD, one), bf16),
                pltpu.VMEM((heads, 1, count), f32),
                pltpu.VMEM((2, one, HEAD), f32),
                pltpu.VMEM((2, one, HEAD), f32),
                pltpu.VMEM((heads, HEAD, count), f32),
            ),
            cost=10 ** 10,
        )

    if fancy:
        far, dq_far = attend_back(kvs[1], poss[1], bf16, ())
        got_kv = (swap_x(far),)
        dkv, dq = attend_back(kvs[0], poss[0], f32, (dq_far, cos, sin))
    else:
        zero = jnp.zeros((heads, HEAD, count), f32)
        dkv, dq = attend_back(kvs[0], poss[0], bf16, (zero, cos, sin))
        dkv = lax.psum_scatter(dkv, "seq", scatter_dimension=0, tiled=True)
        got_kv = (jnp.zeros((count, 256), bf16),)

    out_sums = [out_parts[0]] + collect([out_parts[0], *after_all(out_parts[1:], mixed_grads)])[1:]
    dq_ready = after(dq, *branches[1:3])
    got = whole_call(
        functools.partial(qkv_back_kernel, n, rows),
        tuple([sds((m, d), bf16)] * n) + (sds((count, cols), bf16), sds((1, d), f32)),
        (where, dq_ready, dkv, *got_kv, cos, sin, wa, wb, *xs),
        scratch=(pltpu.VMEM((d, cols), bf16),),
        flops=2 * count * d * cols,
        prefetch=1,
    )
    first_parts, (grads, gain_one_part) = got[:n], got[n:]
    grads = after(grads, *out_sums[:3])
    sums = collect(first_parts)
    weight_shape = sds((half_p, rows + LINES, cols + wide), bf16)
    weight_keep, weight_send = whole_call(
        functools.partial(weight_back_kernel, n, rows),
        (weight_shape, weight_shape),
        (where, x1, grads, router_part, gain_one_part, gain_two_part, *branches, *mixed),
        scratch=(pltpu.VMEM((d, cols + wide), bf16), pltpu.VMEM((n_p, LINES, rows), bf16)),
        flops=2 * count * d * (cols + wide),
        prefetch=1,
    )

    (input_grad,) = whole_call(
        functools.partial(input_kernel, n), (sds((m, d), bf16),), (own, gain_one, middle_grad, *sums)
    )
    (output,) = whole_call(
        functools.partial(output_kernel, n), (sds((m, d), bf16),), (middle, *out_sums)
    )
    weights = plane_scatter(weight_keep, weight_send, fancy)
    total = weights[rows : rows + E + 2, :rows]
    for bit in range(n.bit_length() - 1):
        total = total + across(total, 1 << bit)
    total = lax.dynamic_slice_in_dim(total, me * shard, shard, axis=1)
    weights = weights[:rows]
    kv_wide = key_projection.shape[1]
    return (
        output[None],
        input_grad[None],
        weights[:, :wide],
        weights[:, wide : wide + kv_wide],
        weights[:, wide + kv_wide : cols],
        weights[:, cols:],
        expert_grads[0].astype(f32),
        expert_grads[1].astype(f32),
        expert_grads[2].astype(f32),
        total[E],
        total[E + 1],
        total[:E].T,
    )


def solution(mesh):
    placed = (
        P("dp", ("seq", "tensor"), None),
        P("dp", ("seq", "tensor"), None),
        P("dp", None),
        P("dp", "seq", None),
        P("dp", "seq"),
        P(("dp", "seq", "tensor")),
        P(("dp", "seq", "tensor")),
        P(("dp", "seq", "tensor"), None),
        P(("dp", "seq"), "tensor"),
        P(("dp", "seq"), "tensor"),
        P(("dp", "seq"), "tensor"),
        P(("dp", "seq"), "tensor"),
        P(None, ("dp", "seq"), "tensor"),
        P(None, ("dp", "seq"), "tensor"),
        P(None, ("dp", "seq"), "tensor"),
    )
    return jax.shard_map(
        per_device,
        mesh=mesh,
        in_specs=placed,
        out_specs=(
            P("dp", ("seq", "tensor"), None),
            P("dp", ("seq", "tensor"), None),
            P(("dp", "seq"), "tensor"),
            P(("dp", "seq"), "tensor"),
            P(("dp", "seq"), "tensor"),
            P(("dp", "seq"), "tensor"),
            P(None, ("dp", "seq"), "tensor"),
            P(None, ("dp", "seq"), "tensor"),
            P(None, ("dp", "seq"), "tensor"),
            P(("dp", "seq", "tensor")),
            P(("dp", "seq", "tensor")),
            P(("dp", "seq", "tensor"), None),
        ),
        check_vma=False,
    )
```

```python
import functools
import math

import jax
import jax.numpy as jnp
from jax import lax
from jax.experimental import pallas as pl
from jax.experimental.pallas import tpu as pltpu
from jax.sharding import PartitionSpec as P

HEAD = 64
E = 16
PIECE = 256
CAP = 320
EPS = 1e-06
FILL = -1e30
EXPERTS_PER_STEP = 4
ROW_TILE = 256
LINES = 32
f32 = jnp.float32
bf16 = jnp.bfloat16

NT = (((1,), (1,)), ((), ()))
NN = (((1,), (0,)), ((), ()))


def dot(a, b, dims=NN):
    return lax.dot_general(a, b, dims, preferred_element_type=f32)


def full(shape):
    rank = len(shape)
    return pl.BlockSpec(shape, lambda *_: (0,) * rank)


def whole_call(body, outs, args, scratch=(), flops=0, prefetch=0, cost=0):
    moved = sum(math.prod(a.shape) * a.dtype.itemsize for a in (*args, *outs))
    return pl.pallas_call(
        body,
        out_shape=outs,
        grid_spec=pltpu.PrefetchScalarGridSpec(
            num_scalar_prefetch=prefetch,
            grid=(1,),
            in_specs=[full(a.shape) for a in args[prefetch:]],
            out_specs=[full(o.shape) for o in outs],
            scratch_shapes=list(scratch),
        ),
        cost_estimate=pl.CostEstimate(flops=int(cost), bytes_accessed=0, transcendentals=0),
    )(*args)


def sds(shape, dtype):
    return jax.ShapeDtypeStruct(shape, dtype)


def turn(v, cos, sin):
    lane = lax.broadcasted_iota(jnp.int32, v.shape, 1) % HEAD
    other = jnp.where(lane < HEAD // 2, pltpu.roll(v, 128 - HEAD // 2, 1), pltpu.roll(v, HEAD // 2, 1))
    return v * cos + other * sin


def lay(out, stacks, where, rows):
    first = 0
    for r in stacks:
        for i in range(r.shape[0]):
            out[pl.ds(pl.multiple_of(where[first + i] * rows, rows), rows), :] = r[i, 0:rows, :]
        first += r.shape[0]


def qkv_kernel(n, rows, where, *refs):
    xs, (gain, cos, sin, wa, wb), (x1, q, kv, w) = refs[:n], refs[n : n + 5], refs[n + 5 :]
    lay(w, (wa, wb), where, rows)
    m = xs[0].shape[0]
    x_width = x1.shape[1]
    for j in range(n):
        v = xs[j][:, : x_width].astype(f32)
        r = lax.rsqrt(jnp.mean(v * v, axis=-1, keepdims=True) + EPS)
        x1[j * m : (j + 1) * m, :] = (v * r * gain[...]).astype(bf16)
    out = dot(x1[...], w[...])
    c, s = cos[...], sin[...]
    q[:, 0:128] = turn(out[:, 0:128], c, s).astype(bf16)
    q[:, 128:256] = turn(out[:, 128:256], c, s).astype(bf16)
    kv[:, 0:128] = turn(out[:, 256:384], c, s).astype(bf16)
    kv[:, 128:256] = out[:, 384:512].astype(bf16)


SCORE = HEAD ** (-0.5) * math.log2(math.e)


def attend_kernel(parts, n, q, lim, *refs):
    kvs, poss = refs[:parts], refs[parts : 2 * parts]
    mixed, (ot, lse) = refs[2 * parts : 2 * parts + n], refs[2 * parts + n : 2 * parts + n + 2]
    qs, ks, vt, kp = refs[2 * parts + n + 2 :]
    count = q.shape[0]
    heads = q.shape[1] // HEAD
    first = 0
    for kvr, pr in zip(kvs, poss):
        span = slice(first, first + kvr.shape[0])
        first += kvr.shape[0]
        v = kvr[:, 128:256].astype(f32).T.astype(bf16)
        for g in range(2):
            ks[g, span, :] = kvr[:, g * HEAD : (g + 1) * HEAD]
            vt[g, :, span] = v[g * HEAD : (g + 1) * HEAD, :]
        kp[span, :] = pr[...]
    for h in range(heads):
        qs[h] = q[:, h * HEAD : (h + 1) * HEAD]
    tiles = count // ROW_TILE

    def body(i, carry):
        h, t = i // tiles, i % tiles
        at = pl.ds(pl.multiple_of(t * ROW_TILE, ROW_TILE), ROW_TILE)
        g = h // 2
        s = dot(ks[g], qs[h, at, :], NT)
        s = jnp.where(kp[...] <= lim[:, at], s, FILL)
        top = jnp.max(s, axis=0, keepdims=True)
        p = jnp.exp2((s - top) * SCORE)
        total = jnp.sum(p, axis=0, keepdims=True)
        o = dot(vt[g], p.astype(bf16))
        ot[h, :, at] = o / total
        lse[h, :, at] = top * SCORE + jnp.log2(total)
        return carry

    lax.fori_loop(0, heads * tiles, body, 0)
    out = ot[...].reshape(heads * HEAD, count).T.astype(bf16)
    m = count // n
    for j in range(n):
        mixed[j][...] = out[j * m : (j + 1) * m, :]


def attend_back_kernel(n, last, q, lim, kv, kpos, lse, ot, *refs):
    dos_in, refs = refs[:n], refs[n:]
    if last:
        (dq_in, cos, sin), refs = refs[:3], refs[3:]
    dkv, dq_out = refs[:2]
    qs, dos, ks, vs, kt, delta, dk, dv, dqt = refs[2:]
    count = q.shape[0]
    heads = q.shape[1] // HEAD
    m = count // n
    for j in range(n):
        block = dos_in[j][...]
        turned = block.astype(f32).T
        for h in range(heads):
            span = slice(h * HEAD, (h + 1) * HEAD)
            dos[h, j * m : (j + 1) * m, :] = block[:, span]
            delta[h, :, j * m : (j + 1) * m] = jnp.sum(
                turned[span, :] * ot[h, :, j * m : (j + 1) * m], axis=0, keepdims=True
            )
    k_turned = kv[:, 0:128].astype(f32).T.astype(bf16)
    for g in range(2):
        ks[g] = kv[:, g * HEAD : (g + 1) * HEAD]
        vs[g] = kv[:, 128 + g * HEAD : 128 + (g + 1) * HEAD]
        kt[g] = k_turned[g * HEAD : (g + 1) * HEAD, :]
    for h in range(heads):
        qs[h] = q[:, h * HEAD : (h + 1) * HEAD]
    dk[...] = jnp.zeros_like(dk)
    dv[...] = jnp.zeros_like(dv)
    tiles = count // ROW_TILE

    def body(i, carry):
        h, t = i // tiles, i % tiles
        at = pl.ds(pl.multiple_of(t * ROW_TILE, ROW_TILE), ROW_TILE)
        g = h // 2
        q_h, do_h = qs[h, at, :], dos[h, at, :]
        s = dot(ks[g], q_h, NT)
        p = jnp.where(kpos[...] <= lim[:, at], jnp.exp2(s * SCORE - lse[h, :, at]), 0.0)
        dp = dot(vs[g], do_h, NT)
        ds = (p * (dp - delta[h, :, at])).astype(bf16)
        dv[g] += dot(p.astype(bf16), do_h)
        dk[g] += dot(ds, q_h)
        dqt[h, :, at] = dot(kt[g], ds)
        return carry

    lax.fori_loop(0, heads * tiles, body, 0)
    scale = HEAD ** (-0.5)
    dkv[...] = jnp.concatenate([dk[0] * scale, dk[1] * scale, dv[0], dv[1]], axis=1).astype(dkv.dtype)
    if last:
        whole = ((dqt[...] + dq_in[...]).reshape(heads * HEAD, count) * scale).T
        for half in range(2):
            lanes = slice(half * 128, (half + 1) * 128)
            dq_out[:, lanes] = turn(whole[:, lanes], cos[...], -sin[...]).astype(bf16)
    else:
        dq_out[...] = dqt[...]


def middle_kernel(n, where, x, gain, wa, wb, *refs):
    mixed, (middle, second, w) = refs[:n], refs[n:]
    lay(w, (wa, wb), where, wa.shape[1])
    both = jnp.concatenate([r[...] for r in mixed], axis=1)
    value = x[...].astype(f32) + dot(both, w[...], NT)
    middle[...] = value
    r = lax.rsqrt(jnp.mean(value * value, axis=-1, keepdims=True) + EPS)
    second[...] = (value * r * gain[...]).astype(bf16)


def middle_back_kernel(n, where, middle, gain, cot, wa, wb, *refs):
    parts, refs = refs[:n], refs[n:]
    middle_grad, branch, gain_grad = refs[:3]
    pieces, w = refs[3:-1], refs[-1]
    lay(w, (wa, wb), where, wa.shape[1])
    u = parts[0][...].astype(f32)
    for r in parts[1:]:
        u = u + r[...].astype(f32)
    value = middle[...]
    r = lax.rsqrt(jnp.mean(value * value, axis=-1, keepdims=True) + EPS)
    normal = value * r
    gain_grad[...] = jnp.sum(u * normal, axis=0, keepdims=True)
    scaled = u * gain[...]
    grad = cot[...].astype(f32) + r * (scaled - normal * jnp.mean(scaled * normal, axis=-1, keepdims=True))
    middle_grad[...] = grad
    low = grad.astype(bf16)
    branch[...] = low
    out = dot(low, w[...]).astype(bf16)
    wide = out.shape[1] // n
    for j in range(n):
        pieces[j][...] = out[:, j * wide : (j + 1) * wide]


def pick(table, index):
    lane = lax.broadcasted_iota(jnp.int32, table.shape, 1)
    return jnp.sum(jnp.where(lane == index, table, 0.0), axis=1, keepdims=True)


def expert_kernel(n, chosen, kept, router, ws, *refs):
    xs, cs, refs = refs[:n], refs[n : 2 * n], refs[2 * n :]
    outs, (active_out, gate_out, up_out, router_grad) = refs[:n], refs[n : n + 4]
    x, c, w, total, soft, share = refs[n + 4 :]
    step, steps = pl.program_id(0), pl.num_programs(0)
    m = xs[0].shape[0]
    eb = EXPERTS_PER_STEP
    blocks, _, _, rows, fe = ws.shape
    wide = eb * fe

    @pl.when(step == 0)
    def _():
        for j in range(n):
            x[j * m : (j + 1) * m, :] = xs[j][...]
            c[j * m : (j + 1) * m, :] = cs[j][...]
        logits = jnp.where(chosen[...] > 0.0, dot(x[...], router[...]), FILL)
        top = jnp.max(logits, axis=1, keepdims=True)
        e = jnp.where(chosen[...] > 0.0, jnp.exp(logits - top), 0.0)
        soft[...] = e / jnp.sum(e, axis=1, keepdims=True)
        total[...] = jnp.zeros_like(total)
        share[...] = jnp.zeros_like(share)

    for b in range(blocks):
        for kind in range(3):
            for i in range(eb):
                at = kind * wide + i * fe
                w[b * rows : (b + 1) * rows, at : at + fe] = ws[b, kind, i]
    gu = dot(x[...], w[:, : 2 * wide])
    down = dot(c[...], w[:, 2 * wide :])
    table = soft[...] * kept[...]
    lane = lax.broadcasted_iota(jnp.int32, share.shape, 1)
    sums = jnp.zeros(share.shape, f32)
    gate_parts, up_parts = [], []
    for i in range(eb):
        span = slice(i * fe, (i + 1) * fe)
        gate, up, d = gu[:, span], gu[:, wide + i * fe : wide + (i + 1) * fe], down[:, span]
        index = step * eb + i
        weight = pick(table, index)
        sig = jax.nn.sigmoid(gate)
        silu = gate * sig
        active = silu * up
        active_out[:, span] = (active * weight).astype(bf16)
        sums = sums + jnp.where(lane == index, jnp.sum(active * d, axis=1, keepdims=True), 0.0)
        ag = d * weight
        gp = (ag * up * (sig * (1.0 + gate * (1.0 - sig)))).astype(bf16)
        ug = (ag * silu).astype(bf16)
        gate_out[:, span] = gp
        up_out[:, span] = ug
        gate_parts.append(gp)
        up_parts.append(ug)
    share[...] += sums
    total[...] += dot(jnp.concatenate(gate_parts + up_parts, axis=1), w[:, : 2 * wide], NT)

    @pl.when(step == steps - 1)
    def _():
        pair = share[...] * kept[...]
        mine = soft[...]
        logit = mine * (pair - jnp.sum(mine * pair, axis=1, keepdims=True))
        high = logit.astype(bf16)
        low = (logit - high.astype(f32)).astype(bf16)
        value = total[...] + (dot(high, router[...], NT) + dot(low, router[...], NT))
        for j in range(n):
            outs[j][...] = value[j * m : (j + 1) * m, :].astype(bf16)
        across_rows = (((0,), (0,)), ((), ()))
        router_grad[...] = dot(high, x[...], across_rows) + dot(low, x[...], across_rows)


def expert_back_kernel(n, active, gate, up, ws, *refs):
    xs, cs, refs = refs[:n], refs[n : 2 * n], refs[2 * n :]
    outs, grads = refs[:n], refs[n]
    xt, ct, w, total = refs[n + 1 :]
    step, steps = pl.program_id(0), pl.num_programs(0)
    m = xs[0].shape[0]
    eb = EXPERTS_PER_STEP
    blocks, _, _, rows, fe = ws.shape

    @pl.when(step == 0)
    def _():
        for j in range(n):
            xt[:, j * m : (j + 1) * m] = xs[j][...].T
            ct[:, j * m : (j + 1) * m] = cs[j][...].T
        total[...] = jnp.zeros_like(total)

    for b in range(blocks):
        for i in range(eb):
            w[b * rows : (b + 1) * rows, i * fe : (i + 1) * fe] = ws[b, 0, i]
    total[...] += dot(active[...], w[...], NT)
    for kind, (left, right) in enumerate(((xt, gate), (xt, up), (ct, active))):
        value = dot(left[...], right[...]).astype(bf16)
        for b in range(blocks):
            for i in range(eb):
                grads[b, kind, i] = value[b * rows : (b + 1) * rows, i * fe : (i + 1) * fe]

    @pl.when(step == steps - 1)
    def _():
        for j in range(n):
            outs[j][...] = total[j * m : (j + 1) * m, :].astype(bf16)


def qkv_back_kernel(n, rows, where, dq, dkv, got, cos, sin, wa, wb, *refs):
    xs, refs = refs[:n], refs[n:]
    outs, (grads, gain_grad, w) = refs[:n], refs[n:]
    lay(w, (wa, wb), where, rows)
    m = xs[0].shape[0]
    both = dkv[...].astype(f32)
    if got is not None:
        both = both + got[...].astype(f32)
    grads[:, 0:256] = dq[...]
    grads[:, 256:384] = turn(both[:, 0:128], cos[...], -sin[...]).astype(bf16)
    grads[:, 384:512] = both[:, 128:256].astype(bf16)
    u = dot(grads[...], w[...], NT)
    sums = jnp.zeros(gain_grad.shape, f32)
    x_width = u.shape[1]
    for j in range(n):
        v = xs[j][:, : x_width].astype(f32)
        r = lax.rsqrt(jnp.mean(v * v, axis=-1, keepdims=True) + EPS)
        part = u[j * m : (j + 1) * m, :]
        sums = sums + jnp.sum(part * (v * r), axis=0, keepdims=True)
        outs[j][...] = part.astype(bf16)
    gain_grad[...] = sums


def weight_back_kernel(n, rows, where, x1, grads, router_part, gain_one, gain_two, *refs):
    bs, ms, (keep, send, value, vectors) = refs[:n], refs[n : 2 * n], refs[2 * n :]
    wide = grads.shape[1]
    value[:, :wide] = dot(x1[...].T, grads[...]).astype(bf16)
    branch = jnp.concatenate([r[...] for r in bs], axis=0)
    mixed = jnp.concatenate([r[...] for r in ms], axis=0)
    value[:, wide:] = dot(branch.T, mixed).astype(bf16)
    lines = vectors.shape[1]
    for q in range(vectors.shape[0]):
        columns = slice(q * rows, (q + 1) * rows)
        block = [router_part[:, columns], gain_one[:, columns], gain_two[:, columns]]
        block.append(jnp.zeros((lines - E - 2, rows), f32))
        vectors[q] = jnp.concatenate(block, axis=0).astype(bf16)
    half = keep.shape[0]
    for b in range(2 * half):
        target = keep if b < half else send
        target[b % half, 0:rows, :] = value[pl.ds(pl.multiple_of(where[b] * rows, rows), rows), :]
        target[b % half, rows : rows + lines, 0:rows] = vectors[where[b]]
        target[b % half, rows : rows + lines, rows:] = jnp.zeros((lines, value.shape[1] - rows), bf16)


def input_kernel(n, x, gain, middle_grad, *refs):
    parts, out = refs[:n], refs[n]
    u = parts[0][...].astype(f32)
    for r in parts[1:]:
        u = u + r[...].astype(f32)
    v = x[...].astype(f32)
    r = lax.rsqrt(jnp.mean(v * v, axis=-1, keepdims=True) + EPS)
    normal = v * r
    scaled = u * gain[...]
    grad = r * (scaled - normal * jnp.mean(scaled * normal, axis=-1, keepdims=True))
    out[...] = (middle_grad[...] + grad).astype(bf16)


def output_kernel(n, middle, *refs):
    parts, out = refs[:n], refs[n]
    u = middle[...]
    for r in parts:
        u = u + r[...].astype(f32)
    out[...] = u.astype(bf16)


def across(v, j):
    return lax.ppermute(v, "tensor", [(i, i ^ j) for i in range(lax.axis_size("tensor"))])


def spread(v):
    return [v] + [across(v, j) for j in range(1, lax.axis_size("tensor"))]


def spread_by_two(v):
    if lax.axis_size("tensor") != 4:
        return spread(v)
    near = across(v, 1)
    return [v, near, across(v, 2), across(near, 2)]


def collect(parts):
    return [parts[0]] + [across(parts[j], j) for j in range(1, len(parts))]


def after(v, *others):
    return lax.optimization_barrier((v, *others))[0]


def swap_x(v):
    return lax.ppermute(v, "seq", [(0, 1), (1, 0)])


def swap_core(v):
    return lax.ppermute(v, "dp", [(i, i ^ 1) for i in range(4)])


def swap_y(v):
    return lax.ppermute(v, "dp", [(i, i ^ 2) for i in range(4)])


def swap_xy(v):
    return lax.ppermute(v, ("dp", "seq"), [(i, i ^ 5) for i in range(8)])


def after_all(values, others):
    return lax.optimization_barrier((*values, *others))[: len(values)]


def plane_gather(v, fancy, near=False, first=()):
    if fancy and near:
        near = after(jnp.stack([v, swap_x(v), swap_y(v), swap_xy(v)]), *first)
        return near, swap_core(near)
    if fancy:
        near = jnp.stack([v, swap_x(v)])
        near = jnp.concatenate([near, swap_y(near)])
        return near, swap_core(near)
    every = lax.all_gather(v, ("dp", "seq"), axis=0, tiled=False)
    half = every.shape[0] // 2
    return every[:half], every[half:]


def plane_scatter(keep, send, fancy):
    if not fancy:
        both = jnp.concatenate([keep, send], axis=0)
        return lax.psum_scatter(both, ("dp", "seq"), scatter_dimension=0, tiled=False).astype(f32)
    got = swap_core(send)
    low = [(keep[i].astype(f32) + got[i].astype(f32)).astype(bf16) for i in (1, 2, 3)]
    far = swap_x(low[0]).astype(f32) + swap_y(low[1]).astype(f32) + swap_xy(low[2]).astype(f32)
    return keep[0].astype(f32) + got[0].astype(f32) + far


def per_device(
    hidden_in,
    cotangent,
    piece_starts,
    expert_ids,
    claim_order,
    first_gain,
    second_gain,
    router,
    w_query,
    key_projection,
    value_projection,
    w_out,
    w_gate,
    w_up,
    w_down,
):
    n_dp, n_seq, n = lax.axis_size("dp"), lax.axis_size("seq"), lax.axis_size("tensor")
    fancy = n_dp == 4 and n_seq == 2
    n_p = n_dp * n_seq
    me = lax.axis_index("tensor")
    seq_at = lax.axis_index("seq")
    place = lax.axis_index("dp") * n_seq + seq_at
    m, d = hidden_in.shape[1:]
    count = m * n
    rows = d // n_p
    if hidden_in.shape[0] != 1 or expert_ids.shape[1] != count:
        raise ValueError("shapes")
    wide = w_query.shape[1]
    order = (0, 1, 4, 5, 2, 3, 6, 7) if fancy else tuple(range(n_p))
    where = (place ^ jnp.array(order, jnp.int32)) if fancy else jnp.arange(n_p, dtype=jnp.int32)

    own, cot = hidden_in[0], cotangent[0]

    shard = first_gain.shape[0]
    small = jnp.concatenate([router.reshape(-1), first_gain, second_gain])
    size = small.shape[0]
    smalls = spread(small.reshape(1, size))
    which = me ^ jnp.arange(n)
    pick_rows = (which[:, None] == jnp.arange(n)[None, :]).astype(f32)
    stacked = jnp.concatenate(smalls, axis=0).astype(f32)
    natural = jnp.sum(pick_rows[:, :, None] * stacked[None], axis=1).astype(bf16)
    qkv_w = jnp.concatenate([w_query, key_projection, value_projection], axis=1)
    cols = qkv_w.shape[1]
    natural = jnp.pad(natural.reshape(-1), (0, 16 * cols - n * size)).reshape(16, cols)
    xs = spread(own)
    wa, wb = plane_gather(jnp.concatenate([qkv_w, natural], axis=0), fancy, near=True)
    tail = jnp.concatenate([wa[:, rows:], wb[:, rows:]], axis=0).reshape(n_p, -1)[:, : n * size]
    ordered = (where[None, :] == jnp.arange(n_p, dtype=jnp.int32)[:, None]).astype(f32)
    tail = jnp.sum(ordered[:, :, None] * tail.astype(f32)[None], axis=1).reshape(n_p, n, size)
    gain_one = tail[:, :, size - 2 * shard : size - shard].reshape(1, d)
    gain_two = tail[:, :, size - shard :].reshape(1, d)
    router_all = tail[:, :, : size - 2 * shard].reshape(d, E).astype(bf16)

    blocks = me ^ jnp.arange(n, dtype=jnp.int32)
    positions = (seq_at * count + blocks[:, None] * m + jnp.arange(m, dtype=jnp.int32)[None, :]).reshape(count)
    starts = piece_starts[0]
    inside = (positions[:, None] >= starts[None, :]) & (positions[:, None] < starts[None, :] + PIECE)
    limit = jnp.maximum(
        positions, jnp.max(jnp.where(inside, starts[None, :] + PIECE - 1, -1), axis=1)
    ).reshape(1, count)
    half = HEAD // 2
    freqs = jnp.exp(jnp.arange(half).astype(f32) * (-2.0 * math.log(10000.0) / HEAD))
    angles = positions.astype(f32)[:, None] * freqs[None, :]
    cosine, sine = jnp.cos(angles), jnp.sin(angles)
    cos = jnp.concatenate([cosine] * 4, axis=1)
    sin = jnp.concatenate([-sine, sine] * 2, axis=1)

    ids, claim = expert_ids[0], claim_order[0]
    experts = jnp.arange(E, dtype=jnp.int32)
    chosen = jnp.max((ids[:, :, None] == experts[None, None, :]).astype(f32), axis=1)
    before = (claim[None, :] < claim[:, None]).astype(bf16)
    taken = dot(before, chosen.astype(bf16))
    kept = jnp.where(taken < CAP, chosen, 0.0)
    tables = jnp.concatenate([chosen, kept], axis=1).reshape(n, m, 2 * E)
    tables = jnp.sum(
        (blocks[:, None] == jnp.arange(n)[None, :]).astype(f32)[:, :, None, None] * tables[None], axis=1
    ).reshape(count, 2 * E)
    chosen, kept = tables[:, :E], tables[:, E:]

    x1, q, kv = whole_call(
        functools.partial(qkv_kernel, n, rows),
        (sds((count, d), bf16), sds((count, wide), bf16), sds((count, 256), bf16)),
        (where, *xs, gain_one, cos, sin, wa, wb),
        scratch=(pltpu.VMEM((d, cols), bf16),),
        flops=2 * count * d * cols,
        prefetch=1,
    )
    key_pos = positions.reshape(count, 1)
    if fancy:
        kvs = [kv, swap_x(kv)]
        poss = [key_pos, key_pos + (1 - 2 * seq_at) * count]
    else:
        kvs = [lax.all_gather(kv, "seq", axis=0, tiled=True)]
        poss = [lax.all_gather(key_pos.astype(f32), "seq", axis=0, tiled=True).astype(jnp.int32)]
    span = sum(v.shape[0] for v in kvs)
    heads = wide // HEAD
    got = whole_call(
        functools.partial(attend_kernel, len(kvs), n),
        tuple([sds((m, wide), bf16)] * n) + (sds((heads, HEAD, count), f32), sds((heads, 1, count), f32)),
        (q, limit, *kvs, *poss),
        scratch=(
            pltpu.VMEM((heads, count, HEAD), bf16),
            pltpu.VMEM((2, span, HEAD), bf16),
            pltpu.VMEM((2, HEAD, span), bf16),
            pltpu.VMEM((span, 1), jnp.int32),
        ),
        cost=10 ** 10,
    )
    mixed, (mixed_t, lse) = got[:n], got[n:]

    out_w = jnp.concatenate(spread(after(w_out, wa)), axis=1)
    cots = [cot] + spread(after(cot, kv))[1:]
    oa, ob = plane_gather(after(out_w, kvs[-1]), fancy, near=True, first=())
    mine = collect([mixed[0], *after_all(mixed[1:], cots[1:])])
    oa, ob = (oa, swap_core(after(oa, *mine))) if fancy else (oa, ob)
    middle, second = whole_call(
        functools.partial(middle_kernel, n),
        (sds((m, d), f32), sds((m, d), bf16)),
        (where, own, gain_two, oa, ob, *mine),
        scratch=(pltpu.VMEM((d, n * wide), bf16),),
        flops=2 * m * d * d,
        prefetch=1,
    )

    seconds = spread(second)

    packed = jnp.stack([w_gate, w_up, w_down])
    ws = lax.all_gather(packed, ("dp", "seq"), axis=0, tiled=False)
    eb, fe = EXPERTS_PER_STEP, w_gate.shape[2]
    steps = E // eb
    block = pl.BlockSpec((count, eb * fe), lambda s: (0, s))
    wide_out = sds((count, E * fe), bf16)
    got = pl.pallas_call(
        functools.partial(expert_kernel, n),
        out_shape=tuple([sds((m, d), bf16)] * n) + (wide_out, wide_out, wide_out, sds((E, d), f32)),
        grid=(steps,),
        in_specs=[full((count, E)), full((count, E)), full((d, E))]
        + [pl.BlockSpec((n_p, 3, eb, rows, fe), lambda s: (0, 0, s, 0, 0))]
        + [full((m, d))] * (2 * n),
        out_specs=[full((m, d))] * n + [block] * 3 + [full((E, d))],
        scratch_shapes=[
            pltpu.VMEM((count, d), bf16),
            pltpu.VMEM((count, d), bf16),
            pltpu.VMEM((d, 3 * eb * fe), bf16),
            pltpu.VMEM((count, d), f32),
            pltpu.VMEM((count, E), f32),
            pltpu.VMEM((count, E), f32),
        ],
        cost_estimate=pl.CostEstimate(flops=0, bytes_accessed=0, transcendentals=0),
    )(chosen, kept, router_all, ws, *seconds, *cots)
    second_parts, (active, gate_g, up_g, router_part) = got[:n], got[n:]
    half_p = n_p // 2
    got = pl.pallas_call(
        functools.partial(expert_back_kernel, n),
        out_shape=tuple([sds((m, d), bf16)] * n) + (sds((n_p, 3, E, rows, fe), bf16),),
        grid=(steps,),
        in_specs=[block] * 3
        + [pl.BlockSpec((n_p, 1, eb, rows, fe), lambda s: (0, 2, s, 0, 0))]
        + [full((m, d))] * (2 * n),
        out_specs=[full((m, d))] * n + [pl.BlockSpec((n_p, 3, eb, rows, fe), lambda s: (0, 0, s, 0, 0))],
        scratch_shapes=[
            pltpu.VMEM((d, count), bf16),
            pltpu.VMEM((d, count), bf16),
            pltpu.VMEM((d, eb * fe), bf16),
            pltpu.VMEM((count, d), f32),
        ],
        cost_estimate=pl.CostEstimate(flops=0, bytes_accessed=0, transcendentals=0),
    )(active, gate_g, up_g, ws, *seconds, *cots)
    out_parts, expert_parts = got[:n], got[n]

    sums = collect(second_parts)
    expert_parts = after(expert_parts, *sums)
    expert_grads = lax.psum_scatter(expert_parts, ("dp", "seq"), scatter_dimension=0, tiled=False)
    got = whole_call(
        functools.partial(middle_back_kernel, n),
        (sds((m, d), f32), sds((m, d), bf16), sds((1, d), f32)) + tuple([sds((m, wide), bf16)] * n),
        (where, middle, gain_two, cot, oa, ob, *sums),
        scratch=(pltpu.VMEM((d, n * wide), bf16),),
        flops=2 * m * d * d,
        prefetch=1,
    )
    (middle_grad, branch, gain_two_part), pieces = got[:3], got[3:]
    mixed_grads = collect(pieces)
    branches = [branch] + spread_by_two(after(branch, *mixed_grads))[1:]

    def attend_back(kv_one, pos_one, dtype, extra):
        one = kv_one.shape[0]
        last = bool(extra)
        return whole_call(
            functools.partial(attend_back_kernel, n, last),
            (
                sds((one, 256), dtype),
                sds((count, wide), bf16) if last else sds((heads, HEAD, count), f32),
            ),
            (q, limit, kv_one, pos_one, lse, mixed_t, *mixed_grads, *extra),
            scratch=(
                pltpu.VMEM((heads, count, HEAD), bf16),
                pltpu.VMEM((heads, count, HEAD), bf16),
                pltpu.VMEM((2, one, HEAD), bf16),
                pltpu.VMEM((2, one, HEAD), bf16),
                pltpu.VMEM((2, HEAD, one), bf16),
                pltpu.VMEM((heads, 1, count), f32),
                pltpu.VMEM((2, one, HEAD), f32),
                pltpu.VMEM((2, one, HEAD), f32),
                pltpu.VMEM((heads, HEAD, count), f32),
            ),
            cost=10 ** 10,
        )

    if fancy:
        far, dq_far = attend_back(kvs[1], poss[1], bf16, ())
        got_kv = (swap_x(far),)
        dkv, dq = attend_back(kvs[0], poss[0], f32, (dq_far, cos, sin))
    else:
        zero = jnp.zeros((heads, HEAD, count), f32)
        dkv, dq = attend_back(kvs[0], poss[0], bf16, (zero, cos, sin))
        dkv = lax.psum_scatter(dkv, "seq", scatter_dimension=0, tiled=True)
        got_kv = (jnp.zeros((count, 256), bf16),)

    out_sums = [out_parts[0]] + collect([out_parts[0], *after_all(out_parts[1:], mixed_grads)])[1:]
    dq_ready = after(dq, *branches[1:3])
    got = whole_call(
        functools.partial(qkv_back_kernel, n, rows),
        tuple([sds((m, d), bf16)] * n) + (sds((count, cols), bf16), sds((1, d), f32)),
        (where, dq_ready, dkv, *got_kv, cos, sin, wa, wb, *xs),
        scratch=(pltpu.VMEM((d, cols), bf16),),
        flops=2 * count * d * cols,
        prefetch=1,
    )
    first_parts, (grads, gain_one_part) = got[:n], got[n:]
    grads = after(grads, *out_sums[:3])
    sums = collect(first_parts)
    weight_shape = sds((half_p, rows + LINES, cols + wide), bf16)
    weight_keep, weight_send = whole_call(
        functools.partial(weight_back_kernel, n, rows),
        (weight_shape, weight_shape),
        (where, x1, grads, router_part, gain_one_part, gain_two_part, *branches, *mixed),
        scratch=(pltpu.VMEM((d, cols + wide), bf16), pltpu.VMEM((n_p, LINES, rows), bf16)),
        flops=2 * count * d * (cols + wide),
        prefetch=1,
    )

    (input_grad,) = whole_call(
        functools.partial(input_kernel, n), (sds((m, d), bf16),), (own, gain_one, middle_grad, *sums)
    )
    (output,) = whole_call(
        functools.partial(output_kernel, n), (sds((m, d), bf16),), (middle, *out_sums)
    )
    weights = plane_scatter(weight_keep, weight_send, fancy)
    total = weights[rows : rows + E + 2, :rows]
    total = sum(spread(total)[1:], total)
    total = lax.dynamic_slice_in_dim(total, me * shard, shard, axis=1)
    weights = weights[:rows]
    kv_wide = key_projection.shape[1]
    return (
        output[None],
        input_grad[None],
        weights[:, :wide],
        weights[:, wide : wide + kv_wide],
        weights[:, wide + kv_wide : cols],
        weights[:, cols:],
        expert_grads[0].astype(f32),
        expert_grads[1].astype(f32),
        expert_grads[2].astype(f32),
        total[E],
        total[E + 1],
        total[:E].T,
    )


def solution(mesh):
    placed = (
        P("dp", ("seq", "tensor"), None),
        P("dp", ("seq", "tensor"), None),
        P("dp", None),
        P("dp", "seq", None),
        P("dp", "seq"),
        P(("dp", "seq", "tensor")),
        P(("dp", "seq", "tensor")),
        P(("dp", "seq", "tensor"), None),
        P(("dp", "seq"), "tensor"),
        P(("dp", "seq"), "tensor"),
        P(("dp", "seq"), "tensor"),
        P(("dp", "seq"), "tensor"),
        P(None, ("dp", "seq"), "tensor"),
        P(None, ("dp", "seq"), "tensor"),
        P(None, ("dp", "seq"), "tensor"),
    )
    return jax.shard_map(
        per_device,
        mesh=mesh,
        in_specs=placed,
        out_specs=(
            P("dp", ("seq", "tensor"), None),
            P("dp", ("seq", "tensor"), None),
            P(("dp", "seq"), "tensor"),
            P(("dp", "seq"), "tensor"),
            P(("dp", "seq"), "tensor"),
            P(("dp", "seq"), "tensor"),
            P(None, ("dp", "seq"), "tensor"),
            P(None, ("dp", "seq"), "tensor"),
            P(None, ("dp", "seq"), "tensor"),
            P(("dp", "seq", "tensor")),
            P(("dp", "seq", "tensor")),
            P(("dp", "seq", "tensor"), None),
        ),
        check_vma=False,
    )
```

```python
import functools
import math

import jax
import jax.numpy as jnp
from jax import lax
from jax.experimental import pallas as pl
from jax.experimental.pallas import tpu as pltpu
from jax.sharding import PartitionSpec as P

HEAD = 64
E = 16
PIECE = 256
CAP = 320
COST = 10**10
EPS = 1e-06
FILL = -1e30
EXPERTS_PER_STEP = 4
ROW_TILE = 256
LINES = 32
f32 = jnp.float32
bf16 = jnp.bfloat16

NT = (((1,), (1,)), ((), ()))
NN = (((1,), (0,)), ((), ()))


def dot(a, b, dims=NN):
    return lax.dot_general(a, b, dims, preferred_element_type=f32)


def full(shape):
    rank = len(shape)
    return pl.BlockSpec(shape, lambda *_: (0,) * rank)


def whole_call(body, outs, args, scratch=(), flops=0, prefetch=0, cost=0):
    moved = sum(math.prod(a.shape) * a.dtype.itemsize for a in (*args, *outs))
    return pl.pallas_call(
        body,
        out_shape=outs,
        grid_spec=pltpu.PrefetchScalarGridSpec(
            num_scalar_prefetch=prefetch,
            grid=(1,),
            in_specs=[full(a.shape) for a in args[prefetch:]],
            out_specs=[full(o.shape) for o in outs],
            scratch_shapes=list(scratch),
        ),
        cost_estimate=pl.CostEstimate(flops=int(cost), bytes_accessed=0, transcendentals=0),
    )(*args)


def sds(shape, dtype):
    return jax.ShapeDtypeStruct(shape, dtype)


def turn(v, cos, sin):
    lane = lax.broadcasted_iota(jnp.int32, v.shape, 1) % HEAD
    other = jnp.where(lane < HEAD // 2, pltpu.roll(v, 128 - HEAD // 2, 1), pltpu.roll(v, HEAD // 2, 1))
    return v * cos + other * sin


def lay(out, stacks, where, rows):
    first = 0
    for r in stacks:
        for i in range(r.shape[0]):
            out[pl.ds(pl.multiple_of(where[first + i] * rows, rows), rows), :] = r[i, 0:rows, :]
        first += r.shape[0]


def qkv_kernel(n, rows, where, *refs):
    xs, (gain, cos, sin, wa, wb), (x1, q, kv, w) = refs[:n], refs[n : n + 5], refs[n + 5 :]
    lay(w, (wa, wb), where, rows)
    m = xs[0].shape[0]
    x_width = x1.shape[1]
    for j in range(n):
        v = xs[j][:, : x_width].astype(f32)
        r = lax.rsqrt(jnp.mean(v * v, axis=-1, keepdims=True) + EPS)
        x1[j * m : (j + 1) * m, :] = (v * r * gain[...]).astype(bf16)
    out = dot(x1[...], w[...])
    c, s = cos[...], sin[...]
    q[:, 0:128] = turn(out[:, 0:128], c, s).astype(bf16)
    q[:, 128:256] = turn(out[:, 128:256], c, s).astype(bf16)
    kv[:, 0:128] = turn(out[:, 256:384], c, s).astype(bf16)
    kv[:, 128:256] = out[:, 384:512].astype(bf16)


SCORE = HEAD ** (-0.5) * math.log2(math.e)


def attend_kernel(parts, n, q, lim, *refs):
    kvs, poss = refs[:parts], refs[parts : 2 * parts]
    mixed, (ot, lse) = refs[2 * parts : 2 * parts + n], refs[2 * parts + n : 2 * parts + n + 2]
    qs, ks, vt, kp = refs[2 * parts + n + 2 :]
    count = q.shape[0]
    heads = q.shape[1] // HEAD
    first = 0
    for kvr, pr in zip(kvs, poss):
        span = slice(first, first + kvr.shape[0])
        first += kvr.shape[0]
        v = kvr[:, 128:256].astype(f32).T.astype(bf16)
        for g in range(2):
            ks[g, span, :] = kvr[:, g * HEAD : (g + 1) * HEAD]
            vt[g, :, span] = v[g * HEAD : (g + 1) * HEAD, :]
        kp[span, :] = pr[...]
    for h in range(heads):
        qs[h] = q[:, h * HEAD : (h + 1) * HEAD]
    tiles = count // ROW_TILE

    def body(i, carry):
        h, t = i // tiles, i % tiles
        at = pl.ds(pl.multiple_of(t * ROW_TILE, ROW_TILE), ROW_TILE)
        g = h // 2
        s = dot(ks[g], qs[h, at, :], NT)
        s = jnp.where(kp[...] <= lim[:, at], s, FILL)
        top = jnp.max(s, axis=0, keepdims=True)
        p = jnp.exp2((s - top) * SCORE)
        total = jnp.sum(p, axis=0, keepdims=True)
        o = dot(vt[g], p.astype(bf16))
        ot[h, :, at] = o / total
        lse[h, :, at] = top * SCORE + jnp.log2(total)
        return carry

    lax.fori_loop(0, heads * tiles, body, 0)
    out = ot[...].reshape(heads * HEAD, count).T.astype(bf16)
    m = count // n
    for j in range(n):
        mixed[j][...] = out[j * m : (j + 1) * m, :]


def attend_back_kernel(n, last, q, lim, kv, kpos, lse, ot, *refs):
    dos_in, refs = refs[:n], refs[n:]
    if last:
        (dq_in, cos, sin), refs = refs[:3], refs[3:]
    dkv, dq_out = refs[:2]
    qs, dos, ks, vs, kt, delta, dk, dv, dqt = refs[2:]
    count = q.shape[0]
    heads = q.shape[1] // HEAD
    m = count // n
    for j in range(n):
        block = dos_in[j][...]
        turned = block.astype(f32).T
        for h in range(heads):
            span = slice(h * HEAD, (h + 1) * HEAD)
            dos[h, j * m : (j + 1) * m, :] = block[:, span]
            delta[h, :, j * m : (j + 1) * m] = jnp.sum(
                turned[span, :] * ot[h, :, j * m : (j + 1) * m], axis=0, keepdims=True
            )
    k_turned = kv[:, 0:128].astype(f32).T.astype(bf16)
    for g in range(2):
        ks[g] = kv[:, g * HEAD : (g + 1) * HEAD]
        vs[g] = kv[:, 128 + g * HEAD : 128 + (g + 1) * HEAD]
        kt[g] = k_turned[g * HEAD : (g + 1) * HEAD, :]
    for h in range(heads):
        qs[h] = q[:, h * HEAD : (h + 1) * HEAD]
    dk[...] = jnp.zeros_like(dk)
    dv[...] = jnp.zeros_like(dv)
    tiles = count // ROW_TILE

    def body(i, carry):
        h, t = i // tiles, i % tiles
        at = pl.ds(pl.multiple_of(t * ROW_TILE, ROW_TILE), ROW_TILE)
        g = h // 2
        q_h, do_h = qs[h, at, :], dos[h, at, :]
        s = dot(ks[g], q_h, NT)
        p = jnp.where(kpos[...] <= lim[:, at], jnp.exp2(s * SCORE - lse[h, :, at]), 0.0)
        dp = dot(vs[g], do_h, NT)
        ds = (p * (dp - delta[h, :, at])).astype(bf16)
        dv[g] += dot(p.astype(bf16), do_h)
        dk[g] += dot(ds, q_h)
        dqt[h, :, at] = dot(kt[g], ds)
        return carry

    lax.fori_loop(0, heads * tiles, body, 0)
    scale = HEAD ** (-0.5)
    dkv[...] = jnp.concatenate([dk[0] * scale, dk[1] * scale, dv[0], dv[1]], axis=1).astype(dkv.dtype)
    if last:
        whole = ((dqt[...] + dq_in[...]).reshape(heads * HEAD, count) * scale).T
        for half in range(2):
            lanes = slice(half * 128, (half + 1) * 128)
            dq_out[:, lanes] = turn(whole[:, lanes], cos[...], -sin[...]).astype(bf16)
    else:
        dq_out[...] = dqt[...]


def middle_kernel(n, where, x, gain, wa, wb, *refs):
    mixed, (middle, second, w) = refs[:n], refs[n:]
    lay(w, (wa, wb), where, wa.shape[1])
    both = jnp.concatenate([r[...] for r in mixed], axis=1)
    value = x[...].astype(f32) + dot(both, w[...], NT)
    middle[...] = value
    r = lax.rsqrt(jnp.mean(value * value, axis=-1, keepdims=True) + EPS)
    second[...] = (value * r * gain[...]).astype(bf16)


def middle_back_kernel(n, where, middle, gain, cot, wa, wb, *refs):
    parts, refs = refs[:n], refs[n:]
    middle_grad, branch, gain_grad = refs[:3]
    pieces, w = refs[3:-1], refs[-1]
    lay(w, (wa, wb), where, wa.shape[1])
    u = parts[0][...].astype(f32)
    for r in parts[1:]:
        u = u + r[...].astype(f32)
    value = middle[...]
    r = lax.rsqrt(jnp.mean(value * value, axis=-1, keepdims=True) + EPS)
    normal = value * r
    gain_grad[...] = jnp.sum(u * normal, axis=0, keepdims=True)
    scaled = u * gain[...]
    grad = cot[...].astype(f32) + r * (scaled - normal * jnp.mean(scaled * normal, axis=-1, keepdims=True))
    middle_grad[...] = grad
    low = grad.astype(bf16)
    branch[...] = low
    out = dot(low, w[...]).astype(bf16)
    wide = out.shape[1] // n
    for j in range(n):
        pieces[j][...] = out[:, j * wide : (j + 1) * wide]


def pick(table, index):
    lane = lax.broadcasted_iota(jnp.int32, table.shape, 1)
    return jnp.sum(jnp.where(lane == index, table, 0.0), axis=1, keepdims=True)


def expert_kernel(n, second, chosen, kept, router, ws, *refs):
    xs, cs, refs = refs[:n], refs[n : 2 * n], refs[2 * n :]
    if second:
        router_before, refs = refs[0], refs[4:]
    outs, (active_out, gate_out, up_out, router_grad) = refs[:n], refs[n : n + 4]
    x, c, w, total, soft, share = refs[n + 4 :]
    step, steps = pl.program_id(0), pl.num_programs(0)
    m = xs[0].shape[0]
    eb = EXPERTS_PER_STEP
    blocks, _, _, rows, fe = ws.shape
    wide = eb * fe

    @pl.when(step == 0)
    def _():
        for j in range(n):
            x[j * m : (j + 1) * m, :] = xs[j][...]
            c[j * m : (j + 1) * m, :] = cs[j][...]
        logits = jnp.where(chosen[...] > 0.0, dot(x[...], router[...]), FILL)
        top = jnp.max(logits, axis=1, keepdims=True)
        e = jnp.where(chosen[...] > 0.0, jnp.exp(logits - top), 0.0)
        soft[...] = e / jnp.sum(e, axis=1, keepdims=True)
        total[...] = jnp.zeros_like(total)
        share[...] = jnp.zeros_like(share)

    for b in range(blocks):
        for kind in range(3):
            for i in range(eb):
                at = kind * wide + i * fe
                w[b * rows : (b + 1) * rows, at : at + fe] = ws[b, kind, i]
    gu = dot(x[...], w[:, : 2 * wide])
    down = dot(c[...], w[:, 2 * wide :])
    table = soft[...] * kept[...]
    lane = lax.broadcasted_iota(jnp.int32, share.shape, 1)
    sums = jnp.zeros(share.shape, f32)
    gate_parts, up_parts = [], []
    for i in range(eb):
        span = slice(i * fe, (i + 1) * fe)
        gate, up, d = gu[:, span], gu[:, wide + i * fe : wide + (i + 1) * fe], down[:, span]
        index = step * eb + i
        weight = pick(table, index)
        sig = jax.nn.sigmoid(gate)
        silu = gate * sig
        active = silu * up
        active_out[:, span] = (active * weight).astype(bf16)
        sums = sums + jnp.where(lane == index, jnp.sum(active * d, axis=1, keepdims=True), 0.0)
        ag = d * weight
        gp = (ag * up * (sig * (1.0 + gate * (1.0 - sig)))).astype(bf16)
        ug = (ag * silu).astype(bf16)
        gate_out[:, span] = gp
        up_out[:, span] = ug
        gate_parts.append(gp)
        up_parts.append(ug)
    share[...] += sums
    total[...] += dot(jnp.concatenate(gate_parts + up_parts, axis=1), w[:, : 2 * wide], NT)

    @pl.when(step == steps - 1)
    def _():
        pair = share[...] * kept[...]
        mine = soft[...]
        logit = mine * (pair - jnp.sum(mine * pair, axis=1, keepdims=True))
        high = logit.astype(bf16)
        low = (logit - high.astype(f32)).astype(bf16)
        value = total[...] + (dot(high, router[...], NT) + dot(low, router[...], NT))
        for j in range(n):
            outs[j][...] = value[j * m : (j + 1) * m, :].astype(bf16)
        across_rows = (((0,), (0,)), ((), ()))
        value = dot(high, x[...], across_rows) + dot(low, x[...], across_rows)
        router_grad[...] = value + router_before[...] if second else value


def expert_back_kernel(n, active, gate, up, ws, *refs):
    xs, cs, refs = refs[:n], refs[n : 2 * n], refs[2 * n :]
    outs, grads = refs[:n], refs[n]
    xt, ct, w, total = refs[n + 1 :]
    step, steps = pl.program_id(0), pl.num_programs(0)
    m = xs[0].shape[0]
    eb = EXPERTS_PER_STEP
    blocks, _, _, rows, fe = ws.shape

    @pl.when(step == 0)
    def _():
        for j in range(n):
            xt[:, j * m : (j + 1) * m] = xs[j][...].T
            ct[:, j * m : (j + 1) * m] = cs[j][...].T
        total[...] = jnp.zeros_like(total)

    for b in range(blocks):
        for i in range(eb):
            w[b * rows : (b + 1) * rows, i * fe : (i + 1) * fe] = ws[b, 0, i]
    total[...] += dot(active[...], w[...], NT)
    for kind, (left, right) in enumerate(((xt, gate), (xt, up), (ct, active))):
        value = dot(left[...], right[...]).astype(bf16)
        for b in range(blocks):
            for i in range(eb):
                grads[b, kind, i] = value[b * rows : (b + 1) * rows, i * fe : (i + 1) * fe]

    @pl.when(step == steps - 1)
    def _():
        for j in range(n):
            outs[j][...] = total[j * m : (j + 1) * m, :].astype(bf16)


def qkv_back_kernel(n, rows, where, dq, dkv, got, cos, sin, wa, wb, *refs):
    xs, refs = refs[:n], refs[n:]
    outs, (grads, gain_grad, w) = refs[:n], refs[n:]
    lay(w, (wa, wb), where, rows)
    m = xs[0].shape[0]
    both = dkv[...].astype(f32)
    if got is not None:
        both = both + got[...].astype(f32)
    grads[:, 0:256] = dq[...]
    grads[:, 256:384] = turn(both[:, 0:128], cos[...], -sin[...]).astype(bf16)
    grads[:, 384:512] = both[:, 128:256].astype(bf16)
    u = dot(grads[...], w[...], NT)
    sums = jnp.zeros(gain_grad.shape, f32)
    x_width = u.shape[1]
    for j in range(n):
        v = xs[j][:, : x_width].astype(f32)
        r = lax.rsqrt(jnp.mean(v * v, axis=-1, keepdims=True) + EPS)
        part = u[j * m : (j + 1) * m, :]
        sums = sums + jnp.sum(part * (v * r), axis=0, keepdims=True)
        outs[j][...] = part.astype(bf16)
    gain_grad[...] = sums


def weight_back_kernel(n, rows, where, x1, grads, router_part, gain_one, gain_two, *refs):
    bs, ms, (keep, send, value, vectors) = refs[:n], refs[n : 2 * n], refs[2 * n :]
    wide = grads.shape[1]
    value[:, :wide] = dot(x1[...].T, grads[...]).astype(bf16)
    branch = jnp.concatenate([r[...] for r in bs], axis=0)
    mixed = jnp.concatenate([r[...] for r in ms], axis=0)
    value[:, wide:] = dot(branch.T, mixed).astype(bf16)
    lines = vectors.shape[1]
    for q in range(vectors.shape[0]):
        columns = slice(q * rows, (q + 1) * rows)
        block = [router_part[:, columns], gain_one[:, columns], gain_two[:, columns]]
        block.append(jnp.zeros((lines - E - 2, rows), f32))
        vectors[q] = jnp.concatenate(block, axis=0).astype(bf16)
    half = keep.shape[0]
    for b in range(2 * half):
        target = keep if b < half else send
        target[b % half, 0:rows, :] = value[pl.ds(pl.multiple_of(where[b] * rows, rows), rows), :]
        target[b % half, rows : rows + lines, 0:rows] = vectors[where[b]]
        target[b % half, rows : rows + lines, rows:] = jnp.zeros((lines, value.shape[1] - rows), bf16)


def input_kernel(n, x, gain, middle_grad, *refs):
    parts, out = refs[:n], refs[n]
    u = parts[0][...].astype(f32)
    for r in parts[1:]:
        u = u + r[...].astype(f32)
    v = x[...].astype(f32)
    r = lax.rsqrt(jnp.mean(v * v, axis=-1, keepdims=True) + EPS)
    normal = v * r
    scaled = u * gain[...]
    grad = r * (scaled - normal * jnp.mean(scaled * normal, axis=-1, keepdims=True))
    out[...] = (middle_grad[...] + grad).astype(bf16)


def output_kernel(n, middle, *refs):
    parts, out = refs[:n], refs[n]
    u = middle[...]
    for r in parts:
        u = u + r[...].astype(f32)
    out[...] = u.astype(bf16)


def across(v, j):
    return lax.ppermute(v, "tensor", [(i, i ^ j) for i in range(lax.axis_size("tensor"))])


def spread(v):
    return [v] + [across(v, j) for j in range(1, lax.axis_size("tensor"))]


def spread_by_two(v):
    if lax.axis_size("tensor") != 4:
        return spread(v)
    near = across(v, 1)
    return [v, near, across(v, 2), across(near, 2)]


def collect(parts):
    return [parts[0]] + [across(parts[j], j) for j in range(1, len(parts))]


def after(v, *others):
    return lax.optimization_barrier((v, *others))[0]


def swap_x(v):
    return lax.ppermute(v, "seq", [(0, 1), (1, 0)])


def swap_core(v):
    return lax.ppermute(v, "dp", [(i, i ^ 1) for i in range(4)])


def swap_y(v):
    return lax.ppermute(v, "dp", [(i, i ^ 2) for i in range(4)])


def swap_xy(v):
    return lax.ppermute(v, ("dp", "seq"), [(i, i ^ 5) for i in range(8)])


def after_all(values, others):
    return lax.optimization_barrier((*values, *others))[: len(values)]


def plane_gather(v, fancy, near=False, first=()):
    if fancy and near:
        near = after(jnp.stack([v, swap_x(v), swap_y(v), swap_xy(v)]), *first)
        return near, swap_core(near)
    if fancy:
        near = jnp.stack([v, swap_x(v)])
        near = jnp.concatenate([near, swap_y(near)])
        return near, swap_core(near)
    every = lax.all_gather(v, ("dp", "seq"), axis=0, tiled=False)
    half = every.shape[0] // 2
    return every[:half], every[half:]


def plane_scatter(keep, send, fancy):
    if not fancy:
        both = jnp.concatenate([keep, send], axis=0)
        return lax.psum_scatter(both, ("dp", "seq"), scatter_dimension=0, tiled=False).astype(f32)
    got = swap_core(send)
    low = [(keep[i].astype(f32) + got[i].astype(f32)).astype(bf16) for i in (1, 2, 3)]
    far = swap_x(low[0]).astype(f32) + swap_y(low[1]).astype(f32) + swap_xy(low[2]).astype(f32)
    return keep[0].astype(f32) + got[0].astype(f32) + far


def per_device(
    hidden_in,
    cotangent,
    piece_starts,
    expert_ids,
    claim_order,
    first_gain,
    second_gain,
    router,
    w_query,
    key_projection,
    value_projection,
    w_out,
    w_gate,
    w_up,
    w_down,
):
    n_dp, n_seq, n = lax.axis_size("dp"), lax.axis_size("seq"), lax.axis_size("tensor")
    fancy = n_dp == 4 and n_seq == 2
    n_p = n_dp * n_seq
    me = lax.axis_index("tensor")
    seq_at = lax.axis_index("seq")
    place = lax.axis_index("dp") * n_seq + seq_at
    m, d = hidden_in.shape[1:]
    count = m * n
    rows = d // n_p
    if hidden_in.shape[0] != 1 or expert_ids.shape[1] != count:
        raise ValueError("shapes")
    wide = w_query.shape[1]
    order = (0, 1, 4, 5, 2, 3, 6, 7) if fancy else tuple(range(n_p))
    where = (place ^ jnp.array(order, jnp.int32)) if fancy else jnp.arange(n_p, dtype=jnp.int32)

    own, cot = hidden_in[0], cotangent[0]

    shard = first_gain.shape[0]
    small = jnp.concatenate([router.reshape(-1), first_gain, second_gain])
    size = small.shape[0]
    smalls = spread(small.reshape(1, size))
    which = me ^ jnp.arange(n)
    pick_rows = (which[:, None] == jnp.arange(n)[None, :]).astype(f32)
    stacked = jnp.concatenate(smalls, axis=0).astype(f32)
    natural = jnp.sum(pick_rows[:, :, None] * stacked[None], axis=1).astype(bf16)
    qkv_w = jnp.concatenate([w_query, key_projection, value_projection], axis=1)
    cols = qkv_w.shape[1]
    natural = jnp.pad(natural.reshape(-1), (0, 16 * cols - n * size)).reshape(16, cols)
    xs = spread(own)
    wa, wb = plane_gather(jnp.concatenate([qkv_w, natural], axis=0), fancy, near=True)
    tail = jnp.concatenate([wa[:, rows:], wb[:, rows:]], axis=0).reshape(n_p, -1)[:, : n * size]
    ordered = (where[None, :] == jnp.arange(n_p, dtype=jnp.int32)[:, None]).astype(f32)
    tail = jnp.sum(ordered[:, :, None] * tail.astype(f32)[None], axis=1).reshape(n_p, n, size)
    gain_one = tail[:, :, size - 2 * shard : size - shard].reshape(1, d)
    gain_two = tail[:, :, size - shard :].reshape(1, d)
    router_all = tail[:, :, : size - 2 * shard].reshape(d, E).astype(bf16)

    blocks = me ^ jnp.arange(n, dtype=jnp.int32)
    positions = (seq_at * count + blocks[:, None] * m + jnp.arange(m, dtype=jnp.int32)[None, :]).reshape(count)
    starts = piece_starts[0]
    inside = (positions[:, None] >= starts[None, :]) & (positions[:, None] < starts[None, :] + PIECE)
    limit = jnp.maximum(
        positions, jnp.max(jnp.where(inside, starts[None, :] + PIECE - 1, -1), axis=1)
    ).reshape(1, count)
    half = HEAD // 2
    freqs = jnp.exp(jnp.arange(half).astype(f32) * (-2.0 * math.log(10000.0) / HEAD))
    angles = positions.astype(f32)[:, None] * freqs[None, :]
    cosine, sine = jnp.cos(angles), jnp.sin(angles)
    cos = jnp.concatenate([cosine] * 4, axis=1)
    sin = jnp.concatenate([-sine, sine] * 2, axis=1)

    ids, claim = expert_ids[0], claim_order[0]
    experts = jnp.arange(E, dtype=jnp.int32)
    chosen = jnp.max((ids[:, :, None] == experts[None, None, :]).astype(f32), axis=1)
    before = (claim[None, :] < claim[:, None]).astype(bf16)
    taken = dot(before, chosen.astype(bf16))
    kept = jnp.where(taken < CAP, chosen, 0.0)
    tables = jnp.concatenate([chosen, kept], axis=1).reshape(n, m, 2 * E)
    tables = jnp.sum(
        (blocks[:, None] == jnp.arange(n)[None, :]).astype(f32)[:, :, None, None] * tables[None], axis=1
    ).reshape(count, 2 * E)
    chosen, kept = tables[:, :E], tables[:, E:]

    x1, q, kv = whole_call(
        functools.partial(qkv_kernel, n, rows),
        (sds((count, d), bf16), sds((count, wide), bf16), sds((count, 256), bf16)),
        (where, *xs, gain_one, cos, sin, wa, wb),
        scratch=(pltpu.VMEM((d, cols), bf16),),
        flops=2 * count * d * cols,
        prefetch=1,
    )
    key_pos = positions.reshape(count, 1)
    if fancy:
        kvs = [kv, swap_x(kv)]
        poss = [key_pos, key_pos + (1 - 2 * seq_at) * count]
    else:
        kvs = [lax.all_gather(kv, "seq", axis=0, tiled=True)]
        poss = [lax.all_gather(key_pos.astype(f32), "seq", axis=0, tiled=True).astype(jnp.int32)]
    span = sum(v.shape[0] for v in kvs)
    heads = wide // HEAD
    got = whole_call(
        functools.partial(attend_kernel, len(kvs), n),
        tuple([sds((m, wide), bf16)] * n) + (sds((heads, HEAD, count), f32), sds((heads, 1, count), f32)),
        (q, limit, *kvs, *poss),
        scratch=(
            pltpu.VMEM((heads, count, HEAD), bf16),
            pltpu.VMEM((2, span, HEAD), bf16),
            pltpu.VMEM((2, HEAD, span), bf16),
            pltpu.VMEM((span, 1), jnp.int32),
        ),
        cost=10 ** 10,
    )
    mixed, (mixed_t, lse) = got[:n], got[n:]

    out_w = jnp.concatenate(spread(after(w_out, wa)), axis=1)
    cots = [cot] + spread(after(cot, kv))[1:]
    oa, ob = plane_gather(after(out_w, kvs[-1]), fancy, near=True, first=())
    mine = collect([mixed[0], *after_all(mixed[1:], cots[1:])])
    oa, ob = (oa, swap_core(after(oa, *mine))) if fancy else (oa, ob)
    middle, second = whole_call(
        functools.partial(middle_kernel, n),
        (sds((m, d), f32), sds((m, d), bf16)),
        (where, own, gain_two, oa, ob, *mine),
        scratch=(pltpu.VMEM((d, n * wide), bf16),),
        flops=2 * m * d * d,
        prefetch=1,
    )

    seconds = spread(second)

    packed = jnp.stack([w_gate, w_up, w_down])
    ws = lax.all_gather(packed, ("dp", "seq"), axis=0, tiled=False)
    eb, fe = EXPERTS_PER_STEP, w_gate.shape[2]
    steps = E // eb
    block = pl.BlockSpec((count, eb * fe), lambda s: (0, s))
    wide_out = sds((count, E * fe), bf16)
    def expert_call(at, parts, begun):
        tall = m * parts
        return pl.pallas_call(
            functools.partial(expert_kernel, parts, bool(begun)),
            out_shape=tuple([sds((m, d), bf16)] * parts) + (wide_out, wide_out, wide_out, sds((E, d), f32)),
            grid=(steps,),
            in_specs=[full((tall, E)), full((tall, E)), full((d, E))]
            + [pl.BlockSpec((n_p, 3, eb, rows, fe), lambda s: (0, 0, s, 0, 0))]
            + [full((m, d))] * (2 * parts)
            + ([full((E, d))] + [pl.BlockSpec(memory_space=pl.ANY)] * 3 if begun else []),
            out_specs=[full((m, d))] * parts
            + [pl.BlockSpec((tall, eb * fe), lambda s: (at // parts, s))] * 3
            + [full((E, d))],
            scratch_shapes=[
                pltpu.VMEM((tall, d), bf16),
                pltpu.VMEM((tall, d), bf16),
                pltpu.VMEM((d, 3 * eb * fe), bf16),
                pltpu.VMEM((tall, d), f32),
                pltpu.VMEM((tall, E), f32),
                pltpu.VMEM((tall, E), f32),
            ],
            input_output_aliases={5 + 2 * parts + i: parts + i for i in range(3)} if begun else {},
            cost_estimate=pl.CostEstimate(flops=0 if begun else COST, bytes_accessed=0, transcendentals=0),
        )(
            chosen[at * m : at * m + tall],
            kept[at * m : at * m + tall],
            router_all,
            ws,
            *seconds[at : at + parts],
            *cots[at : at + parts],
            *begun,
        )

    split = n // 2 if n % 2 == 0 else n
    got = expert_call(0, split, ())
    second_parts, (active, gate_g, up_g, router_part) = got[:split], got[split:]
    if split < n:
        got = expert_call(split, split, (router_part, active, gate_g, up_g))
        second_parts, (active, gate_g, up_g, router_part) = (*second_parts, *got[:split]), got[split:]
    half_p = n_p // 2
    got = pl.pallas_call(
        functools.partial(expert_back_kernel, n),
        out_shape=tuple([sds((m, d), bf16)] * n) + (sds((n_p, 3, E, rows, fe), bf16),),
        grid=(steps,),
        in_specs=[block] * 3
        + [pl.BlockSpec((n_p, 1, eb, rows, fe), lambda s: (0, 2, s, 0, 0))]
        + [full((m, d))] * (2 * n),
        out_specs=[full((m, d))] * n + [pl.BlockSpec((n_p, 3, eb, rows, fe), lambda s: (0, 0, s, 0, 0))],
        scratch_shapes=[
            pltpu.VMEM((d, count), bf16),
            pltpu.VMEM((d, count), bf16),
            pltpu.VMEM((d, eb * fe), bf16),
            pltpu.VMEM((count, d), f32),
        ],
        cost_estimate=pl.CostEstimate(flops=0, bytes_accessed=0, transcendentals=0),
    )(active, gate_g, up_g, ws, *seconds, *cots)
    out_parts, expert_parts = got[:n], got[n]

    sums = collect(second_parts)
    expert_parts = after(expert_parts, *sums)
    expert_grads = lax.psum_scatter(expert_parts, ("dp", "seq"), scatter_dimension=0, tiled=False)
    got = whole_call(
        functools.partial(middle_back_kernel, n),
        (sds((m, d), f32), sds((m, d), bf16), sds((1, d), f32)) + tuple([sds((m, wide), bf16)] * n),
        (where, middle, gain_two, cot, oa, ob, *sums),
        scratch=(pltpu.VMEM((d, n * wide), bf16),),
        flops=2 * m * d * d,
        prefetch=1,
    )
    (middle_grad, branch, gain_two_part), pieces = got[:3], got[3:]
    mixed_grads = collect(pieces)
    branches = [branch] + spread_by_two(after(branch, *mixed_grads))[1:]

    def attend_back(kv_one, pos_one, dtype, extra):
        one = kv_one.shape[0]
        last = bool(extra)
        return whole_call(
            functools.partial(attend_back_kernel, n, last),
            (
                sds((one, 256), dtype),
                sds((count, wide), bf16) if last else sds((heads, HEAD, count), f32),
            ),
            (q, limit, kv_one, pos_one, lse, mixed_t, *mixed_grads, *extra),
            scratch=(
                pltpu.VMEM((heads, count, HEAD), bf16),
                pltpu.VMEM((heads, count, HEAD), bf16),
                pltpu.VMEM((2, one, HEAD), bf16),
                pltpu.VMEM((2, one, HEAD), bf16),
                pltpu.VMEM((2, HEAD, one), bf16),
                pltpu.VMEM((heads, 1, count), f32),
                pltpu.VMEM((2, one, HEAD), f32),
                pltpu.VMEM((2, one, HEAD), f32),
                pltpu.VMEM((heads, HEAD, count), f32),
            ),
            cost=10 ** 10,
        )

    if fancy:
        far, dq_far = attend_back(kvs[1], poss[1], bf16, ())
        got_kv = (swap_x(far),)
        dkv, dq = attend_back(kvs[0], poss[0], f32, (dq_far, cos, sin))
    else:
        zero = jnp.zeros((heads, HEAD, count), f32)
        dkv, dq = attend_back(kvs[0], poss[0], bf16, (zero, cos, sin))
        dkv = lax.psum_scatter(dkv, "seq", scatter_dimension=0, tiled=True)
        got_kv = (jnp.zeros((count, 256), bf16),)

    out_sums = [out_parts[0]] + collect([out_parts[0], *after_all(out_parts[1:], mixed_grads)])[1:]
    dq_ready = after(dq, *branches[1:3])
    got = whole_call(
        functools.partial(qkv_back_kernel, n, rows),
        tuple([sds((m, d), bf16)] * n) + (sds((count, cols), bf16), sds((1, d), f32)),
        (where, dq_ready, dkv, *got_kv, cos, sin, wa, wb, *xs),
        scratch=(pltpu.VMEM((d, cols), bf16),),
        flops=2 * count * d * cols,
        prefetch=1,
    )
    first_parts, (grads, gain_one_part) = got[:n], got[n:]
    grads = after(grads, *out_sums[:3])
    sums = collect(first_parts)
    weight_shape = sds((half_p, rows + LINES, cols + wide), bf16)
    weight_keep, weight_send = whole_call(
        functools.partial(weight_back_kernel, n, rows),
        (weight_shape, weight_shape),
        (where, x1, grads, router_part, gain_one_part, gain_two_part, *branches, *mixed),
        scratch=(pltpu.VMEM((d, cols + wide), bf16), pltpu.VMEM((n_p, LINES, rows), bf16)),
        flops=2 * count * d * (cols + wide),
        prefetch=1,
    )

    (input_grad,) = whole_call(
        functools.partial(input_kernel, n), (sds((m, d), bf16),), (own, gain_one, middle_grad, *sums)
    )
    (output,) = whole_call(
        functools.partial(output_kernel, n), (sds((m, d), bf16),), (middle, *out_sums)
    )
    weights = plane_scatter(weight_keep, weight_send, fancy)
    total = weights[rows : rows + E + 2, :rows]
    total = sum(spread(total)[1:], total)
    total = lax.dynamic_slice_in_dim(total, me * shard, shard, axis=1)
    weights = weights[:rows]
    kv_wide = key_projection.shape[1]
    return (
        output[None],
        input_grad[None],
        weights[:, :wide],
        weights[:, wide : wide + kv_wide],
        weights[:, wide + kv_wide : cols],
        weights[:, cols:],
        expert_grads[0].astype(f32),
        expert_grads[1].astype(f32),
        expert_grads[2].astype(f32),
        total[E],
        total[E + 1],
        total[:E].T,
    )


def solution(mesh):
    placed = (
        P("dp", ("seq", "tensor"), None),
        P("dp", ("seq", "tensor"), None),
        P("dp", None),
        P("dp", "seq", None),
        P("dp", "seq"),
        P(("dp", "seq", "tensor")),
        P(("dp", "seq", "tensor")),
        P(("dp", "seq", "tensor"), None),
        P(("dp", "seq"), "tensor"),
        P(("dp", "seq"), "tensor"),
        P(("dp", "seq"), "tensor"),
        P(("dp", "seq"), "tensor"),
        P(None, ("dp", "seq"), "tensor"),
        P(None, ("dp", "seq"), "tensor"),
        P(None, ("dp", "seq"), "tensor"),
    )
    return jax.shard_map(
        per_device,
        mesh=mesh,
        in_specs=placed,
        out_specs=(
            P("dp", ("seq", "tensor"), None),
            P("dp", ("seq", "tensor"), None),
            P(("dp", "seq"), "tensor"),
            P(("dp", "seq"), "tensor"),
            P(("dp", "seq"), "tensor"),
            P(("dp", "seq"), "tensor"),
            P(None, ("dp", "seq"), "tensor"),
            P(None, ("dp", "seq"), "tensor"),
            P(None, ("dp", "seq"), "tensor"),
            P(("dp", "seq", "tensor")),
            P(("dp", "seq", "tensor")),
            P(("dp", "seq", "tensor"), None),
        ),
        check_vma=False,
    )
```

```python
import functools
import math

import jax
import jax.numpy as jnp
from jax import lax
from jax.experimental import pallas as pl
from jax.experimental.pallas import tpu as pltpu
from jax.sharding import PartitionSpec as P

HEAD = 64
E = 16
PIECE = 256
CAP = 320
COST = 10**10
EPS = 1e-06
FILL = -1e30
EXPERTS_PER_STEP = 4
ROW_TILE = 256
LINES = 32
f32 = jnp.float32
bf16 = jnp.bfloat16

NT = (((1,), (1,)), ((), ()))
NN = (((1,), (0,)), ((), ()))


def dot(a, b, dims=NN):
    return lax.dot_general(a, b, dims, preferred_element_type=f32)


def full(shape):
    rank = len(shape)
    return pl.BlockSpec(shape, lambda *_: (0,) * rank)


def whole_call(body, outs, args, scratch=(), flops=0, prefetch=0, cost=0):
    moved = sum(math.prod(a.shape) * a.dtype.itemsize for a in (*args, *outs))
    return pl.pallas_call(
        body,
        out_shape=outs,
        grid_spec=pltpu.PrefetchScalarGridSpec(
            num_scalar_prefetch=prefetch,
            grid=(1,),
            in_specs=[full(a.shape) for a in args[prefetch:]],
            out_specs=[full(o.shape) for o in outs],
            scratch_shapes=list(scratch),
        ),
        cost_estimate=pl.CostEstimate(flops=int(cost), bytes_accessed=0, transcendentals=0),
    )(*args)


def sds(shape, dtype):
    return jax.ShapeDtypeStruct(shape, dtype)


def turn(v, cos, sin):
    lane = lax.broadcasted_iota(jnp.int32, v.shape, 1) % HEAD
    other = jnp.where(lane < HEAD // 2, pltpu.roll(v, 128 - HEAD // 2, 1), pltpu.roll(v, HEAD // 2, 1))
    return v * cos + other * sin


def lay(out, stacks, where, rows):
    first = 0
    for r in stacks:
        for i in range(r.shape[0]):
            out[pl.ds(pl.multiple_of(where[first + i] * rows, rows), rows), :] = r[i, 0:rows, :]
        first += r.shape[0]


def qkv_kernel(n, rows, where, *refs):
    xs, (gain, cos, sin, wa, wb), (x1, q, kv, w) = refs[:n], refs[n : n + 5], refs[n + 5 :]
    lay(w, (wa, wb), where, rows)
    m = xs[0].shape[0]
    x_width = x1.shape[1]
    for j in range(n):
        v = xs[j][:, : x_width].astype(f32)
        r = lax.rsqrt(jnp.mean(v * v, axis=-1, keepdims=True) + EPS)
        x1[j * m : (j + 1) * m, :] = (v * r * gain[...]).astype(bf16)
    out = dot(x1[...], w[...])
    c, s = cos[...], sin[...]
    q[:, 0:128] = turn(out[:, 0:128], c, s).astype(bf16)
    q[:, 128:256] = turn(out[:, 128:256], c, s).astype(bf16)
    kv[:, 0:128] = turn(out[:, 256:384], c, s).astype(bf16)
    kv[:, 128:256] = out[:, 384:512].astype(bf16)


SCORE = HEAD ** (-0.5) * math.log2(math.e)


def attend_kernel(parts, n, q, lim, *refs):
    kvs, poss = refs[:parts], refs[parts : 2 * parts]
    mixed, (ot, lse) = refs[2 * parts : 2 * parts + n], refs[2 * parts + n : 2 * parts + n + 2]
    qs, ks, vt, kp = refs[2 * parts + n + 2 :]
    count = q.shape[0]
    heads = q.shape[1] // HEAD
    first = 0
    for kvr, pr in zip(kvs, poss):
        span = slice(first, first + kvr.shape[0])
        first += kvr.shape[0]
        v = kvr[:, 128:256].astype(f32).T.astype(bf16)
        for g in range(2):
            ks[g, span, :] = kvr[:, g * HEAD : (g + 1) * HEAD]
            vt[g, :, span] = v[g * HEAD : (g + 1) * HEAD, :]
        kp[span, :] = pr[...]
    for h in range(heads):
        qs[h] = q[:, h * HEAD : (h + 1) * HEAD]
    tiles = count // ROW_TILE

    def body(i, carry):
        h, t = i // tiles, i % tiles
        at = pl.ds(pl.multiple_of(t * ROW_TILE, ROW_TILE), ROW_TILE)
        g = h // 2
        s = dot(ks[g], qs[h, at, :], NT)
        s = jnp.where(kp[...] <= lim[:, at], s, FILL)
        top = jnp.max(s, axis=0, keepdims=True)
        p = jnp.exp2((s - top) * SCORE)
        total = jnp.sum(p, axis=0, keepdims=True)
        o = dot(vt[g], p.astype(bf16))
        ot[h, :, at] = o / total
        lse[h, :, at] = top * SCORE + jnp.log2(total)
        return carry

    lax.fori_loop(0, heads * tiles, body, 0)
    out = ot[...].reshape(heads * HEAD, count).T.astype(bf16)
    m = count // n
    for j in range(n):
        mixed[j][...] = out[j * m : (j + 1) * m, :]


def attend_back_kernel(n, last, q, lim, kv, kpos, lse, ot, *refs):
    dos_in, refs = refs[:n], refs[n:]
    if last:
        (dq_in, cos, sin), refs = refs[:3], refs[3:]
    dkv, dq_out = refs[:2]
    qs, dos, ks, vs, kt, delta, dk, dv, dqt = refs[2:]
    count = q.shape[0]
    heads = q.shape[1] // HEAD
    m = count // n
    for j in range(n):
        block = dos_in[j][...]
        turned = block.astype(f32).T
        for h in range(heads):
            span = slice(h * HEAD, (h + 1) * HEAD)
            dos[h, j * m : (j + 1) * m, :] = block[:, span]
            delta[h, :, j * m : (j + 1) * m] = jnp.sum(
                turned[span, :] * ot[h, :, j * m : (j + 1) * m], axis=0, keepdims=True
            )
    k_turned = kv[:, 0:128].astype(f32).T.astype(bf16)
    for g in range(2):
        ks[g] = kv[:, g * HEAD : (g + 1) * HEAD]
        vs[g] = kv[:, 128 + g * HEAD : 128 + (g + 1) * HEAD]
        kt[g] = k_turned[g * HEAD : (g + 1) * HEAD, :]
    for h in range(heads):
        qs[h] = q[:, h * HEAD : (h + 1) * HEAD]
    dk[...] = jnp.zeros_like(dk)
    dv[...] = jnp.zeros_like(dv)
    tiles = count // ROW_TILE

    def body(i, carry):
        h, t = i // tiles, i % tiles
        at = pl.ds(pl.multiple_of(t * ROW_TILE, ROW_TILE), ROW_TILE)
        g = h // 2
        q_h, do_h = qs[h, at, :], dos[h, at, :]
        s = dot(ks[g], q_h, NT)
        p = jnp.where(kpos[...] <= lim[:, at], jnp.exp2(s * SCORE - lse[h, :, at]), 0.0)
        dp = dot(vs[g], do_h, NT)
        ds = (p * (dp - delta[h, :, at])).astype(bf16)
        dv[g] += dot(p.astype(bf16), do_h)
        dk[g] += dot(ds, q_h)
        dqt[h, :, at] = dot(kt[g], ds)
        return carry

    lax.fori_loop(0, heads * tiles, body, 0)
    scale = HEAD ** (-0.5)
    dkv[...] = jnp.concatenate([dk[0] * scale, dk[1] * scale, dv[0], dv[1]], axis=1).astype(dkv.dtype)
    if last:
        whole = ((dqt[...] + dq_in[...]).reshape(heads * HEAD, count) * scale).T
        for half in range(2):
            lanes = slice(half * 128, (half + 1) * 128)
            dq_out[:, lanes] = turn(whole[:, lanes], cos[...], -sin[...]).astype(bf16)
    else:
        dq_out[...] = dqt[...]


def middle_kernel(n, where, x, gain, wa, wb, *refs):
    mixed, (middle, second, w) = refs[:n], refs[n:]
    lay(w, (wa, wb), where, wa.shape[1])
    both = jnp.concatenate([r[...] for r in mixed], axis=1)
    value = x[...].astype(f32) + dot(both, w[...], NT)
    middle[...] = value
    r = lax.rsqrt(jnp.mean(value * value, axis=-1, keepdims=True) + EPS)
    second[...] = (value * r * gain[...]).astype(bf16)


def middle_back_kernel(n, where, middle, gain, cot, wa, wb, *refs):
    parts, refs = refs[:n], refs[n:]
    middle_grad, branch, gain_grad = refs[:3]
    pieces, w = refs[3:-1], refs[-1]
    lay(w, (wa, wb), where, wa.shape[1])
    u = parts[0][...].astype(f32)
    for r in parts[1:]:
        u = u + r[...].astype(f32)
    value = middle[...]
    r = lax.rsqrt(jnp.mean(value * value, axis=-1, keepdims=True) + EPS)
    normal = value * r
    gain_grad[...] = jnp.sum(u * normal, axis=0, keepdims=True)
    scaled = u * gain[...]
    grad = cot[...].astype(f32) + r * (scaled - normal * jnp.mean(scaled * normal, axis=-1, keepdims=True))
    middle_grad[...] = grad
    low = grad.astype(bf16)
    branch[...] = low
    out = dot(low, w[...]).astype(bf16)
    wide = out.shape[1] // n
    for j in range(n):
        pieces[j][...] = out[:, j * wide : (j + 1) * wide]


def pick(table, index):
    lane = lax.broadcasted_iota(jnp.int32, table.shape, 1)
    return jnp.sum(jnp.where(lane == index, table, 0.0), axis=1, keepdims=True)


def expert_kernel(n, second, chosen, kept, router, ws, *refs):
    xs, cs, refs = refs[:n], refs[n : 2 * n], refs[2 * n :]
    if second:
        router_before, refs = refs[0], refs[4:]
    outs, (active_out, gate_out, up_out, router_grad) = refs[:n], refs[n : n + 4]
    x, c, w, total, soft, share = refs[n + 4 :]
    step, steps = pl.program_id(0), pl.num_programs(0)
    m = xs[0].shape[0]
    eb = EXPERTS_PER_STEP
    blocks, _, _, rows, fe = ws.shape
    wide = eb * fe

    @pl.when(step == 0)
    def _():
        for j in range(n):
            x[j * m : (j + 1) * m, :] = xs[j][...]
            c[j * m : (j + 1) * m, :] = cs[j][...]
        logits = jnp.where(chosen[...] > 0.0, dot(x[...], router[...]), FILL)
        top = jnp.max(logits, axis=1, keepdims=True)
        e = jnp.where(chosen[...] > 0.0, jnp.exp(logits - top), 0.0)
        soft[...] = e / jnp.sum(e, axis=1, keepdims=True)
        total[...] = jnp.zeros_like(total)
        share[...] = jnp.zeros_like(share)

    for b in range(blocks):
        for kind in range(3):
            for i in range(eb):
                at = kind * wide + i * fe
                w[b * rows : (b + 1) * rows, at : at + fe] = ws[b, kind, i]
    gu = dot(x[...], w[:, : 2 * wide])
    down = dot(c[...], w[:, 2 * wide :])
    table = soft[...] * kept[...]
    lane = lax.broadcasted_iota(jnp.int32, share.shape, 1)
    sums = jnp.zeros(share.shape, f32)
    gate_parts, up_parts = [], []
    for i in range(eb):
        span = slice(i * fe, (i + 1) * fe)
        gate, up, d = gu[:, span], gu[:, wide + i * fe : wide + (i + 1) * fe], down[:, span]
        index = step * eb + i
        weight = pick(table, index)
        sig = jax.nn.sigmoid(gate)
        silu = gate * sig
        active = silu * up
        active_out[:, span] = (active * weight).astype(bf16)
        sums = sums + jnp.where(lane == index, jnp.sum(active * d, axis=1, keepdims=True), 0.0)
        ag = d * weight
        gp = (ag * up * (sig * (1.0 + gate * (1.0 - sig)))).astype(bf16)
        ug = (ag * silu).astype(bf16)
        gate_out[:, span] = gp
        up_out[:, span] = ug
        gate_parts.append(gp)
        up_parts.append(ug)
    share[...] += sums
    total[...] += dot(jnp.concatenate(gate_parts + up_parts, axis=1), w[:, : 2 * wide], NT)

    @pl.when(step == steps - 1)
    def _():
        pair = share[...] * kept[...]
        mine = soft[...]
        logit = mine * (pair - jnp.sum(mine * pair, axis=1, keepdims=True))
        high = logit.astype(bf16)
        low = (logit - high.astype(f32)).astype(bf16)
        value = total[...] + (dot(high, router[...], NT) + dot(low, router[...], NT))
        for j in range(n):
            outs[j][...] = value[j * m : (j + 1) * m, :].astype(bf16)
        across_rows = (((0,), (0,)), ((), ()))
        value = dot(high, x[...], across_rows) + dot(low, x[...], across_rows)
        router_grad[...] = value + router_before[...] if second else value


def expert_back_kernel(n, active, gate, up, ws, *refs):
    xs, cs, refs = refs[:n], refs[n : 2 * n], refs[2 * n :]
    outs, grads = refs[:n], refs[n]
    xt, ct, w, total = refs[n + 1 :]
    step, steps = pl.program_id(0), pl.num_programs(0)
    m = xs[0].shape[0]
    eb = EXPERTS_PER_STEP
    blocks, _, _, rows, fe = ws.shape

    @pl.when(step == 0)
    def _():
        for j in range(n):
            xt[:, j * m : (j + 1) * m] = xs[j][...].T
            ct[:, j * m : (j + 1) * m] = cs[j][...].T
        total[...] = jnp.zeros_like(total)

    for b in range(blocks):
        for i in range(eb):
            w[b * rows : (b + 1) * rows, i * fe : (i + 1) * fe] = ws[b, 0, i]
    total[...] += dot(active[...], w[...], NT)
    for kind, (left, right) in enumerate(((xt, gate), (xt, up), (ct, active))):
        value = dot(left[...], right[...]).astype(bf16)
        for b in range(blocks):
            for i in range(eb):
                grads[b, kind, i] = value[b * rows : (b + 1) * rows, i * fe : (i + 1) * fe]

    @pl.when(step == steps - 1)
    def _():
        for j in range(n):
            outs[j][...] = total[j * m : (j + 1) * m, :].astype(bf16)


def qkv_back_kernel(n, rows, where, dq, dkv, got, cos, sin, wa, wb, *refs):
    xs, refs = refs[:n], refs[n:]
    outs, (grads, gain_grad, w) = refs[:n], refs[n:]
    lay(w, (wa, wb), where, rows)
    m = xs[0].shape[0]
    both = dkv[...].astype(f32)
    if got is not None:
        both = both + got[...].astype(f32)
    grads[:, 0:256] = dq[...]
    grads[:, 256:384] = turn(both[:, 0:128], cos[...], -sin[...]).astype(bf16)
    grads[:, 384:512] = both[:, 128:256].astype(bf16)
    u = dot(grads[...], w[...], NT)
    sums = jnp.zeros(gain_grad.shape, f32)
    x_width = u.shape[1]
    for j in range(n):
        v = xs[j][:, : x_width].astype(f32)
        r = lax.rsqrt(jnp.mean(v * v, axis=-1, keepdims=True) + EPS)
        part = u[j * m : (j + 1) * m, :]
        sums = sums + jnp.sum(part * (v * r), axis=0, keepdims=True)
        outs[j][...] = part.astype(bf16)
    gain_grad[...] = sums


def weight_back_kernel(n, rows, where, x1, grads, router_part, gain_one, gain_two, *refs):
    bs, ms, (keep, send, value, vectors) = refs[:n], refs[n : 2 * n], refs[2 * n :]
    wide = grads.shape[1]
    value[:, :wide] = dot(x1[...].T, grads[...]).astype(bf16)
    branch = jnp.concatenate([r[...] for r in bs], axis=0)
    mixed = jnp.concatenate([r[...] for r in ms], axis=0)
    value[:, wide:] = dot(branch.T, mixed).astype(bf16)
    lines = vectors.shape[1]
    for q in range(vectors.shape[0]):
        columns = slice(q * rows, (q + 1) * rows)
        block = [router_part[:, columns], gain_one[:, columns], gain_two[:, columns]]
        block.append(jnp.zeros((lines - E - 2, rows), f32))
        vectors[q] = jnp.concatenate(block, axis=0).astype(bf16)
    half = keep.shape[0]
    for b in range(2 * half):
        target = keep if b < half else send
        target[b % half, 0:rows, :] = value[pl.ds(pl.multiple_of(where[b] * rows, rows), rows), :]
        target[b % half, rows : rows + lines, 0:rows] = vectors[where[b]]
        target[b % half, rows : rows + lines, rows:] = jnp.zeros((lines, value.shape[1] - rows), bf16)


def input_kernel(n, x, gain, middle_grad, *refs):
    parts, out = refs[:n], refs[n]
    u = parts[0][...].astype(f32)
    for r in parts[1:]:
        u = u + r[...].astype(f32)
    v = x[...].astype(f32)
    r = lax.rsqrt(jnp.mean(v * v, axis=-1, keepdims=True) + EPS)
    normal = v * r
    scaled = u * gain[...]
    grad = r * (scaled - normal * jnp.mean(scaled * normal, axis=-1, keepdims=True))
    out[...] = (middle_grad[...] + grad).astype(bf16)


def output_kernel(n, middle, *refs):
    parts, out = refs[:n], refs[n]
    u = middle[...]
    for r in parts:
        u = u + r[...].astype(f32)
    out[...] = u.astype(bf16)


def across(v, j):
    return lax.ppermute(v, "tensor", [(i, i ^ j) for i in range(lax.axis_size("tensor"))])


def spread(v):
    return [v] + [across(v, j) for j in range(1, lax.axis_size("tensor"))]


def spread_by_two(v):
    if lax.axis_size("tensor") != 4:
        return spread(v)
    near = across(v, 1)
    return [v, near, across(v, 2), across(near, 2)]


def collect(parts):
    return [parts[0]] + [across(parts[j], j) for j in range(1, len(parts))]


def after(v, *others):
    return lax.optimization_barrier((v, *others))[0]


def swap_x(v):
    return lax.ppermute(v, "seq", [(0, 1), (1, 0)])


def swap_core(v):
    return lax.ppermute(v, "dp", [(i, i ^ 1) for i in range(4)])


def swap_y(v):
    return lax.ppermute(v, "dp", [(i, i ^ 2) for i in range(4)])


def swap_xy(v):
    return lax.ppermute(v, ("dp", "seq"), [(i, i ^ 5) for i in range(8)])


def after_all(values, others):
    return lax.optimization_barrier((*values, *others))[: len(values)]


def plane_gather(v, fancy, near=False, first=()):
    if fancy and near:
        near = after(jnp.stack([v, swap_x(v), swap_y(v), swap_xy(v)]), *first)
        return near, swap_core(near)
    if fancy:
        near = jnp.stack([v, swap_x(v)])
        near = jnp.concatenate([near, swap_y(near)])
        return near, swap_core(near)
    every = lax.all_gather(v, ("dp", "seq"), axis=0, tiled=False)
    half = every.shape[0] // 2
    return every[:half], every[half:]


def plane_scatter(keep, send, fancy):
    if not fancy:
        both = jnp.concatenate([keep, send], axis=0)
        return lax.psum_scatter(both, ("dp", "seq"), scatter_dimension=0, tiled=False).astype(f32)
    got = swap_core(send)
    low = [(keep[i].astype(f32) + got[i].astype(f32)).astype(bf16) for i in (1, 2, 3)]
    far = swap_x(low[0]).astype(f32) + swap_y(low[1]).astype(f32) + swap_xy(low[2]).astype(f32)
    return keep[0].astype(f32) + got[0].astype(f32) + far


def per_device(
    hidden_in,
    cotangent,
    piece_starts,
    expert_ids,
    claim_order,
    first_gain,
    second_gain,
    router,
    w_query,
    key_projection,
    value_projection,
    w_out,
    w_gate,
    w_up,
    w_down,
):
    n_dp, n_seq, n = lax.axis_size("dp"), lax.axis_size("seq"), lax.axis_size("tensor")
    fancy = n_dp == 4 and n_seq == 2
    n_p = n_dp * n_seq
    me = lax.axis_index("tensor")
    seq_at = lax.axis_index("seq")
    place = lax.axis_index("dp") * n_seq + seq_at
    m, d = hidden_in.shape[1:]
    count = m * n
    rows = d // n_p
    if hidden_in.shape[0] != 1 or expert_ids.shape[1] != count:
        raise ValueError("shapes")
    wide = w_query.shape[1]
    order = (0, 1, 4, 5, 2, 3, 6, 7) if fancy else tuple(range(n_p))
    where = (place ^ jnp.array(order, jnp.int32)) if fancy else jnp.arange(n_p, dtype=jnp.int32)

    own, cot = hidden_in[0], cotangent[0]

    shard = first_gain.shape[0]
    small = jnp.concatenate([router.reshape(-1), first_gain, second_gain])
    size = small.shape[0]
    smalls = spread(small.reshape(1, size))
    which = me ^ jnp.arange(n)
    pick_rows = (which[:, None] == jnp.arange(n)[None, :]).astype(f32)
    stacked = jnp.concatenate(smalls, axis=0).astype(f32)
    natural = jnp.sum(pick_rows[:, :, None] * stacked[None], axis=1).astype(bf16)
    qkv_w = jnp.concatenate([w_query, key_projection, value_projection], axis=1)
    cols = qkv_w.shape[1]
    natural = jnp.pad(natural.reshape(-1), (0, 16 * cols - n * size)).reshape(16, cols)
    xs = spread(own)
    wa, wb = plane_gather(jnp.concatenate([qkv_w, natural], axis=0), fancy, near=True)
    tail = jnp.concatenate([wa[:, rows:], wb[:, rows:]], axis=0).reshape(n_p, -1)[:, : n * size]
    ordered = (where[None, :] == jnp.arange(n_p, dtype=jnp.int32)[:, None]).astype(f32)
    tail = jnp.sum(ordered[:, :, None] * tail.astype(f32)[None], axis=1).reshape(n_p, n, size)
    gain_one = tail[:, :, size - 2 * shard : size - shard].reshape(1, d)
    gain_two = tail[:, :, size - shard :].reshape(1, d)
    router_all = tail[:, :, : size - 2 * shard].reshape(d, E).astype(bf16)

    blocks = me ^ jnp.arange(n, dtype=jnp.int32)
    positions = (seq_at * count + blocks[:, None] * m + jnp.arange(m, dtype=jnp.int32)[None, :]).reshape(count)
    starts = piece_starts[0]
    inside = (positions[:, None] >= starts[None, :]) & (positions[:, None] < starts[None, :] + PIECE)
    limit = jnp.maximum(
        positions, jnp.max(jnp.where(inside, starts[None, :] + PIECE - 1, -1), axis=1)
    ).reshape(1, count)
    half = HEAD // 2
    freqs = jnp.exp(jnp.arange(half).astype(f32) * (-2.0 * math.log(10000.0) / HEAD))
    angles = positions.astype(f32)[:, None] * freqs[None, :]
    cosine, sine = jnp.cos(angles), jnp.sin(angles)
    cos = jnp.concatenate([cosine] * 4, axis=1)
    sin = jnp.concatenate([-sine, sine] * 2, axis=1)

    ids, claim = expert_ids[0], claim_order[0]
    experts = jnp.arange(E, dtype=jnp.int32)
    chosen = jnp.max((ids[:, :, None] == experts[None, None, :]).astype(f32), axis=1)
    before = (claim[None, :] < claim[:, None]).astype(bf16)
    taken = dot(before, chosen.astype(bf16))
    kept = jnp.where(taken < CAP, chosen, 0.0)
    tables = jnp.concatenate([chosen, kept], axis=1).reshape(n, m, 2 * E)
    tables = jnp.sum(
        (blocks[:, None] == jnp.arange(n)[None, :]).astype(f32)[:, :, None, None] * tables[None], axis=1
    ).reshape(count, 2 * E)
    chosen, kept = tables[:, :E], tables[:, E:]

    x1, q, kv = whole_call(
        functools.partial(qkv_kernel, n, rows),
        (sds((count, d), bf16), sds((count, wide), bf16), sds((count, 256), bf16)),
        (where, *xs, gain_one, cos, sin, wa, wb),
        scratch=(pltpu.VMEM((d, cols), bf16),),
        flops=2 * count * d * cols,
        prefetch=1,
    )
    key_pos = positions.reshape(count, 1)
    if fancy:
        kvs = [kv, swap_x(kv)]
        poss = [key_pos, key_pos + (1 - 2 * seq_at) * count]
    else:
        kvs = [lax.all_gather(kv, "seq", axis=0, tiled=True)]
        poss = [lax.all_gather(key_pos.astype(f32), "seq", axis=0, tiled=True).astype(jnp.int32)]
    span = sum(v.shape[0] for v in kvs)
    heads = wide // HEAD
    got = whole_call(
        functools.partial(attend_kernel, len(kvs), n),
        tuple([sds((m, wide), bf16)] * n) + (sds((heads, HEAD, count), f32), sds((heads, 1, count), f32)),
        (q, limit, *kvs, *poss),
        scratch=(
            pltpu.VMEM((heads, count, HEAD), bf16),
            pltpu.VMEM((2, span, HEAD), bf16),
            pltpu.VMEM((2, HEAD, span), bf16),
            pltpu.VMEM((span, 1), jnp.int32),
        ),
        cost=10 ** 10,
    )
    mixed, (mixed_t, lse) = got[:n], got[n:]

    out_w = jnp.concatenate(spread(after(w_out, wa)), axis=1)
    cots = [cot] + spread(after(cot, kv))[1:]
    oa, ob = plane_gather(after(out_w, kvs[-1]), fancy, near=True, first=())
    mine = collect([mixed[0], *after_all(mixed[1:], cots[1:3])])
    oa, ob = (oa, swap_core(after(oa, *mine))) if fancy else (oa, ob)
    middle, second = whole_call(
        functools.partial(middle_kernel, n),
        (sds((m, d), f32), sds((m, d), bf16)),
        (where, own, gain_two, oa, ob, *mine),
        scratch=(pltpu.VMEM((d, n * wide), bf16),),
        flops=2 * m * d * d,
        prefetch=1,
    )

    seconds = spread(second)

    packed = jnp.stack([w_gate, w_up, w_down])
    ws = lax.all_gather(packed, ("dp", "seq"), axis=0, tiled=False)
    eb, fe = EXPERTS_PER_STEP, w_gate.shape[2]
    steps = E // eb
    block = pl.BlockSpec((count, eb * fe), lambda s: (0, s))
    wide_out = sds((count, E * fe), bf16)
    def expert_call(at, parts, begun):
        tall = m * parts
        return pl.pallas_call(
            functools.partial(expert_kernel, parts, bool(begun)),
            out_shape=tuple([sds((m, d), bf16)] * parts) + (wide_out, wide_out, wide_out, sds((E, d), f32)),
            grid=(steps,),
            in_specs=[full((tall, E)), full((tall, E)), full((d, E))]
            + [pl.BlockSpec((n_p, 3, eb, rows, fe), lambda s: (0, 0, s, 0, 0))]
            + [full((m, d))] * (2 * parts)
            + ([full((E, d))] + [pl.BlockSpec(memory_space=pl.ANY)] * 3 if begun else []),
            out_specs=[full((m, d))] * parts
            + [pl.BlockSpec((tall, eb * fe), lambda s: (at // parts, s))] * 3
            + [full((E, d))],
            scratch_shapes=[
                pltpu.VMEM((tall, d), bf16),
                pltpu.VMEM((tall, d), bf16),
                pltpu.VMEM((d, 3 * eb * fe), bf16),
                pltpu.VMEM((tall, d), f32),
                pltpu.VMEM((tall, E), f32),
                pltpu.VMEM((tall, E), f32),
            ],
            input_output_aliases={5 + 2 * parts + i: parts + i for i in range(3)} if begun else {},
            cost_estimate=pl.CostEstimate(flops=0 if begun else COST, bytes_accessed=0, transcendentals=0),
        )(
            chosen[at * m : at * m + tall],
            kept[at * m : at * m + tall],
            router_all,
            ws,
            *seconds[at : at + parts],
            *cots[at : at + parts],
            *begun,
        )

    split = n // 2 if n % 2 == 0 else n
    got = expert_call(0, split, ())
    second_parts, (active, gate_g, up_g, router_part) = got[:split], got[split:]
    if split < n:
        got = expert_call(split, split, (router_part, active, gate_g, up_g))
        second_parts, (active, gate_g, up_g, router_part) = (*second_parts, *got[:split]), got[split:]
    half_p = n_p // 2
    got = pl.pallas_call(
        functools.partial(expert_back_kernel, n),
        out_shape=tuple([sds((m, d), bf16)] * n) + (sds((n_p, 3, E, rows, fe), bf16),),
        grid=(steps,),
        in_specs=[block] * 3
        + [pl.BlockSpec((n_p, 1, eb, rows, fe), lambda s: (0, 2, s, 0, 0))]
        + [full((m, d))] * (2 * n),
        out_specs=[full((m, d))] * n + [pl.BlockSpec((n_p, 3, eb, rows, fe), lambda s: (0, 0, s, 0, 0))],
        scratch_shapes=[
            pltpu.VMEM((d, count), bf16),
            pltpu.VMEM((d, count), bf16),
            pltpu.VMEM((d, eb * fe), bf16),
            pltpu.VMEM((count, d), f32),
        ],
        cost_estimate=pl.CostEstimate(flops=0, bytes_accessed=0, transcendentals=0),
    )(active, gate_g, up_g, ws, *seconds, *cots)
    out_parts, expert_parts = got[:n], got[n]

    sums = collect(second_parts)
    expert_parts = after(expert_parts, *sums)
    expert_grads = lax.psum_scatter(expert_parts, ("dp", "seq"), scatter_dimension=0, tiled=False)
    got = whole_call(
        functools.partial(middle_back_kernel, n),
        (sds((m, d), f32), sds((m, d), bf16), sds((1, d), f32)) + tuple([sds((m, wide), bf16)] * n),
        (where, middle, gain_two, cot, oa, ob, *sums),
        scratch=(pltpu.VMEM((d, n * wide), bf16),),
        flops=2 * m * d * d,
        prefetch=1,
    )
    (middle_grad, branch, gain_two_part), pieces = got[:3], got[3:]
    mixed_grads = collect(pieces)
    branches = [branch] + spread_by_two(after(branch, *mixed_grads))[1:]

    def attend_back(kv_one, pos_one, dtype, extra):
        one = kv_one.shape[0]
        last = bool(extra)
        return whole_call(
            functools.partial(attend_back_kernel, n, last),
            (
                sds((one, 256), dtype),
                sds((count, wide), bf16) if last else sds((heads, HEAD, count), f32),
            ),
            (q, limit, kv_one, pos_one, lse, mixed_t, *mixed_grads, *extra),
            scratch=(
                pltpu.VMEM((heads, count, HEAD), bf16),
                pltpu.VMEM((heads, count, HEAD), bf16),
                pltpu.VMEM((2, one, HEAD), bf16),
                pltpu.VMEM((2, one, HEAD), bf16),
                pltpu.VMEM((2, HEAD, one), bf16),
                pltpu.VMEM((heads, 1, count), f32),
                pltpu.VMEM((2, one, HEAD), f32),
                pltpu.VMEM((2, one, HEAD), f32),
                pltpu.VMEM((heads, HEAD, count), f32),
            ),
            cost=10 ** 10,
        )

    if fancy:
        far, dq_far = attend_back(kvs[1], poss[1], bf16, ())
        got_kv = (swap_x(far),)
        dkv, dq = attend_back(kvs[0], poss[0], f32, (dq_far, cos, sin))
    else:
        zero = jnp.zeros((heads, HEAD, count), f32)
        dkv, dq = attend_back(kvs[0], poss[0], bf16, (zero, cos, sin))
        dkv = lax.psum_scatter(dkv, "seq", scatter_dimension=0, tiled=True)
        got_kv = (jnp.zeros((count, 256), bf16),)

    out_sums = [out_parts[0]] + collect([out_parts[0], *after_all(out_parts[1:], mixed_grads)])[1:]
    dq_ready = after(dq, *branches[1:3])
    got = whole_call(
        functools.partial(qkv_back_kernel, n, rows),
        tuple([sds((m, d), bf16)] * n) + (sds((count, cols), bf16), sds((1, d), f32)),
        (where, dq_ready, dkv, *got_kv, cos, sin, wa, wb, *xs),
        scratch=(pltpu.VMEM((d, cols), bf16),),
        flops=2 * count * d * cols,
        prefetch=1,
    )
    first_parts, (grads, gain_one_part) = got[:n], got[n:]
    grads = after(grads, *out_sums[:3])
    sums = collect(first_parts)
    weight_shape = sds((half_p, rows + LINES, cols + wide), bf16)
    weight_keep, weight_send = whole_call(
        functools.partial(weight_back_kernel, n, rows),
        (weight_shape, weight_shape),
        (where, x1, grads, router_part, gain_one_part, gain_two_part, *branches, *mixed),
        scratch=(pltpu.VMEM((d, cols + wide), bf16), pltpu.VMEM((n_p, LINES, rows), bf16)),
        flops=2 * count * d * (cols + wide),
        prefetch=1,
    )

    (input_grad,) = whole_call(
        functools.partial(input_kernel, n), (sds((m, d), bf16),), (own, gain_one, middle_grad, *sums)
    )
    (output,) = whole_call(
        functools.partial(output_kernel, n), (sds((m, d), bf16),), (middle, *out_sums)
    )
    weights = plane_scatter(weight_keep, weight_send, fancy)
    total = weights[rows : rows + E + 2, :rows]
    total = sum(spread(total)[1:], total)
    total = lax.dynamic_slice_in_dim(total, me * shard, shard, axis=1)
    weights = weights[:rows]
    kv_wide = key_projection.shape[1]
    return (
        output[None],
        input_grad[None],
        weights[:, :wide],
        weights[:, wide : wide + kv_wide],
        weights[:, wide + kv_wide : cols],
        weights[:, cols:],
        expert_grads[0].astype(f32),
        expert_grads[1].astype(f32),
        expert_grads[2].astype(f32),
        total[E],
        total[E + 1],
        total[:E].T,
    )


def solution(mesh):
    placed = (
        P("dp", ("seq", "tensor"), None),
        P("dp", ("seq", "tensor"), None),
        P("dp", None),
        P("dp", "seq", None),
        P("dp", "seq"),
        P(("dp", "seq", "tensor")),
        P(("dp", "seq", "tensor")),
        P(("dp", "seq", "tensor"), None),
        P(("dp", "seq"), "tensor"),
        P(("dp", "seq"), "tensor"),
        P(("dp", "seq"), "tensor"),
        P(("dp", "seq"), "tensor"),
        P(None, ("dp", "seq"), "tensor"),
        P(None, ("dp", "seq"), "tensor"),
        P(None, ("dp", "seq"), "tensor"),
    )
    return jax.shard_map(
        per_device,
        mesh=mesh,
        in_specs=placed,
        out_specs=(
            P("dp", ("seq", "tensor"), None),
            P("dp", ("seq", "tensor"), None),
            P(("dp", "seq"), "tensor"),
            P(("dp", "seq"), "tensor"),
            P(("dp", "seq"), "tensor"),
            P(("dp", "seq"), "tensor"),
            P(None, ("dp", "seq"), "tensor"),
            P(None, ("dp", "seq"), "tensor"),
            P(None, ("dp", "seq"), "tensor"),
            P(("dp", "seq", "tensor")),
            P(("dp", "seq", "tensor")),
            P(("dp", "seq", "tensor"), None),
        ),
        check_vma=False,
    )
```
